32 devices in a mesh: pack: 16 (over z, x, core), head: 2 (over y), rep: 1.
Axes of the slice: x: 2, y: 2, z: 4, core: 2. Of those that a mesh axis runs over, the one named last changes fastest.
Arguments:
- tokens: bfloat16 [49152, 1024], P(('rep', 'pack')), may hold values from -12 to 12
- ln_gain: float32 [1024], replicated, may hold values from 0.5 to 2
- attn_weight: bfloat16 [1024, 3, 1024], P(None, None, 'head'), may hold values from -6 to 6
- attn_proj: bfloat16 [1024, 1024], P('head'), may hold values from -0.1875 to 0.1875
- page_gain: float32 [1024], replicated, may hold values from 0.5 to 2
- page_weight: bfloat16 [1024, 3, 1024], P(None, None, 'head'), may hold values from -6 to 6
- page_proj: bfloat16 [1024, 1024], P('head'), may hold values from -0.1875 to 0.1875
- page_windows: int32 [48], P('rep'), may hold values from 1 to 12, 192 in all
- page_width: int32 [48], P('rep'), may hold values from 1 to 3
- doc_pages: int32 [12], P('rep'), may hold values from 1 to 8, 48 in all
Outputs:
- mixed: bfloat16 [49152, 1024], P(('rep', 'pack'), 'head')
- page_out: float32 [48, 1024], P('rep', 'head')
The draws below stay inside these ranges and needn't reach their ends.
Inputs may be any that keep to these rules, and one draw needn't show every extreme that they name: `page_windows`: the pages fill all 192 windows, and one page has exactly 12. `page_width`: A page's last row of windows may be short. `doc_pages`: the documents hold all 48 pages, and one has exactly 8.
All inputs are finite; a program needn't handle non-finite values.
Results may differ from the reference program's by a relative error of at most 0.03.
The reference program's roundings to bfloat16 on the way count: a program that leaves them out, or rounds other values in their place, can miss the bound.
Values may be sent and summed in bfloat16 or wider, within the bound.
A program may use at most 128 MiB of HBM per device.

```python
import math
import jax
import jax.numpy as jnp
import numpy as np
from jax import lax

D = 1024
HEADS = 32
WIN = 16
HALO = 4
PW_MAX = 3
PAGE_MOST = 12
WINDOWS = 192
TOKENS = 49152
PAGES = 48
DOCS = 12
DOC_MOST = 8


def draw_tokens(key, part):
    keys_all = jax.random.split(jax.random.fold_in(key, 11), 3)
    position = jnp.arange(TOKENS, dtype=jnp.float32)
    rising = 1.0 + 2.0 * position / TOKENS
    row_scale = jnp.exp(jax.random.uniform(keys_all[1], (TOKENS,), minval=math.log(0.1), maxval=0.0))
    col_scale = jnp.exp(jax.random.uniform(keys_all[2], (D,), minval=math.log(0.1), maxval=0.0))
    values_raw = jnp.clip(jax.random.normal(keys_all[0], (TOKENS, D)), -4.0, 4.0)
    return (values_raw * (rising * row_scale)[:, None] * col_scale[None, :]).astype(jnp.bfloat16)


def projection_draw(key, salt):
    keys_all = jax.random.split(jax.random.fold_in(key, salt), 1)
    entries = jnp.clip(jax.random.normal(keys_all[0], (D, 3, D)), -4.0, 4.0) / math.sqrt(D)
    return entries


def draw_attn_weight(key, part):
    return projection_draw(key, 21).astype(jnp.bfloat16)


def draw_page_weight(key, part):
    return projection_draw(key, 37).astype(jnp.bfloat16)


def place_ends(values, stream_key, least, high):
    spot = [jax.random.randint(jax.random.fold_in(stream_key, axis), (), 0, length) for axis, length in enumerate(values.shape)]
    longest = values.shape.index(max(values.shape))
    next_to = spot[:longest] + [(spot[longest] + 1) % values.shape[longest]] + spot[longest + 1:]
    return values.at[tuple(spot)].set(least).at[tuple(next_to)].set(high)


def block_scale(own_key, extent, cuts, least, largest):
    factor_of, own = 1.0, jax.random.fold_in(own_key, 6)
    for dim, blocks in cuts:
        draws = jnp.exp(jax.random.uniform(jax.random.fold_in(own, dim), (blocks,), jnp.float32, least / len(cuts), largest / len(cuts)))
        factor_of = factor_of * jnp.repeat(draws, extent[dim] // blocks).reshape([-1 if axis == dim else 1 for axis in range(len(extent))])
    return factor_of


def length_profile(number_of, total, most, lean):
    portions = [(1 << 20) // math.isqrt(rank ** lean) + 1 for rank in range(2, number_of + 1)]
    spare, holding = total - most - (number_of - 1), [1] * (number_of - 1)
    while spare > 0:
        movable = [i for i in range(number_of - 1) if holding[i] < most]
        whole, left = sum([portions[i] for i in movable]), spare
        for i in movable:
            extra = min(most - holding[i], max(1, left * portions[i] // whole), spare)
            holding[i] = holding[i] + extra
            spare = spare - extra
    return np.array([most] + holding)


def uneven(stream_key, count, total, reach, slope):
    if count == 2:
        one = jax.random.randint(stream_key, (), max(1, total - reach), min(reach, total - 1) + 1)
        return jnp.stack([one, total - one])
    tallies = jnp.asarray(length_profile(count, total, reach, slope), jnp.int32)
    couples = (count - 1) // 2
    giver, taker = tallies[1:1 + 2 * couples:2], tallies[2:2 + 2 * couples:2]
    margin = jnp.minimum(giver - 1, reach - taker)
    passed = jax.random.randint(jax.random.fold_in(stream_key, 1), (couples,), 0, 1 << 20) % (margin + 1)
    tallies = tallies.at[1:1 + 2 * couples:2].set(giver - passed).at[2:2 + 2 * couples:2].set(taker + passed)
    return tallies[jax.random.permutation(jax.random.fold_in(stream_key, 2), count)]


def gaussian(key, extent, deviation, bound, cuts=(), kind=jnp.bfloat16):
    loudness = block_scale(key, extent, cuts, -0.22, 0.18) if cuts else 1.0
    values = jax.random.normal(key, extent, jnp.float32) * deviation * loudness
    return jnp.minimum(jnp.maximum(values, -bound), bound).astype(kind)


def setup_inputs(seed: int = 0, part: int = 0) -> dict:
    splits = jax.random.split(jax.random.key(seed), 11)
    part_splits = jax.random.split(jax.random.fold_in(splits[10], part), 11)
    tokens = draw_tokens(jax.random.fold_in(jax.random.fold_in(splits[10], part), 71), part)
    ln_gain = jnp.clip(jnp.exp(jax.random.uniform(splits[1], (D,), jnp.float32, math.log(0.5), math.log(2.0))), 0.5, 2.0)
    attn_weight = draw_attn_weight(jax.random.fold_in(splits[10], 71), part)
    attn_proj = gaussian(splits[3], (D, D), D ** -0.5, 0.1875, ((0, 2),))
    page_gain = jnp.clip(jnp.exp(jax.random.uniform(splits[4], (D,), jnp.float32, math.log(0.5), math.log(2.0))), 0.5, 2.0)
    page_weight = draw_page_weight(jax.random.fold_in(splits[10], 71), part)
    page_proj = gaussian(splits[6], (D, D), D ** -0.5, 0.1875, ((0, 2),))
    page_windows = uneven(part_splits[7], PAGES, WINDOWS, PAGE_MOST, 2).astype(jnp.int32)
    page_width = place_ends(jax.random.randint(part_splits[8], (PAGES,), 1, PW_MAX + 1), jax.random.fold_in(part_splits[8], 1), 1, PW_MAX).astype(jnp.int32)
    doc_pages = uneven(part_splits[9], DOCS, PAGES, DOC_MOST, 1).astype(jnp.int32)
    return dict(tokens=tokens, ln_gain=ln_gain, attn_weight=attn_weight, attn_proj=attn_proj, page_gain=page_gain, page_weight=page_weight, page_proj=page_proj, page_windows=page_windows, page_width=page_width, doc_pages=doc_pages)


EPS = 1e-05
OFFSETS = ((-1, -1), (-1, 0), (-1, 1), (0, -1), (0, 0), (0, 1), (1, -1), (1, 0), (1, 1))

def layer_norm(values, gain):
    values = values.astype(jnp.float32)
    center = values - lax.optimization_barrier(jnp.mean(values, axis=-1, keepdims=True))
    spread = lax.optimization_barrier(jnp.mean(center * center, axis=-1, keepdims=True))
    return (center * lax.rsqrt(spread + EPS) * gain.astype(jnp.float32)).astype(jnp.bfloat16)

def page_member(window_ids, page_windows):
    page_ends = jnp.cumsum(page_windows).astype(jnp.int32)
    page_starts = (page_ends - page_windows).astype(jnp.int32)
    return (window_ids[:, None] >= page_starts[None, :]) & (window_ids[:, None] < page_ends[None, :])

def window_geometry(window_ids, page_windows, page_width):
    page_ends = jnp.cumsum(page_windows).astype(jnp.int32)
    page_starts = (page_ends - page_windows).astype(jnp.int32)
    member = page_member(window_ids, page_windows).astype(jnp.int32)
    begin = lax.optimization_barrier(jnp.sum(member * page_starts[None, :], axis=1)).astype(jnp.int32)
    across = lax.optimization_barrier(jnp.sum(member * page_width[None, :], axis=1)).astype(jnp.int32)
    total = lax.optimization_barrier(jnp.sum(member * page_windows[None, :], axis=1)).astype(jnp.int32)
    inside = window_ids - begin
    grid_row = inside // across
    grid_col = inside - grid_row * across
    rows_near = jnp.stack([grid_row + pair[0] for pair in OFFSETS], axis=1)
    cols_near = jnp.stack([grid_col + pair[1] for pair in OFFSETS], axis=1)
    place = rows_near * across[:, None] + cols_near
    valid = (cols_near >= 0) & (cols_near < across[:, None]) & (rows_near >= 0) & (place < total[:, None])
    return ((begin[:, None] + place).astype(jnp.int32), valid)

def gather_keys(extended, tile_index, valid):
    count = tile_index.shape[0]
    feats = extended.shape[-1]
    tiles = extended[tile_index]
    tiles = tiles.reshape(count, 3, 3, WIN, WIN, feats).transpose(0, 1, 3, 2, 4, 5).reshape(count, 3 * WIN, 3 * WIN, feats)
    lower_edge = WIN - HALO
    upper_edge = 2 * WIN + HALO
    region = tiles[:, lower_edge:upper_edge, lower_edge:upper_edge].reshape(count, -1, feats)
    grid_keep = jnp.broadcast_to(valid.reshape(count, 3, 1, 3, 1), (count, 3, WIN, 3, WIN)).reshape(count, 3 * WIN, 3 * WIN)
    keep = grid_keep[:, lower_edge:upper_edge, lower_edge:upper_edge].reshape(count, -1)
    return (region, keep)

def attention(query, keys, values, mask, heads):
    count, qlen, width = query.shape
    depth = width // heads
    q_heads = query.astype(jnp.float32).reshape(count, qlen, heads, depth)
    k_heads = keys.astype(jnp.float32).reshape(count, -1, heads, depth)
    v_heads = values.astype(jnp.float32).reshape(count, -1, heads, depth)
    scores = jnp.einsum('nqhd,nkhd->nhqk', q_heads, k_heads) / math.sqrt(depth)
    scores = jnp.where(mask[:, None], scores, -1e+30)
    top_score = lax.optimization_barrier(jnp.max(scores, axis=-1, keepdims=True))
    weights = jnp.exp(scores - top_score)
    probs = (weights / lax.optimization_barrier(jnp.sum(weights, axis=-1, keepdims=True))).astype(jnp.bfloat16)
    output = jnp.einsum('nhqk,nkhd->nqhd', probs.astype(jnp.float32), v_heads)
    return output.reshape(count, qlen, width).astype(jnp.bfloat16)

def reference(tokens, ln_gain, attn_weight, attn_proj, page_gain, page_weight, page_proj, page_windows, page_width, doc_pages):
    normed = layer_norm(tokens, ln_gain)
    qkv = jnp.dot(normed, attn_weight.reshape(D, 3 * D), preferred_element_type=jnp.float32).astype(jnp.bfloat16)
    queries = qkv[:, :D].reshape(WINDOWS, WIN * WIN, D)
    keyvals = qkv[:, D:].reshape(WINDOWS, WIN * WIN, 2 * D)
    window_ids = jnp.arange(WINDOWS, dtype=jnp.int32)
    neighbor, valid = window_geometry(window_ids, page_windows, page_width)
    tile_index = jnp.where(valid, neighbor, window_ids[:, None]).astype(jnp.int32)

    def attend(block):
        query_block, index_block, valid_block = block
        region, keep = gather_keys(keyvals, index_block, valid_block)
        return attention(query_block, region[..., :D], region[..., D:], keep[:, None, :], HEADS)
    mixed = lax.map(attend, (queries.reshape(WINDOWS, 1, WIN * WIN, D), tile_index.reshape(WINDOWS, 1, 9), valid.reshape(WINDOWS, 1, 9)))
    mixed = mixed.reshape(TOKENS, D)
    member = page_member(window_ids, page_windows).astype(jnp.float32)
    token_sums = lax.optimization_barrier(jnp.sum(tokens.reshape(WINDOWS, WIN * WIN, D), axis=1, dtype=jnp.float32))
    mixed_sums = lax.optimization_barrier(jnp.sum(mixed.reshape(WINDOWS, WIN * WIN, D), axis=1, dtype=jnp.float32))
    page_tokens = jnp.dot(member.T, token_sums, precision=lax.Precision.HIGHEST)
    page_mixed = jnp.dot(member.T, mixed_sums, precision=lax.Precision.HIGHEST)
    projected = jnp.dot(page_mixed, attn_proj.astype(jnp.float32), precision=lax.Precision.HIGHEST)
    counts = WIN * WIN * page_windows.astype(jnp.float32)
    pooled = (page_tokens + projected) / counts[:, None]
    page_normed = layer_norm(pooled, page_gain)
    page_qkv = jnp.dot(page_normed, page_weight.reshape(D, 3 * D), preferred_element_type=jnp.float32).astype(jnp.bfloat16)
    doc_ends = jnp.cumsum(doc_pages).astype(jnp.int32)
    page_ids = jnp.arange(PAGES, dtype=jnp.int32)
    doc_of = lax.optimization_barrier(jnp.sum((page_ids[:, None] >= doc_ends[None, :]).astype(jnp.int32), axis=1))
    same_doc = doc_of[:, None] == doc_of[None, :]
    context = attention(page_qkv[None, :, :D], page_qkv[None, :, D:2 * D], page_qkv[None, :, 2 * D:], same_doc[None], HEADS)[0]
    page_out = pooled + jnp.dot(context, page_proj, preferred_element_type=jnp.float32)
    return (mixed, page_out)
```

```python
import functools
import math

import jax
import jax.numpy as jnp
import numpy as np
from jax import lax
from jax.experimental import pallas as pl
from jax.experimental.pallas import tpu as pltpu
from jax.sharding import PartitionSpec as P

D = 1024
HDIM = 32
WIN = 16
HALO = 4
HALO_WIN = 4
TOK = WIN * WIN
STRIP = WIN * HALO
CORNER = HALO * HALO
SIDE_KEYS = 4 * STRIP + 4 * CORNER
KEYS = TOK + SIDE_KEYS
SUM_LEAST = 2.0**-60
SUM_MOST = 2.0**60
EPS = 1e-05
LOG2E = 1.4426950408889634
OFFSETS = ((-1, 0), (1, 0), (0, -1), (0, 1), (-1, -1), (-1, 1), (1, -1), (1, 1))


def edge_rows():
    table = np.zeros((2 * STRIP, TOK), np.float32)
    for i in range(STRIP):
        row, col = i // HALO, i % HALO
        table[i, row * WIN + col] = 1.0
        table[STRIP + i, row * WIN + WIN - HALO + col] = 1.0
    return jnp.asarray(table, jnp.bfloat16)


def nn_dot(a, b):
    return jnp.dot(a, b, preferred_element_type=jnp.float32)


def normalize(values, gain):
    center = values - jnp.mean(values, axis=-1, keepdims=True)
    spread = jnp.mean(center * center, axis=-1, keepdims=True)
    return (center * lax.rsqrt(spread + EPS) * gain).astype(jnp.bfloat16)


def qkv_kernel(
    count,
    win_count,
    width,
    tok_ref,
    gain_ref,
    w_hbm,
    sel_ref,
    qt_ref,
    k_ref,
    v_ref,
    ek_ref,
    ev_ref,
    tsum_ref,
    tok_s,
    w_s,
    even_s,
    odd_s,
    own_sem,
    w_sem,
    send_sem,
    recv_sem,
):
    me = lax.axis_index("pack")
    after = {"pack": lax.rem(me + 1, count)}
    before = {"pack": lax.rem(me + count - 1, count)}
    groups = width // 128

    def own(w):
        return pltpu.make_async_copy(
            tok_ref.at[pl.ds(w * TOK, TOK)], tok_s.at[w], own_sem.at[w]
        )

    weight = pltpu.make_async_copy(w_hbm, w_s, w_sem.at[0])
    for w in range(win_count):
        own(w).start()
        if w == 0:
            weight.start()

    pieces = [
        (after, (win_count - 1) * TOK, TOK, win_count, 0),
        (before, 0, TOK, win_count + 2, 0),
    ]
    for i in range(HALO_WIN - 1):
        high = (win_count - HALO_WIN + i + 1) * TOK - STRIP
        pieces.append((after, high, STRIP, win_count + 1, i * STRIP))
        pieces.append((before, (i + 1) * TOK, STRIP, win_count + 3, i * STRIP))
    copies = [
        pltpu.make_async_remote_copy(
            src_ref=tok_ref.at[pl.ds(start, size)],
            dst_ref=tok_s.at[block, pl.ds(row, size)],
            send_sem=send_sem.at[i],
            recv_sem=recv_sem.at[i],
            device_id=where,
            device_id_type=pl.DeviceIdType.MESH,
        )
        for i, (where, start, size, block, row) in enumerate(pieces)
    ]
    barrier = pltpu.get_barrier_semaphore()
    for where in (after, before):
        pl.semaphore_signal(barrier, inc=1, device_id=where, device_id_type=pl.DeviceIdType.MESH)
    spare = (HALO_WIN - 1) * STRIP
    for block in (win_count + 1, win_count + 3):
        tok_s[block, spare:] = jnp.zeros((TOK - spare, D), tok_s.dtype)

    def norm(block, out_s):
        for lo in range(0, TOK, 32):
            values = tok_s[block, lo : lo + 32].astype(jnp.float32)
            out_s[lo : lo + 32] = normalize(values, gain_ref[...])
        sums = nn_dot(jnp.ones((16, TOK), jnp.bfloat16), tok_s[block])
        tsum_ref[block] = sums[:1]

    def project(block, in_s):
        values = in_s[...]
        q = nn_dot(values, w_s[0]).astype(jnp.bfloat16)
        for g in range(groups):
            qt_ref[block, g] = q[:, g * 128 : (g + 1) * 128].T
        for part, out_ref, edge_ref in ((1, k_ref, ek_ref), (2, v_ref, ev_ref)):
            made = nn_dot(values, w_s[part]).astype(jnp.bfloat16)
            edge = nn_dot(sel_ref[...], made).astype(jnp.bfloat16)
            for g in range(groups):
                out_ref[block, g] = made[:, g * 128 : (g + 1) * 128]
                edge_ref[block, g] = edge[:, g * 128 : (g + 1) * 128]

    own(0).wait()
    norm(0, even_s)
    pl.semaphore_wait(barrier, 2)
    for copy in copies:
        copy.start()
    weight.wait()

    def arrive(block):
        @pl.when(block < win_count)
        def _():
            own(jnp.minimum(block, win_count - 1)).wait()

        @pl.when(block == win_count)
        def _():
            for copy in copies:
                copy.wait_recv()

    blocks = win_count + 4

    def pair(i, carry):
        arrive(2 * i + 1)
        project(2 * i, even_s)
        norm(2 * i + 1, odd_s)
        arrive(2 * i + 2)
        project(2 * i + 1, odd_s)
        norm(2 * i + 2, even_s)
        return carry

    lax.fori_loop(0, blocks // 2 - 1, pair, 0)
    project(blocks - 2, even_s)
    norm(blocks - 1, odd_s)
    project(blocks - 1, odd_s)
    for copy in copies:
        copy.wait_send()


def window_qkv(tokens, gain, weight):
    win_count = tokens.shape[0] // TOK
    width = weight.shape[2]
    groups = width // 128
    blocks = win_count + 4
    bf = jnp.bfloat16
    vmem = pl.BlockSpec(memory_space=pltpu.VMEM)
    hbm = pl.BlockSpec(memory_space=pl.ANY)
    return pl.pallas_call(
        functools.partial(qkv_kernel, lax.axis_size("pack"), win_count, width),
        out_shape=(
            pltpu.VMEM((blocks, groups, 128, TOK), bf),
            pltpu.VMEM((blocks, groups, TOK, 128), bf),
            pltpu.VMEM((blocks, groups, TOK, 128), bf),
            pltpu.VMEM((blocks, groups, 2 * STRIP, 128), bf),
            pltpu.VMEM((blocks, groups, 2 * STRIP, 128), bf),
            pltpu.VMEM((blocks, 1, D), jnp.float32),
        ),
        in_specs=[hbm, vmem, hbm, vmem],
        out_specs=(vmem,) * 6,
        scratch_shapes=[
            pltpu.VMEM((blocks, TOK, D), bf),
            pltpu.VMEM((3, D, width), bf),
            pltpu.VMEM((TOK, D), bf),
            pltpu.VMEM((TOK, D), bf),
            pltpu.SemaphoreType.DMA((win_count,)),
            pltpu.SemaphoreType.DMA((1,)),
            pltpu.SemaphoreType.DMA((8,)),
            pltpu.SemaphoreType.DMA((8,)),
        ],
        compiler_params=pltpu.CompilerParams(
            collective_id=1, has_side_effects=True, vmem_limit_bytes=24 << 20
        ),
    )(tokens, gain.reshape(1, D), weight.transpose(1, 0, 2), edge_rows())


def attend_kernel(
    win_count,
    width,
    pages,
    windows_ref,
    across_ref,
    qt_ref,
    k_ref,
    v_ref,
    ek_ref,
    ev_ref,
    mixed_hbm,
    msum_ref,
    pk_s,
    pv_s,
    mask_s,
    out_s,
    low_s,
    high_s,
    out_sem,
):
    first = lax.axis_index("pack") * win_count
    groups = width // 128
    per = 128 // HDIM
    extra_most = KEYS - TOK
    factor = LOG2E / math.sqrt(HDIM)
    bf = jnp.bfloat16

    def copy_out(w):
        slot = lax.rem(w, 2)
        return pltpu.make_async_copy(
            out_s.at[slot], mixed_hbm.at[pl.ds(w * TOK, TOK)], out_sem.at[slot]
        )

    def find(p, carry):
        page, begin, run = carry
        run = run + windows_ref[p]
        passed = run <= first
        return jnp.where(passed, p + 1, page), jnp.where(passed, run, begin), run

    def locate(block):
        inner = jnp.where(block == -1, win_count, jnp.where(block == win_count, win_count + 2, block))
        inner = jnp.where(block < -1, win_count + 1, inner)
        return jnp.where(block > win_count, win_count + 3, inner)

    def pack(w, page, begin):
        across = across_ref[page]
        total = windows_ref[page]
        inside = first + w - begin
        row = lax.div(inside, across)
        col = inside - row * across
        filled = jnp.int32(0)
        for a, b in OFFSETS:
            place = inside + a * across + b
            valid = (col + b >= 0) & (col + b < across) & (row + a >= 0) & (place < total)
            near = w + a * across + b
            block = locate(near)
            size = CORNER if a and b else STRIP
            if a < 0:
                index = jnp.where(near < -1, near + HALO_WIN, (TOK - size) // size if b == 0 else 3)
            elif a > 0:
                index = jnp.where(near > win_count, near - win_count - 1, 0)
            else:
                index = 0
            if b == 0:
                start = index * STRIP
            else:
                start = index * CORNER + (STRIP if b < 0 else 0)
            keys, values = (k_ref, v_ref) if b == 0 else (ek_ref, ev_ref)

            @pl.when(valid)
            def _(block=block, start=start, size=size, keys=keys, values=values, filled=filled):
                source = pl.ds(pl.multiple_of(start, 16), size)
                target = pl.ds(pl.multiple_of(filled, 16), size)
                pk_s[:, target, :] = keys[block, :, source, :]
                pv_s[:, target, :] = values[block, :, source, :]

            filled = filled + jnp.where(valid, size, 0)
        blank = jnp.zeros((groups, 3 * CORNER, 128), bf)
        target = pl.ds(pl.multiple_of(filled, 16), 3 * CORNER)
        pk_s[:, target, :] = blank
        pv_s[:, target, :] = blank
        lane = lax.broadcasted_iota(jnp.int32, mask_s.shape, 1)
        mask_s[...] = jnp.where(lane < filled, 1.0, 0.0).astype(bf)
        return filled

    def finish(w, g, parts):
        piece = jnp.concatenate(parts, axis=0).T
        slot = lax.rem(w, 2)
        out_s[slot, :, g * 128 : (g + 1) * 128] = piece
        sums = nn_dot(jnp.ones((16, TOK), bf), piece)
        msum_ref[w, :, g * 128 : (g + 1) * 128] = sums[:1]

    def spread(queries, j):
        above = [jnp.zeros((j * HDIM, TOK), bf)] if j else []
        below = [jnp.zeros((128 - (j + 1) * HDIM, TOK), bf)] if j + 1 < per else []
        return jnp.concatenate(above + [queries[j * HDIM : (j + 1) * HDIM]] + below, axis=0)

    def fast(w, extra):
        low, high = low_s[...], high_s[...]
        for g in range(groups):
            queries = qt_ref[w, g]
            own_v = v_ref[w, g].T
            near_v = pv_s[g, :extra].T if extra else None
            parts = []
            for j in range(per):
                qz = spread(queries, j)
                rows = slice(j * HDIM, (j + 1) * HDIM)
                weights = jnp.exp2(nn_dot(k_ref[w, g], qz) * factor).astype(bf)
                lhs = jnp.concatenate([own_v[rows], jnp.ones((16, TOK), bf)], axis=0)
                summed = nn_dot(lhs, weights)
                if extra:
                    weights = jnp.exp2(nn_dot(pk_s[g, :extra], qz) * factor).astype(bf)
                    lhs = jnp.concatenate([near_v[rows], mask_s[:, :extra]], axis=0)
                    summed = summed + nn_dot(lhs, weights)
                total = summed[HDIM : HDIM + 1]
                low = jnp.minimum(low, total)
                high = jnp.maximum(high, total)
                parts.append((summed[:HDIM] * (1.0 / total)).astype(bf))
            finish(w, g, parts)
        low_s[...] = low
        high_s[...] = high

    def safe(w, filled):
        row = lax.broadcasted_iota(jnp.int32, (extra_most, TOK), 0)
        for g in range(groups):
            queries = qt_ref[w, g]
            own_v = v_ref[w, g].T
            near_v = pv_s[g, :extra_most].T
            parts = []
            for j in range(per):
                qz = spread(queries, j)
                rows = slice(j * HDIM, (j + 1) * HDIM)
                own = nn_dot(k_ref[w, g], qz) * factor
                near = nn_dot(pk_s[g, :extra_most], qz) * factor
                near = jnp.where(row < filled, near, -1e30)
                top = jnp.maximum(
                    jnp.max(own, axis=0, keepdims=True), jnp.max(near, axis=0, keepdims=True)
                )
                own = jnp.exp2(own - top)
                near = jnp.exp2(near - top)
                total = jnp.sum(own, axis=0, keepdims=True) + jnp.sum(near, axis=0, keepdims=True)
                summed = nn_dot(own_v[rows], own.astype(bf)) + nn_dot(near_v[rows], near.astype(bf))
                parts.append((summed * (1.0 / total)).astype(bf))
            finish(w, g, parts)

    def sweep(guarded):
        def step(w, carry):
            page, begin = carry
            end = begin + windows_ref[page]
            passed = first + w >= end
            page = jnp.where(passed, page + 1, page)
            begin = jnp.where(passed, end, begin)
            filled = pack(w, page, begin)

            @pl.when(w >= 2)
            def _():
                copy_out(w - 2).wait()

            if guarded:
                safe(w, filled)
            else:
                chunks = lax.div(filled + STRIP - 1, STRIP)
                for c in range(extra_most // STRIP + 1):

                    @pl.when(chunks == c)
                    def _(c=c):
                        fast(w, c * STRIP)

            copy_out(w).start()
            return page, begin

        zero = jnp.int32(0)
        page, begin, _ = lax.fori_loop(0, pages, find, (zero, zero, zero))
        lax.fori_loop(0, win_count, step, (page, begin))
        copy_out(win_count - 2).wait()
        copy_out(win_count - 1).wait()

    pk_s[...] = jnp.zeros_like(pk_s)
    pv_s[...] = jnp.zeros_like(pv_s)
    low_s[...] = jnp.ones_like(low_s)
    high_s[...] = jnp.ones_like(high_s)
    sweep(False)
    calm = (jnp.min(low_s[...]) >= SUM_LEAST) & (jnp.max(high_s[...]) <= SUM_MOST)

    @pl.when(jnp.logical_not(calm))
    def _():
        sweep(True)


def window_attention(tables, page_windows, page_width, win_count):
    qt, k, v, ek, ev = tables
    groups = k.shape[1]
    width = groups * 128
    bf = jnp.bfloat16
    vmem = pl.BlockSpec(memory_space=pltpu.VMEM)
    smem = pl.BlockSpec(memory_space=pltpu.SMEM)
    hbm = pl.BlockSpec(memory_space=pl.ANY)
    room = KEYS - TOK + STRIP
    arrays = [pltpu.with_memory_space_constraint(a, pltpu.VMEM) for a in tables]
    return pl.pallas_call(
        functools.partial(attend_kernel, win_count, width, page_windows.shape[0]),
        out_shape=(
            jax.ShapeDtypeStruct((win_count * TOK, width), bf),
            jax.ShapeDtypeStruct((win_count, 1, width), jnp.float32),
        ),
        in_specs=[smem, smem] + [vmem] * 5,
        out_specs=(hbm, vmem),
        scratch_shapes=[
            pltpu.VMEM((groups, room, 128), bf),
            pltpu.VMEM((groups, room, 128), bf),
            pltpu.VMEM((16, room), bf),
            pltpu.VMEM((2, TOK, width), bf),
            pltpu.VMEM((1, TOK), jnp.float32),
            pltpu.VMEM((1, TOK), jnp.float32),
            pltpu.SemaphoreType.DMA((2,)),
        ],
        compiler_params=pltpu.CompilerParams(vmem_limit_bytes=16 << 20),
    )(page_windows, page_width, *arrays)


def sum_kernel(count, heads, x_ref, out_ref, land, acc, full, send_sem, recv_sem):
    me = lax.axis_index("pack") * heads + lax.axis_index("head")

    def device(k):
        other = lax.rem(me + k, count)
        return other, {"pack": lax.div(other, heads), "head": lax.rem(other, heads)}

    barrier = pltpu.get_barrier_semaphore()

    @pl.loop(1, count)
    def _(k):
        pl.semaphore_signal(
            barrier, inc=1, device_id=device(k)[1], device_id_type=pl.DeviceIdType.MESH
        )

    pl.semaphore_wait(barrier, count - 1)

    def copy(k, phase):
        other, where = device(k)
        return pltpu.make_async_remote_copy(
            src_ref=acc if phase else x_ref.at[other],
            dst_ref=full.at[me] if phase else land.at[k],
            send_sem=send_sem.at[phase, k],
            recv_sem=recv_sem.at[phase, k],
            device_id=where,
            device_id_type=pl.DeviceIdType.MESH,
        )

    for phase in (0, 1):

        @pl.loop(1, count)
        def _(k):
            copy(k, phase).start()

        if phase:
            full[me] = acc[...]
        else:
            land[0] = x_ref[me]

        @pl.loop(1, count)
        def _(k):
            copy(k, phase).wait_recv()

        if phase:
            out_ref[...] = full[...]
        else:
            acc[...] = jnp.sum(land[...], axis=0)

    @pl.loop(1, count)
    def _(k):
        copy(k, 0).wait_send()
        copy(k, 1).wait_send()


def sum_over_devices(values):
    heads = lax.axis_size("head")
    count = lax.axis_size("pack") * heads
    rows = values.size // (count * 128)
    shape = (count, rows, 128)
    total = pl.pallas_call(
        lambda *refs: sum_kernel(count, heads, *refs),
        out_shape=jax.ShapeDtypeStruct(shape, jnp.float32),
        in_specs=[pl.BlockSpec(memory_space=pltpu.VMEM)],
        out_specs=pl.BlockSpec(memory_space=pltpu.VMEM),
        scratch_shapes=[
            pltpu.VMEM(shape, jnp.float32),
            pltpu.VMEM(shape[1:], jnp.float32),
            pltpu.VMEM(shape, jnp.float32),
            pltpu.SemaphoreType.DMA((2, count)),
            pltpu.SemaphoreType.DMA((2, count)),
        ],
        compiler_params=pltpu.CompilerParams(collective_id=0, has_side_effects=True),
    )(values.reshape(shape))
    return total.reshape(values.shape)


def keep_share(values):
    heads = lax.axis_size("head")
    me = lax.axis_index("head")
    columns = values.shape[1] // heads
    rounded = values.astype(jnp.bfloat16)

    def part(k):
        start = lax.rem(me + k, heads) * columns
        return lax.dynamic_slice_in_dim(rounded, start, columns, 1)

    total = part(0).astype(jnp.float32)
    for k in range(1, heads):
        pairs = [(i, (i + k) % heads) for i in range(heads)]
        total = total + lax.ppermute(part(k), "head", pairs).astype(jnp.float32)
    return total


def layer_norm(values, gain):
    values = values.astype(jnp.float32)
    return normalize(values, gain)


def page_member(window_ids, page_windows):
    page_ends = jnp.cumsum(page_windows)
    page_starts = page_ends - page_windows
    return (window_ids[:, None] >= page_starts[None, :]) & (
        window_ids[:, None] < page_ends[None, :]
    )


def attention(query, keys, values, mask, heads):
    qlen, width = query.shape
    depth = width // heads
    q_heads = query.reshape(qlen, heads, depth)
    k_heads = keys.reshape(-1, heads, depth)
    v_heads = values.reshape(-1, heads, depth)
    scores = jnp.einsum(
        "qhd,khd->hqk", q_heads, k_heads, preferred_element_type=jnp.float32
    ) / math.sqrt(depth)
    scores = jnp.where(mask[None], scores, -1e30)
    top_score = jnp.max(scores, axis=-1, keepdims=True)
    weights = jnp.exp(scores - top_score)
    probs = (weights / jnp.sum(weights, axis=-1, keepdims=True)).astype(jnp.bfloat16)
    output = jnp.einsum("hqk,khd->qhd", probs, v_heads, preferred_element_type=jnp.float32)
    return output.reshape(qlen, width).astype(jnp.bfloat16)


def shards(
    tokens,
    ln_gain,
    attn_weight,
    attn_proj,
    page_gain,
    page_weight,
    page_proj,
    page_windows,
    page_width,
    doc_pages,
):
    win_count = tokens.shape[0] // TOK
    local_width = attn_weight.shape[2]
    local_heads = local_width // HDIM
    window_ids = lax.axis_index("pack") * win_count + jnp.arange(win_count, dtype=jnp.int32)
    *tables, token_sums = window_qkv(tokens, ln_gain, attn_weight)
    mixed, mixed_sums = window_attention(tables, page_windows, page_width, win_count)
    token_sums = token_sums[:win_count]
    member = page_member(window_ids, page_windows).astype(jnp.float32)
    highest = lax.Precision.HIGHEST
    page_tokens = jnp.dot(member.T, token_sums[:, 0], precision=highest)
    page_mixed = jnp.dot(member.T, mixed_sums[:, 0], precision=highest)
    projected = jnp.dot(page_mixed, attn_proj.astype(jnp.float32), precision=highest)
    share = jnp.where(lax.axis_index("head") == 0, 1.0, 0.0)
    counts = TOK * page_windows.astype(jnp.float32)
    total = sum_over_devices(page_tokens * share + projected)
    pooled = total / counts[:, None]
    page_count = page_windows.shape[0]
    page_normed = layer_norm(pooled, page_gain)
    page_qkv = jnp.dot(
        page_normed, page_weight.reshape(D, 3 * local_width), preferred_element_type=jnp.float32
    ).astype(jnp.bfloat16)
    doc_ends = jnp.cumsum(doc_pages)
    page_ids = jnp.arange(page_count, dtype=jnp.int32)
    doc_of = jnp.sum((page_ids[:, None] >= doc_ends[None, :]).astype(jnp.int32), axis=1)
    same_doc = doc_of[:, None] == doc_of[None, :]
    context = attention(
        page_qkv[:, :local_width],
        page_qkv[:, local_width : 2 * local_width],
        page_qkv[:, 2 * local_width :],
        same_doc,
        local_heads,
    )
    branch = jnp.dot(context, page_proj, preferred_element_type=jnp.float32)
    my_share = keep_share(branch)
    column_start = lax.axis_index("head") * my_share.shape[1]
    page_out = lax.dynamic_slice_in_dim(pooled, column_start, my_share.shape[1], 1) + my_share
    return (mixed, page_out)


def solution(mesh):
    placed = (
        P(("rep", "pack"), None),
        P(),
        P(None, None, "head"),
        P("head", None),
        P(),
        P(None, None, "head"),
        P("head", None),
        P("rep"),
        P("rep"),
        P("rep"),
    )
    return jax.shard_map(
        shards,
        mesh=mesh,
        in_specs=placed,
        out_specs=(P(("rep", "pack"), "head"), P("rep", "head")),
        check_vma=False,
    )
```

```python
import functools
import math

import jax
import jax.numpy as jnp
import numpy as np
from jax import lax
from jax.experimental import pallas as pl
from jax.experimental.pallas import tpu as pltpu
from jax.sharding import PartitionSpec as P

D = 1024
HDIM = 32
WIN = 16
HALO = 4
HALO_WIN = 4
TOK = WIN * WIN
STRIP = WIN * HALO
CORNER = HALO * HALO
SIDE_KEYS = 4 * STRIP + 4 * CORNER
KEYS = TOK + SIDE_KEYS
SUM_LEAST = 2.0**-60
SUM_MOST = 2.0**60
EPS = 1e-05
LOG2E = 1.4426950408889634
OFFSETS = ((-1, 0), (1, 0), (0, -1), (0, 1), (-1, -1), (-1, 1), (1, -1), (1, 1))


def edge_rows():
    table = np.zeros((2 * STRIP, TOK), np.float32)
    for i in range(STRIP):
        row, col = i // HALO, i % HALO
        table[i, row * WIN + col] = 1.0
        table[STRIP + i, row * WIN + WIN - HALO + col] = 1.0
    return jnp.asarray(table, jnp.bfloat16)


def nn_dot(a, b):
    return jnp.dot(a, b, preferred_element_type=jnp.float32)


def normalize(values, gain):
    center = values - jnp.mean(values, axis=-1, keepdims=True)
    spread = jnp.mean(center * center, axis=-1, keepdims=True)
    return (center * lax.rsqrt(spread + EPS) * gain).astype(jnp.bfloat16)


def qkv_kernel(
    count,
    win_count,
    width,
    tok_ref,
    gain_ref,
    w_hbm,
    sel_ref,
    qt_ref,
    k_ref,
    v_ref,
    ek_ref,
    ev_ref,
    tsum_ref,
    tok_s,
    w_s,
    even_s,
    odd_s,
    own_sem,
    w_sem,
    send_sem,
    recv_sem,
):
    me = lax.axis_index("pack")
    after = {"pack": lax.rem(me + 1, count)}
    before = {"pack": lax.rem(me + count - 1, count)}
    groups = width // 128

    def own(w):
        return pltpu.make_async_copy(
            tok_ref.at[pl.ds(w * TOK, TOK)], tok_s.at[w], own_sem.at[w]
        )

    weight = pltpu.make_async_copy(w_hbm, w_s, w_sem.at[0])
    for w in range(win_count):
        own(w).start()
        if w == 0:
            weight.start()

    pieces = [
        (after, (win_count - 1) * TOK, TOK, win_count, 0),
        (before, 0, TOK, win_count + 2, 0),
    ]
    for i in range(HALO_WIN - 1):
        high = (win_count - HALO_WIN + i + 1) * TOK - STRIP
        pieces.append((after, high, STRIP, win_count + 1, i * STRIP))
        pieces.append((before, (i + 1) * TOK, STRIP, win_count + 3, i * STRIP))
    copies = [
        pltpu.make_async_remote_copy(
            src_ref=tok_ref.at[pl.ds(start, size)],
            dst_ref=tok_s.at[block, pl.ds(row, size)],
            send_sem=send_sem.at[i],
            recv_sem=recv_sem.at[i],
            device_id=where,
            device_id_type=pl.DeviceIdType.MESH,
        )
        for i, (where, start, size, block, row) in enumerate(pieces)
    ]
    barrier = pltpu.get_barrier_semaphore()
    for where in (after, before):
        pl.semaphore_signal(barrier, inc=1, device_id=where, device_id_type=pl.DeviceIdType.MESH)
    spare = (HALO_WIN - 1) * STRIP
    for block in (win_count + 1, win_count + 3):
        tok_s[block, spare:] = jnp.zeros((TOK - spare, D), tok_s.dtype)

    def norm(block, out_s):
        for lo in range(0, TOK, 32):
            values = tok_s[block, lo : lo + 32].astype(jnp.float32)
            out_s[lo : lo + 32] = normalize(values, gain_ref[...])
        sums = nn_dot(jnp.ones((16, TOK), jnp.bfloat16), tok_s[block])
        tsum_ref[block] = sums[:1]

    def project(block, in_s):
        values = in_s[...]
        q = nn_dot(values, w_s[0]).astype(jnp.bfloat16)
        for g in range(groups):
            qt_ref[block, g] = q[:, g * 128 : (g + 1) * 128].T
        for part, out_ref, edge_ref in ((1, k_ref, ek_ref), (2, v_ref, ev_ref)):
            made = nn_dot(values, w_s[part]).astype(jnp.bfloat16)
            edge = nn_dot(sel_ref[...], made).astype(jnp.bfloat16)
            for g in range(groups):
                out_ref[block, g] = made[:, g * 128 : (g + 1) * 128]
                edge_ref[block, g] = edge[:, g * 128 : (g + 1) * 128]

    own(0).wait()
    norm(0, even_s)
    pl.semaphore_wait(barrier, 2)
    for copy in copies:
        copy.start()
    weight.wait()

    def arrive(block):
        @pl.when(block < win_count)
        def _():
            own(jnp.minimum(block, win_count - 1)).wait()

        @pl.when(block == win_count)
        def _():
            for copy in copies:
                copy.wait_recv()

    blocks = win_count + 4

    def pair(i, carry):
        arrive(2 * i + 1)
        project(2 * i, even_s)
        norm(2 * i + 1, odd_s)
        arrive(2 * i + 2)
        project(2 * i + 1, odd_s)
        norm(2 * i + 2, even_s)
        return carry

    lax.fori_loop(0, blocks // 2 - 1, pair, 0)
    project(blocks - 2, even_s)
    norm(blocks - 1, odd_s)
    project(blocks - 1, odd_s)
    for copy in copies:
        copy.wait_send()


def window_qkv(tokens, gain, weight):
    win_count = tokens.shape[0] // TOK
    width = weight.shape[2]
    groups = width // 128
    blocks = win_count + 4
    bf = jnp.bfloat16
    vmem = pl.BlockSpec(memory_space=pltpu.VMEM)
    hbm = pl.BlockSpec(memory_space=pl.ANY)
    return pl.pallas_call(
        functools.partial(qkv_kernel, lax.axis_size("pack"), win_count, width),
        out_shape=(
            pltpu.VMEM((blocks, groups, 128, TOK), bf),
            pltpu.VMEM((blocks, groups, TOK, 128), bf),
            pltpu.VMEM((blocks, groups, TOK, 128), bf),
            pltpu.VMEM((blocks, groups, 2 * STRIP, 128), bf),
            pltpu.VMEM((blocks, groups, 2 * STRIP, 128), bf),
            pltpu.VMEM((blocks, 1, D), jnp.float32),
        ),
        in_specs=[hbm, vmem, hbm, vmem],
        out_specs=(vmem,) * 6,
        scratch_shapes=[
            pltpu.VMEM((blocks, TOK, D), bf),
            pltpu.VMEM((3, D, width), bf),
            pltpu.VMEM((TOK, D), bf),
            pltpu.VMEM((TOK, D), bf),
            pltpu.SemaphoreType.DMA((win_count,)),
            pltpu.SemaphoreType.DMA((1,)),
            pltpu.SemaphoreType.DMA((8,)),
            pltpu.SemaphoreType.DMA((8,)),
        ],
        compiler_params=pltpu.CompilerParams(
            collective_id=1, has_side_effects=True, vmem_limit_bytes=24 << 20
        ),
    )(tokens, gain.reshape(1, D), weight.transpose(1, 0, 2), edge_rows())


def attend_kernel(
    win_count,
    width,
    pages,
    windows_ref,
    across_ref,
    qt_ref,
    k_ref,
    v_ref,
    ek_ref,
    ev_ref,
    mixed_hbm,
    msum_ref,
    pk_s,
    pv_s,
    mask_s,
    prob_s,
    out_s,
    low_s,
    high_s,
    out_sem,
):
    first = lax.axis_index("pack") * win_count
    groups = width // 128
    per = 128 // HDIM
    extra_most = KEYS - TOK
    factor = LOG2E / math.sqrt(HDIM)
    bf = jnp.bfloat16

    def copy_out(w):
        slot = lax.rem(w, 2)
        return pltpu.make_async_copy(
            out_s.at[slot], mixed_hbm.at[pl.ds(w * TOK, TOK)], out_sem.at[slot]
        )

    def find(p, carry):
        page, begin, run = carry
        run = run + windows_ref[p]
        passed = run <= first
        return jnp.where(passed, p + 1, page), jnp.where(passed, run, begin), run

    def locate(block):
        inner = jnp.where(block == -1, win_count, jnp.where(block == win_count, win_count + 2, block))
        inner = jnp.where(block < -1, win_count + 1, inner)
        return jnp.where(block > win_count, win_count + 3, inner)

    def pack(w, page, begin):
        across = across_ref[page]
        total = windows_ref[page]
        inside = first + w - begin
        row = lax.div(inside, across)
        col = inside - row * across
        filled = jnp.int32(0)
        for a, b in OFFSETS:
            place = inside + a * across + b
            valid = (col + b >= 0) & (col + b < across) & (row + a >= 0) & (place < total)
            near = w + a * across + b
            block = locate(near)
            size = CORNER if a and b else STRIP
            if a < 0:
                index = jnp.where(near < -1, near + HALO_WIN, (TOK - size) // size if b == 0 else 3)
            elif a > 0:
                index = jnp.where(near > win_count, near - win_count - 1, 0)
            else:
                index = 0
            if b == 0:
                start = index * STRIP
            else:
                start = index * CORNER + (STRIP if b < 0 else 0)
            keys, values = (k_ref, v_ref) if b == 0 else (ek_ref, ev_ref)

            @pl.when(valid)
            def _(block=block, start=start, size=size, keys=keys, values=values, filled=filled):
                source = pl.ds(pl.multiple_of(start, 16), size)
                target = pl.ds(pl.multiple_of(filled, 16), size)
                pk_s[:, target, :] = keys[block, :, source, :]
                pv_s[:, target, :] = values[block, :, source, :]

            filled = filled + jnp.where(valid, size, 0)
        blank = jnp.zeros((groups, 3 * CORNER, 128), bf)
        target = pl.ds(pl.multiple_of(filled, 16), 3 * CORNER)
        pk_s[:, target, :] = blank
        pv_s[:, target, :] = blank
        lane = lax.broadcasted_iota(jnp.int32, mask_s.shape, 1)
        mask_s[...] = jnp.where(lane < filled, 1.0, 0.0).astype(bf)
        return filled

    def finish(w, g, parts):
        piece = jnp.concatenate(parts, axis=0).T
        lanes = pl.ds(pl.multiple_of(g * 128, 128), 128)
        out_s[lax.rem(w, 2), :, lanes] = piece
        msum_ref[w, :, lanes] = jnp.sum(piece.astype(jnp.float32), axis=0, keepdims=True)

    def spread(queries, j):
        above = [jnp.zeros((j * HDIM, TOK), bf)] if j else []
        below = [jnp.zeros((128 - (j + 1) * HDIM, TOK), bf)] if j + 1 < per else []
        return jnp.concatenate(above + [queries[j * HDIM : (j + 1) * HDIM]] + below, axis=0)

    def fast(w, extra):
        keys = TOK + extra
        for g in range(groups):
            queries = qt_ref[w, g]
            rows = jnp.concatenate([k_ref[w, g], pk_s[g, :extra]], axis=0) if extra else k_ref[w, g]
            for j in range(per):
                scores = nn_dot(rows, spread(queries, j))
                prob_s[g * per + j, :keys] = jnp.exp2(scores * factor).astype(bf)
        low, high = low_s[...], high_s[...]
        for g in range(groups):
            values = v_ref[w, g].T
            marks = jnp.ones((16, TOK), bf)
            if extra:
                values = jnp.concatenate([values, pv_s[g, :extra].T], axis=1)
                marks = jnp.concatenate([marks, mask_s[:, :extra]], axis=1)
            parts = []
            for j in range(per):
                lhs = jnp.concatenate([values[j * HDIM : (j + 1) * HDIM], marks], axis=0)
                summed = nn_dot(lhs, prob_s[g * per + j, :keys])
                total = summed[HDIM : HDIM + 1]
                low = jnp.minimum(low, total)
                high = jnp.maximum(high, total)
                parts.append((summed[:HDIM] * (1.0 / total)).astype(bf))
            finish(w, g, parts)
        low_s[...] = low
        high_s[...] = high

    def safe(w, filled):
        row = lax.broadcasted_iota(jnp.int32, (extra_most, TOK), 0)

        def group(g, carry):
            queries = qt_ref[w, g]
            values = jnp.concatenate([v_ref[w, g].T, pv_s[g, :extra_most].T], axis=1)
            parts = []
            for j in range(per):
                qz = spread(queries, j)
                near = nn_dot(pk_s[g, :extra_most], qz) * factor
                near = jnp.where(row < filled, near, -1e30)
                scores = jnp.concatenate([nn_dot(k_ref[w, g], qz) * factor, near], axis=0)
                weights = jnp.exp2(scores - jnp.max(scores, axis=0, keepdims=True))
                total = jnp.sum(weights, axis=0, keepdims=True)
                summed = nn_dot(values[j * HDIM : (j + 1) * HDIM], weights.astype(bf))
                parts.append((summed * (1.0 / total)).astype(bf))
            finish(w, g, parts)
            return carry

        lax.fori_loop(0, groups, group, 0)

    def sweep(guarded):
        def step(w, carry):
            page, begin = carry
            end = begin + windows_ref[page]
            passed = first + w >= end
            page = jnp.where(passed, page + 1, page)
            begin = jnp.where(passed, end, begin)
            filled = pack(w, page, begin)

            @pl.when(w >= 2)
            def _():
                copy_out(w - 2).wait()

            if guarded:
                safe(w, filled)
            else:
                chunks = lax.div(filled + STRIP - 1, STRIP)
                for c in range(extra_most // STRIP + 1):

                    @pl.when(chunks == c)
                    def _(c=c):
                        fast(w, c * STRIP)

            copy_out(w).start()
            return page, begin

        zero = jnp.int32(0)
        page, begin, _ = lax.fori_loop(0, pages, find, (zero, zero, zero))
        lax.fori_loop(0, win_count, step, (page, begin))
        copy_out(win_count - 2).wait()
        copy_out(win_count - 1).wait()

    pk_s[...] = jnp.zeros_like(pk_s)
    pv_s[...] = jnp.zeros_like(pv_s)
    low_s[...] = jnp.ones_like(low_s)
    high_s[...] = jnp.ones_like(high_s)
    sweep(False)
    calm = (jnp.min(low_s[...]) >= SUM_LEAST) & (jnp.max(high_s[...]) <= SUM_MOST)

    @pl.when(jnp.logical_not(calm))
    def _():
        sweep(True)


def window_attention(tables, page_windows, page_width, win_count):
    qt, k, v, ek, ev = tables
    groups = k.shape[1]
    width = groups * 128
    bf = jnp.bfloat16
    vmem = pl.BlockSpec(memory_space=pltpu.VMEM)
    smem = pl.BlockSpec(memory_space=pltpu.SMEM)
    hbm = pl.BlockSpec(memory_space=pl.ANY)
    room = KEYS - TOK + STRIP
    arrays = [pltpu.with_memory_space_constraint(a, pltpu.VMEM) for a in tables]
    return pl.pallas_call(
        functools.partial(attend_kernel, win_count, width, page_windows.shape[0]),
        out_shape=(
            jax.ShapeDtypeStruct((win_count * TOK, width), bf),
            jax.ShapeDtypeStruct((win_count, 1, width), jnp.float32),
        ),
        in_specs=[smem, smem] + [vmem] * 5,
        out_specs=(hbm, vmem),
        scratch_shapes=[
            pltpu.VMEM((groups, room, 128), bf),
            pltpu.VMEM((groups, room, 128), bf),
            pltpu.VMEM((16, room), bf),
            pltpu.VMEM((width // HDIM, KEYS, TOK), bf),
            pltpu.VMEM((2, TOK, width), bf),
            pltpu.VMEM((1, TOK), jnp.float32),
            pltpu.VMEM((1, TOK), jnp.float32),
            pltpu.SemaphoreType.DMA((2,)),
        ],
        compiler_params=pltpu.CompilerParams(vmem_limit_bytes=16 << 20),
    )(page_windows, page_width, *arrays)


def sum_kernel(count, heads, x_ref, out_ref, land, acc, full, send_sem, recv_sem):
    me = lax.axis_index("pack") * heads + lax.axis_index("head")

    def device(k):
        other = lax.rem(me + k, count)
        return other, {"pack": lax.div(other, heads), "head": lax.rem(other, heads)}

    barrier = pltpu.get_barrier_semaphore()

    @pl.loop(1, count)
    def _(k):
        pl.semaphore_signal(
            barrier, inc=1, device_id=device(k)[1], device_id_type=pl.DeviceIdType.MESH
        )

    pl.semaphore_wait(barrier, count - 1)

    def copy(k, phase):
        other, where = device(k)
        return pltpu.make_async_remote_copy(
            src_ref=acc if phase else x_ref.at[other],
            dst_ref=full.at[me] if phase else land.at[k],
            send_sem=send_sem.at[phase, k],
            recv_sem=recv_sem.at[phase, k],
            device_id=where,
            device_id_type=pl.DeviceIdType.MESH,
        )

    for phase in (0, 1):

        @pl.loop(1, count)
        def _(k):
            copy(k, phase).start()

        if phase:
            full[me] = acc[...]
        else:
            land[0] = x_ref[me]

        @pl.loop(1, count)
        def _(k):
            copy(k, phase).wait_recv()

        if phase:
            out_ref[...] = full[...]
        else:
            acc[...] = jnp.sum(land[...], axis=0)

    @pl.loop(1, count)
    def _(k):
        copy(k, 0).wait_send()
        copy(k, 1).wait_send()


def sum_over_devices(values):
    heads = lax.axis_size("head")
    count = lax.axis_size("pack") * heads
    rows = values.size // (count * 128)
    shape = (count, rows, 128)
    total = pl.pallas_call(
        lambda *refs: sum_kernel(count, heads, *refs),
        out_shape=jax.ShapeDtypeStruct(shape, jnp.float32),
        in_specs=[pl.BlockSpec(memory_space=pltpu.VMEM)],
        out_specs=pl.BlockSpec(memory_space=pltpu.VMEM),
        scratch_shapes=[
            pltpu.VMEM(shape, jnp.float32),
            pltpu.VMEM(shape[1:], jnp.float32),
            pltpu.VMEM(shape, jnp.float32),
            pltpu.SemaphoreType.DMA((2, count)),
            pltpu.SemaphoreType.DMA((2, count)),
        ],
        compiler_params=pltpu.CompilerParams(collective_id=0, has_side_effects=True),
    )(values.reshape(shape))
    return total.reshape(values.shape)


def keep_share(values):
    heads = lax.axis_size("head")
    me = lax.axis_index("head")
    columns = values.shape[1] // heads
    rounded = values.astype(jnp.bfloat16)

    def part(k):
        start = lax.rem(me + k, heads) * columns
        return lax.dynamic_slice_in_dim(rounded, start, columns, 1)

    total = part(0).astype(jnp.float32)
    for k in range(1, heads):
        pairs = [(i, (i + k) % heads) for i in range(heads)]
        total = total + lax.ppermute(part(k), "head", pairs).astype(jnp.float32)
    return total


def layer_norm(values, gain):
    values = values.astype(jnp.float32)
    return normalize(values, gain)


def page_member(window_ids, page_windows):
    page_ends = jnp.cumsum(page_windows)
    page_starts = page_ends - page_windows
    return (window_ids[:, None] >= page_starts[None, :]) & (
        window_ids[:, None] < page_ends[None, :]
    )


def attention(query, keys, values, mask, heads):
    qlen, width = query.shape
    depth = width // heads
    q_heads = query.reshape(qlen, heads, depth)
    k_heads = keys.reshape(-1, heads, depth)
    v_heads = values.reshape(-1, heads, depth)
    scores = jnp.einsum(
        "qhd,khd->hqk", q_heads, k_heads, preferred_element_type=jnp.float32
    ) / math.sqrt(depth)
    scores = jnp.where(mask[None], scores, -1e30)
    top_score = jnp.max(scores, axis=-1, keepdims=True)
    weights = jnp.exp(scores - top_score)
    probs = (weights / jnp.sum(weights, axis=-1, keepdims=True)).astype(jnp.bfloat16)
    output = jnp.einsum("hqk,khd->qhd", probs, v_heads, preferred_element_type=jnp.float32)
    return output.reshape(qlen, width).astype(jnp.bfloat16)


def shards(
    tokens,
    ln_gain,
    attn_weight,
    attn_proj,
    page_gain,
    page_weight,
    page_proj,
    page_windows,
    page_width,
    doc_pages,
):
    win_count = tokens.shape[0] // TOK
    local_width = attn_weight.shape[2]
    local_heads = local_width // HDIM
    window_ids = lax.axis_index("pack") * win_count + jnp.arange(win_count, dtype=jnp.int32)
    *tables, token_sums = window_qkv(tokens, ln_gain, attn_weight)
    mixed, mixed_sums = window_attention(tables, page_windows, page_width, win_count)
    token_sums = token_sums[:win_count]
    member = page_member(window_ids, page_windows).astype(jnp.float32)
    highest = lax.Precision.HIGHEST
    page_tokens = jnp.dot(member.T, token_sums[:, 0], precision=highest)
    page_mixed = jnp.dot(member.T, mixed_sums[:, 0], precision=highest)
    projected = jnp.dot(page_mixed, attn_proj.astype(jnp.float32), precision=highest)
    share = jnp.where(lax.axis_index("head") == 0, 1.0, 0.0)
    counts = TOK * page_windows.astype(jnp.float32)
    total = sum_over_devices(page_tokens * share + projected)
    pooled = total / counts[:, None]
    page_count = page_windows.shape[0]
    page_normed = layer_norm(pooled, page_gain)
    page_qkv = jnp.dot(
        page_normed, page_weight.reshape(D, 3 * local_width), preferred_element_type=jnp.float32
    ).astype(jnp.bfloat16)
    doc_ends = jnp.cumsum(doc_pages)
    page_ids = jnp.arange(page_count, dtype=jnp.int32)
    doc_of = jnp.sum((page_ids[:, None] >= doc_ends[None, :]).astype(jnp.int32), axis=1)
    same_doc = doc_of[:, None] == doc_of[None, :]
    context = attention(
        page_qkv[:, :local_width],
        page_qkv[:, local_width : 2 * local_width],
        page_qkv[:, 2 * local_width :],
        same_doc,
        local_heads,
    )
    branch = jnp.dot(context, page_proj, preferred_element_type=jnp.float32)
    my_share = keep_share(branch)
    column_start = lax.axis_index("head") * my_share.shape[1]
    page_out = lax.dynamic_slice_in_dim(pooled, column_start, my_share.shape[1], 1) + my_share
    return (mixed, page_out)


def solution(mesh):
    placed = (
        P(("rep", "pack"), None),
        P(),
        P(None, None, "head"),
        P("head", None),
        P(),
        P(None, None, "head"),
        P("head", None),
        P("rep"),
        P("rep"),
        P("rep"),
    )
    return jax.shard_map(
        shards,
        mesh=mesh,
        in_specs=placed,
        out_specs=(P(("rep", "pack"), "head"), P("rep", "head")),
        check_vma=False,
    )
```

```python
import functools
import math

import jax
import jax.numpy as jnp
import numpy as np
from jax import lax
from jax.experimental import pallas as pl
from jax.experimental.pallas import tpu as pltpu
from jax.sharding import PartitionSpec as P

D = 1024
HDIM = 32
WIN = 16
HALO = 4
HALO_WIN = 4
TOK = WIN * WIN
STRIP = WIN * HALO
CORNER = HALO * HALO
SIDE_KEYS = 4 * STRIP + 4 * CORNER
KEYS = TOK + SIDE_KEYS
SUM_LEAST = 2.0**-60
SUM_MOST = 2.0**60
ROWS = 16
EPS = 1e-05
LOG2E = 1.4426950408889634
OFFSETS = ((-1, 0), (1, 0), (0, -1), (0, 1), (-1, -1), (-1, 1), (1, -1), (1, 1))


def edge_rows():
    table = np.zeros((2 * STRIP, TOK), np.float32)
    for i in range(STRIP):
        row, col = i // HALO, i % HALO
        table[i, row * WIN + col] = 1.0
        table[STRIP + i, row * WIN + WIN - HALO + col] = 1.0
    return jnp.asarray(table, jnp.bfloat16)


def nn_dot(a, b):
    return jnp.dot(a, b, preferred_element_type=jnp.float32)


def normalize(values, gain):
    center = values - jnp.mean(values, axis=-1, keepdims=True)
    spread = jnp.mean(center * center, axis=-1, keepdims=True)
    return (center * lax.rsqrt(spread + EPS) * gain).astype(jnp.bfloat16)


def qkv_kernel(
    count,
    win_count,
    width,
    tok_hbm,
    gain_ref,
    w_hbm,
    sel_ref,
    qt_ref,
    k_ref,
    v_ref,
    ek_ref,
    ev_ref,
    tsum_ref,
    tok_s,
    side_s,
    edge_s,
    w_s,
    even_s,
    odd_s,
    own_sem,
    w_sem,
    send_sem,
    recv_sem,
):
    me = lax.axis_index("pack")
    after = {"pack": lax.rem(me + 1, count)}
    before = {"pack": lax.rem(me + count - 1, count)}
    groups = width // 128
    bf = jnp.bfloat16

    def own(w):
        return pltpu.make_async_copy(
            tok_hbm.at[pl.ds(w * TOK, TOK)], tok_s.at[w], own_sem.at[w]
        )

    weight = pltpu.make_async_copy(w_hbm, w_s, w_sem.at[0])
    own(0).start()
    own(win_count - 1).start()
    weight.start()
    for w in range(1, win_count - 1):
        own(w).start()

    pieces = [
        (after, edge_s.at[0], side_s.at[pl.ds(STRIP, STRIP)]),
        (before, edge_s.at[1], side_s.at[pl.ds(0, STRIP)]),
    ]
    for i in range(HALO_WIN):
        place = pl.ds(i * STRIP, STRIP)
        high = (win_count - HALO_WIN + i + 1) * TOK - STRIP
        pieces.append((after, tok_hbm.at[pl.ds(high, STRIP)], tok_s.at[win_count, place]))
        pieces.append((before, tok_hbm.at[pl.ds(i * TOK, STRIP)], tok_s.at[win_count + 1, place]))
    copies = [
        pltpu.make_async_remote_copy(
            src_ref=source,
            dst_ref=target,
            send_sem=send_sem.at[i],
            recv_sem=recv_sem.at[i],
            device_id=where,
            device_id_type=pl.DeviceIdType.MESH,
        )
        for i, (where, source, target) in enumerate(pieces)
    ]
    forward, backward = me < count - 1, me > 0
    barrier = pltpu.get_barrier_semaphore()
    for there, where in ((forward, after), (backward, before)):

        @pl.when(there)
        def _(where=where):
            pl.semaphore_signal(
                barrier, inc=1, device_id=where, device_id_type=pl.DeviceIdType.MESH
            )

    @pl.when(jnp.logical_not(backward))
    def _():
        tok_s[win_count] = jnp.zeros((TOK, D), bf)
        side_s[STRIP:] = jnp.zeros((STRIP, D), bf)

    @pl.when(jnp.logical_not(forward))
    def _():
        tok_s[win_count + 1] = jnp.zeros((TOK, D), bf)
        side_s[:STRIP] = jnp.zeros((STRIP, D), bf)

    def norm(rows, out_s):
        total = jnp.zeros((1, D), jnp.float32)
        for lo in range(0, rows.shape[0], 32):
            values = rows[lo : lo + 32].astype(jnp.float32)
            out_s[lo : lo + 32] = normalize(values, gain_ref[...])
            total = total + jnp.sum(values, axis=0, keepdims=True)
        return total

    def keys_values(values, block):
        for part, out_ref, edge_ref in ((1, k_ref, ek_ref), (2, v_ref, ev_ref)):
            made = nn_dot(values, w_s[part]).astype(bf)
            if block is None:
                edge, at = made, win_count + 2
            else:
                edge, at = nn_dot(sel_ref[...], made).astype(bf), block
            for g in range(groups):
                lanes = slice(g * 128, (g + 1) * 128)
                if block is not None:
                    out_ref[block, g] = made[:, lanes]
                edge_ref[at, g] = edge[:, lanes]

    def project(block, in_s):
        values = in_s[...]
        q = nn_dot(values, w_s[0]).astype(bf)
        for g in range(groups):
            qt_ref[block, g] = q[:, g * 128 : (g + 1) * 128].T
        keys_values(values, block)

    own(win_count - 1).wait()
    edge_s[0] = nn_dot(sel_ref[STRIP:], tok_s[win_count - 1]).astype(bf)
    own(0).wait()
    edge_s[1] = nn_dot(sel_ref[:STRIP], tok_s[0]).astype(bf)
    pl.semaphore_wait(barrier, jnp.where(forward, 1, 0) + jnp.where(backward, 1, 0))
    for i, copy in enumerate(copies):
        pl.when((forward, backward)[i % 2])(copy.start)
    tsum_ref[pl.ds(0, 1)] = norm(tok_s.at[0], even_s)
    weight.wait()

    def arrive(block):
        @pl.when(block < win_count - 1)
        def _():
            own(jnp.minimum(block, win_count - 2)).wait()

        @pl.when(block == win_count)
        def _():
            for i, copy in enumerate(copies):
                pl.when((backward, forward)[i % 2])(copy.wait_recv)

    def pair(i, carry):
        for j, in_s, out_s in ((0, even_s, odd_s), (1, odd_s, even_s)):
            block = 2 * i + j
            arrive(block + 1)
            project(block, in_s)
            tsum_ref[pl.ds(block + 1, 1)] = norm(tok_s.at[block + 1], out_s)
        return carry

    lax.fori_loop(0, win_count // 2, pair, 0)
    keys_values(even_s[...], win_count)
    norm(tok_s.at[win_count + 1], odd_s)
    keys_values(odd_s[...], win_count + 1)
    norm(side_s, even_s)
    keys_values(even_s[: 2 * STRIP], None)
    for i, copy in enumerate(copies):
        pl.when((forward, backward)[i % 2])(copy.wait_send)


def window_qkv(tokens, gain, weight):
    win_count = tokens.shape[0] // TOK
    width = weight.shape[2]
    groups = width // 128
    bf = jnp.bfloat16
    vmem = pl.BlockSpec(memory_space=pltpu.VMEM)
    hbm = pl.BlockSpec(memory_space=pltpu.HBM)
    edges = (win_count + 3, groups, 2 * STRIP, 128)
    return pl.pallas_call(
        functools.partial(qkv_kernel, lax.axis_size("pack"), win_count, width),
        out_shape=(
            pltpu.VMEM((win_count, groups, 128, TOK), bf),
            pltpu.VMEM((win_count + 2, groups, TOK, 128), bf),
            pltpu.VMEM((win_count + 2, groups, TOK, 128), bf),
            pltpu.VMEM(edges, bf),
            pltpu.VMEM(edges, bf),
            pltpu.VMEM((ROWS, D), jnp.float32),
        ),
        in_specs=[hbm, vmem, hbm, vmem],
        out_specs=(vmem,) * 6,
        scratch_shapes=[
            pltpu.VMEM((win_count + 2, TOK, D), bf),
            pltpu.VMEM((2 * STRIP, D), bf),
            pltpu.VMEM((2, STRIP, D), bf),
            pltpu.VMEM((3, D, width), bf),
            pltpu.VMEM((TOK, D), bf),
            pltpu.VMEM((TOK, D), bf),
            pltpu.SemaphoreType.DMA((win_count,)),
            pltpu.SemaphoreType.DMA((1,)),
            pltpu.SemaphoreType.DMA((2 * HALO_WIN + 2,)),
            pltpu.SemaphoreType.DMA((2 * HALO_WIN + 2,)),
        ],
        compiler_params=pltpu.CompilerParams(
            collective_id=1, has_side_effects=True, vmem_limit_bytes=24 << 20
        ),
    )(
        pltpu.with_memory_space_constraint(tokens, pltpu.HBM),
        gain.reshape(1, D),
        pltpu.with_memory_space_constraint(weight.transpose(1, 0, 2), pltpu.HBM),
        edge_rows(),
    )


def attend_kernel(
    win_count,
    width,
    pages,
    windows_ref,
    across_ref,
    qt_ref,
    k_ref,
    v_ref,
    ek_ref,
    ev_ref,
    proj_hbm,
    mixed_hbm,
    projected_ref,
    msum_s,
    proj_s,
    proj_sem,
    pk_s,
    pv_s,
    mask_s,
    prob_s,
    out_s,
    low_s,
    high_s,
    out_sem,
):
    first = lax.axis_index("pack") * win_count
    groups = width // 128
    per = 128 // HDIM
    extra_most = KEYS - TOK
    factor = LOG2E / math.sqrt(HDIM)
    bf = jnp.bfloat16

    def copy_out(w):
        slot = lax.rem(w, 2)
        return pltpu.make_async_copy(
            out_s.at[slot], mixed_hbm.at[pl.ds(w * TOK, TOK)], out_sem.at[slot]
        )

    def find(p, carry):
        page, begin, run = carry
        run = run + windows_ref[p]
        passed = run <= first
        return jnp.where(passed, p + 1, page), jnp.where(passed, run, begin), run

    def pack(w, page, begin):
        across = across_ref[page]
        total = windows_ref[page]
        inside = first + w - begin
        row = lax.div(inside, across)
        col = inside - row * across
        filled = jnp.int32(0)
        for a, b in OFFSETS:
            place = inside + a * across + b
            valid = (col + b >= 0) & (col + b < across) & (row + a >= 0) & (place < total)
            near = w + a * across + b
            size = CORNER if a and b else STRIP
            early, late = near < 0, near >= win_count
            if a < 0:
                block = jnp.where(early, win_count, near)
                index = jnp.where(early, near + HALO_WIN, HALO_WIN - 1)
            elif a > 0:
                block = jnp.where(late, win_count + 1, near)
                index = jnp.where(late, near - win_count, 0)
            else:
                block = jnp.where(early | late, win_count + 2, near)
                index = 0
            start = index * size + (STRIP if b < 0 else 0)
            keys, values = (ek_ref, ev_ref) if b else (k_ref, v_ref)

            @pl.when(valid)
            def _(block=block, start=start, size=size, keys=keys, values=values, filled=filled):
                source = pl.ds(pl.multiple_of(start, 16), size)
                target = pl.ds(pl.multiple_of(filled, 16), size)
                pk_s[:, target, :] = keys[block, :, source, :]
                pv_s[:, target, :] = values[block, :, source, :]

            filled = filled + jnp.where(valid, size, 0)
        blank = jnp.zeros((groups, 3 * CORNER, 128), bf)
        target = pl.ds(pl.multiple_of(filled, 16), 3 * CORNER)
        pk_s[:, target, :] = blank
        pv_s[:, target, :] = blank
        lane = lax.broadcasted_iota(jnp.int32, mask_s.shape, 1)
        mask_s[...] = jnp.where(lane < filled, 1.0, 0.0).astype(bf)
        return filled

    def finish(w, g, parts):
        piece = jnp.concatenate(parts, axis=0).T
        lanes = pl.ds(pl.multiple_of(g * 128, 128), 128)
        out_s[lax.rem(w, 2), :, lanes] = piece
        msum_s[w, :, lanes] = jnp.sum(piece.astype(jnp.float32), axis=0, keepdims=True)

    def spread(queries, j):
        above = [jnp.zeros((j * HDIM, TOK), bf)] if j else []
        below = [jnp.zeros((128 - (j + 1) * HDIM, TOK), bf)] if j + 1 < per else []
        return jnp.concatenate(above + [queries[j * HDIM : (j + 1) * HDIM]] + below, axis=0)

    def fast(w, extra):
        keys = TOK + extra
        for g in range(groups):
            queries = qt_ref[w, g]
            rows = jnp.concatenate([k_ref[w, g], pk_s[g, :extra]], axis=0) if extra else k_ref[w, g]
            for j in range(per):
                scores = nn_dot(rows, spread(queries, j))
                prob_s[g * per + j, :keys] = jnp.exp2(scores * factor).astype(bf)
        low, high = low_s[...], high_s[...]
        for g in range(groups):
            values = v_ref[w, g].T
            marks = jnp.ones((16, TOK), bf)
            if extra:
                values = jnp.concatenate([values, pv_s[g, :extra].T], axis=1)
                marks = jnp.concatenate([marks, mask_s[:, :extra]], axis=1)
            parts = []
            for j in range(per):
                lhs = jnp.concatenate([values[j * HDIM : (j + 1) * HDIM], marks], axis=0)
                summed = nn_dot(lhs, prob_s[g * per + j, :keys])
                total = summed[HDIM : HDIM + 1]
                low = jnp.minimum(low, total)
                high = jnp.maximum(high, total)
                parts.append((summed[:HDIM] * (1.0 / total)).astype(bf))
            finish(w, g, parts)
        low_s[...] = low
        high_s[...] = high

    def safe(w, filled):
        row = lax.broadcasted_iota(jnp.int32, (extra_most, TOK), 0)

        def group(g, carry):
            queries = qt_ref[w, g]
            values = jnp.concatenate([v_ref[w, g].T, pv_s[g, :extra_most].T], axis=1)
            parts = []
            for j in range(per):
                qz = spread(queries, j)
                near = nn_dot(pk_s[g, :extra_most], qz) * factor
                near = jnp.where(row < filled, near, -1e30)
                scores = jnp.concatenate([nn_dot(k_ref[w, g], qz) * factor, near], axis=0)
                weights = jnp.exp2(scores - jnp.max(scores, axis=0, keepdims=True))
                total = jnp.sum(weights, axis=0, keepdims=True)
                summed = nn_dot(values[j * HDIM : (j + 1) * HDIM], weights.astype(bf))
                parts.append((summed * (1.0 / total)).astype(bf))
            finish(w, g, parts)
            return carry

        lax.fori_loop(0, groups, group, 0)

    def sweep(guarded):
        def step(w, carry):
            page, begin = carry
            end = begin + windows_ref[page]
            passed = first + w >= end
            page = jnp.where(passed, page + 1, page)
            begin = jnp.where(passed, end, begin)
            filled = pack(w, page, begin)

            @pl.when(w >= 2)
            def _():
                copy_out(w - 2).wait()

            if guarded:
                safe(w, filled)
            else:
                chunks = lax.div(filled + STRIP - 1, STRIP)
                for c in range(extra_most // STRIP + 1):

                    @pl.when(chunks == c)
                    def _(c=c):
                        fast(w, c * STRIP)

            copy_out(w).start()
            return page, begin

        zero = jnp.int32(0)
        page, begin, _ = lax.fori_loop(0, pages, find, (zero, zero, zero))
        lax.fori_loop(0, win_count, step, (page, begin))
        copy_out(win_count - 2).wait()
        copy_out(win_count - 1).wait()

    proj_load = pltpu.make_async_copy(proj_hbm, proj_s, proj_sem.at[0])
    proj_load.start()
    msum_s[...] = jnp.zeros_like(msum_s)
    pk_s[...] = jnp.zeros_like(pk_s)
    pv_s[...] = jnp.zeros_like(pv_s)
    low_s[...] = jnp.ones_like(low_s)
    high_s[...] = jnp.ones_like(high_s)
    sweep(False)
    calm = (jnp.min(low_s[...]) >= SUM_LEAST) & (jnp.max(high_s[...]) <= SUM_MOST)

    @pl.when(jnp.logical_not(calm))
    def _():
        sweep(True)

    proj_load.wait()
    sums = msum_s[:, 0, :]
    high = sums.astype(bf)
    low = (sums - high.astype(jnp.float32)).astype(bf)
    both = nn_dot(jnp.concatenate([high, low], axis=0), proj_s[...])
    projected_ref[...] = both[:ROWS] + both[ROWS:]


def window_attention(tables, proj, page_windows, page_width, win_count):
    qt, k, v, ek, ev = tables
    groups = k.shape[1]
    width = groups * 128
    bf = jnp.bfloat16
    vmem = pl.BlockSpec(memory_space=pltpu.VMEM)
    smem = pl.BlockSpec(memory_space=pltpu.SMEM)
    hbm = pl.BlockSpec(memory_space=pltpu.HBM)
    room = KEYS - TOK + STRIP
    arrays = [pltpu.with_memory_space_constraint(a, pltpu.VMEM) for a in tables]
    return pl.pallas_call(
        functools.partial(attend_kernel, win_count, width, page_windows.shape[0]),
        out_shape=(
            jax.ShapeDtypeStruct((win_count * TOK, width), bf),
            pltpu.VMEM((ROWS, D), jnp.float32),
        ),
        in_specs=[smem, smem] + [vmem] * 5 + [hbm],
        out_specs=(hbm, vmem),
        scratch_shapes=[
            pltpu.VMEM((ROWS, 1, width), jnp.float32),
            pltpu.VMEM((width, D), bf),
            pltpu.SemaphoreType.DMA((1,)),
            pltpu.VMEM((groups, room, 128), bf),
            pltpu.VMEM((groups, room, 128), bf),
            pltpu.VMEM((16, room), bf),
            pltpu.VMEM((width // HDIM, KEYS, TOK), bf),
            pltpu.VMEM((2, TOK, width), bf),
            pltpu.VMEM((1, TOK), jnp.float32),
            pltpu.VMEM((1, TOK), jnp.float32),
            pltpu.SemaphoreType.DMA((2,)),
        ],
        compiler_params=pltpu.CompilerParams(vmem_limit_bytes=20 << 20),
    )(page_windows, page_width, *arrays, proj)


def page_kernel(
    count,
    heads,
    win_count,
    proj_ref,
    tsum_ref,
    gain_ref,
    windows_ref,
    docs_ref,
    w_hbm,
    out_hbm,
    out_ref,
    share_s,
    land_s,
    all_s,
    half_s,
    give_s,
    back_s,
    w_s,
    out_s,
    load_sem,
    head_send,
    head_recv,
    pack_send,
    pack_recv,
):
    me, head = lax.axis_index("pack"), lax.axis_index("head")
    pages, columns = out_ref.shape
    width = w_s.shape[2]
    bf = jnp.bfloat16
    mesh_id = pl.DeviceIdType.MESH

    loads = [
        pltpu.make_async_copy(w_hbm, w_s, load_sem.at[0]),
        pltpu.make_async_copy(out_hbm, out_s, load_sem.at[1]),
    ]
    for load in loads:
        load.start()

    def other_pack(k):
        return {"pack": lax.rem(me + k, count)}

    def other_head(k):
        return {"head": lax.rem(head + k, heads)}

    barrier = pltpu.get_barrier_semaphore()
    for k in range(1, heads):
        pl.semaphore_signal(barrier, inc=1, device_id=other_head(k), device_id_type=mesh_id)

    @pl.loop(1, count)
    def _(k):
        pl.semaphore_signal(barrier, inc=1, device_id=other_pack(k), device_id_type=mesh_id)

    def head_copy(phase, k, source, target):
        return pltpu.make_async_remote_copy(
            src_ref=source,
            dst_ref=target,
            send_sem=head_send.at[phase, k],
            recv_sem=head_recv.at[phase, k],
            device_id=other_head(k),
            device_id_type=mesh_id,
        )

    def features(k):
        start = lax.rem(head + k, heads) * columns
        return pl.ds(pl.multiple_of(start, 128), columns)

    rows = pl.ds(pl.multiple_of(me * ROWS, ROWS), ROWS)

    def pack_copy(k):
        return pltpu.make_async_remote_copy(
            src_ref=all_s.at[rows],
            dst_ref=all_s.at[rows],
            send_sem=pack_send.at[k],
            recv_sem=pack_recv.at[k],
            device_id=other_pack(k),
            device_id_type=mesh_id,
        )

    for k in range(1, heads):
        share_s[k] = proj_ref[:, features(k)].astype(bf)
    pl.semaphore_wait(barrier, count + heads - 2)
    first = [head_copy(0, k, share_s.at[k], land_s.at[k]) for k in range(1, heads)]
    for copy in first:
        copy.start()
    total = proj_ref[:, features(0)] + tsum_ref[:, features(0)]
    for k, copy in enumerate(first):
        copy.wait_recv()
        total = total + land_s[k + 1].astype(jnp.float32)
    real = lax.broadcasted_iota(jnp.int32, total.shape, 0) < win_count
    all_s[rows] = jnp.where(real, total, 0.0).astype(bf)

    @pl.loop(1, count)
    def _(k):
        pack_copy(k).start()

    def grid(shape, axis):
        return lax.broadcasted_iota(jnp.int32, shape, axis)

    square = (pages, pages)
    sizes = windows_ref[...].reshape(1, pages)
    upto = jnp.where(grid(square, 1) <= grid(square, 0), sizes, 0)
    ends = jnp.sum(upto, axis=1, keepdims=True)
    mine = jnp.sum(
        jnp.where(grid(square, 1) == grid(square, 0), sizes, 0), axis=1, keepdims=True
    )
    begins = ends - mine
    shape = (pages, count * ROWS)
    place = grid(shape, 1)
    inner = place & (ROWS - 1)
    window = (place // ROWS) * win_count + inner
    member = (window >= begins) & (window < ends) & (inner < win_count)
    member = jnp.where(member, 1.0, 0.0).astype(bf)
    scale = 1.0 / (mine.astype(jnp.float32) * TOK)
    docs = docs_ref.shape[0]
    lengths = docs_ref[...].reshape(1, docs)
    small = (docs, docs)
    column = jnp.sum(
        jnp.where(grid(small, 1) <= grid(small, 0), lengths, 0), axis=1, keepdims=True
    )
    across = jnp.sum(jnp.where(grid(small, 1) == grid(small, 0), column, 0), axis=0, keepdims=True)
    doc_row = jnp.sum(
        jnp.where(grid((docs, pages), 1) >= column, 1, 0), axis=0, keepdims=True
    )
    doc_col = jnp.sum(
        jnp.where(grid((pages, docs), 0) >= across, 1, 0), axis=1, keepdims=True
    )
    same = doc_row == doc_col

    @pl.loop(1, count)
    def _(k):
        pack_copy(k).wait_recv()

    pooled = jnp.dot(member, all_s[...], preferred_element_type=jnp.float32) * scale
    half_s[head] = pooled.astype(bf)
    second = [head_copy(1, k, half_s.at[head], half_s.at[head]) for k in range(1, heads)]
    for copy in second:
        copy.start()
    for copy in second:
        copy.wait_recv()
    parts = [jnp.where(head == k, pooled, half_s[k].astype(jnp.float32)) for k in range(heads)]
    normed = normalize(jnp.concatenate(parts, axis=1), gain_ref[...])
    for load in loads:
        load.wait()
    query, keys, values = (nn_dot(normed, w_s[i]).astype(bf) for i in range(3))
    owner = grid((pages, width), 1) // HDIM
    local = width // HDIM
    wide = jnp.concatenate(
        [jnp.where(owner == h, query.astype(jnp.float32), 0.0).astype(bf) for h in range(local)],
        axis=0,
    )
    scores = lax.dot_general(
        wide, keys, (((1,), (1,)), ((), ())), preferred_element_type=jnp.float32
    ) / math.sqrt(HDIM)
    scores = scores.reshape(local, pages, pages)
    scores = jnp.where(same[None], scores, -1e30)
    weights = jnp.exp(scores - jnp.max(scores, axis=-1, keepdims=True))
    probs = (weights / jnp.sum(weights, axis=-1, keepdims=True)).astype(bf)
    mixed = nn_dot(probs.reshape(local * pages, pages), values).reshape(local, pages, width)
    context = jnp.zeros((pages, width), jnp.float32)
    for h in range(local):
        context = jnp.where(owner == h, mixed[h], context)
    branch = nn_dot(context.astype(bf), out_s[...])
    give_s[0] = branch
    for k in range(1, heads):
        back_s[k] = give_s[0, :, features(k)].astype(bf)
    third = [head_copy(2, k, back_s.at[k], back_s.at[heads + k]) for k in range(1, heads)]
    for copy in third:
        copy.start()
    result = pooled + give_s[0, :, features(0)]
    for k, copy in enumerate(third):
        copy.wait_recv()
        result = result + back_s[heads + k + 1].astype(jnp.float32)
    out_ref[...] = result
    for copy in first + second + third:
        copy.wait_send()

    @pl.loop(1, count)
    def _(k):
        pack_copy(k).wait_send()


def page_layer(projected, token_sums, gain, weight, proj, page_windows, doc_pages, win_count):
    heads = lax.axis_size("head")
    count = lax.axis_size("pack")
    pages = page_windows.shape[0]
    width = weight.shape[2]
    columns = D // heads
    bf = jnp.bfloat16
    vmem = pl.BlockSpec(memory_space=pltpu.VMEM)
    hbm = pl.BlockSpec(memory_space=pltpu.HBM)
    return pl.pallas_call(
        functools.partial(page_kernel, count, heads, win_count),
        out_shape=jax.ShapeDtypeStruct((pages, columns), jnp.float32),
        in_specs=[vmem] * 5 + [hbm] * 2,
        out_specs=vmem,
        scratch_shapes=[
            pltpu.VMEM((heads, ROWS, columns), bf),
            pltpu.VMEM((heads, ROWS, columns), bf),
            pltpu.VMEM((count * ROWS, columns), bf),
            pltpu.VMEM((heads, pages, columns), bf),
            pltpu.VMEM((1, pages, D), jnp.float32),
            pltpu.VMEM((2 * heads, pages, columns), bf),
            pltpu.VMEM((3, D, width), bf),
            pltpu.VMEM((width, D), bf),
            pltpu.SemaphoreType.DMA((2,)),
            pltpu.SemaphoreType.DMA((3, heads)),
            pltpu.SemaphoreType.DMA((3, heads)),
            pltpu.SemaphoreType.DMA((count,)),
            pltpu.SemaphoreType.DMA((count,)),
        ],
        compiler_params=pltpu.CompilerParams(
            collective_id=2, has_side_effects=True, vmem_limit_bytes=24 << 20
        ),
    )(
        projected,
        token_sums,
        gain.reshape(1, D),
        page_windows,
        doc_pages,
        weight.transpose(1, 0, 2),
        proj,
    )


def shards(
    tokens,
    ln_gain,
    attn_weight,
    attn_proj,
    page_gain,
    page_weight,
    page_proj,
    page_windows,
    page_width,
    doc_pages,
):
    win_count = tokens.shape[0] // TOK
    *tables, token_sums = window_qkv(tokens, ln_gain, attn_weight)
    mixed, projected = window_attention(tables, attn_proj, page_windows, page_width, win_count)
    page_out = page_layer(
        projected,
        token_sums,
        page_gain,
        page_weight,
        page_proj,
        page_windows,
        doc_pages,
        win_count,
    )
    return (mixed, page_out)


def solution(mesh):
    placed = (
        P(("rep", "pack"), None),
        P(),
        P(None, None, "head"),
        P("head", None),
        P(),
        P(None, None, "head"),
        P("head", None),
        P("rep"),
        P("rep"),
        P("rep"),
    )
    return jax.shard_map(
        shards,
        mesh=mesh,
        in_specs=placed,
        out_specs=(P(("rep", "pack"), "head"), P("rep", "head")),
        check_vma=False,
    )
```

```python
import functools
import math

import jax
import jax.numpy as jnp
import numpy as np
from jax import lax
from jax.experimental import pallas as pl
from jax.experimental.pallas import tpu as pltpu
from jax.sharding import PartitionSpec as P

D = 1024
HDIM = 32
WIN = 16
HALO = 4
HALO_WIN = 4
TOK = WIN * WIN
STRIP = WIN * HALO
CORNER = HALO * HALO
SIDE_KEYS = 4 * STRIP + 4 * CORNER
KEYS = TOK + SIDE_KEYS
SUM_LEAST = 2.0**-60
SUM_MOST = 2.0**60
ROWS = 16
EPS = 1e-05
LOG2E = 1.4426950408889634
OFFSETS = ((-1, 0), (1, 0), (0, -1), (0, 1), (-1, -1), (-1, 1), (1, -1), (1, 1))


CHUNK = 32


def edge_columns(values):
    tall = values.reshape(WIN // 2, 2 * WIN, values.shape[1])
    upper = lax.broadcasted_iota(jnp.int32, (WIN // 2, 8, values.shape[1]), 1) < HALO

    def turned(lo):
        return pltpu.roll(tall[:, lo : lo + 8], HALO, 1)

    left = jnp.where(upper, tall[:, :8], turned(WIN))
    right = jnp.where(upper, turned(8), tall[:, WIN + 8 :])
    return [side.reshape(STRIP, values.shape[1]).astype(jnp.bfloat16) for side in (left, right)]


def nn_dot(a, b):
    return jnp.dot(a, b, preferred_element_type=jnp.float32)


def normalize(values, gain):
    center = values - jnp.mean(values, axis=-1, keepdims=True)
    spread = jnp.mean(center * center, axis=-1, keepdims=True)
    return (center * lax.rsqrt(spread + EPS) * gain).astype(jnp.bfloat16)


def qkv_kernel(
    count,
    win_count,
    width,
    tok_hbm,
    gain_hbm,
    w_hbm,
    qt_ref,
    k_ref,
    v_ref,
    ek_ref,
    ev_ref,
    tsum_ref,
    gain_s,
    tok_s,
    side_s,
    edge_s,
    w_s,
    even_s,
    odd_s,
    own_sem,
    w_sem,
    send_sem,
    recv_sem,
):
    me = lax.axis_index("pack")
    after = {"pack": lax.rem(me + 1, count)}
    before = {"pack": lax.rem(me + count - 1, count)}
    groups = width // 128
    bf = jnp.bfloat16

    def own(w):
        return pltpu.make_async_copy(
            tok_hbm.at[pl.ds(w * TOK, TOK)], tok_s.at[w], own_sem.at[w]
        )

    weight = pltpu.make_async_copy(w_hbm, w_s, w_sem.at[0])
    gain = pltpu.make_async_copy(gain_hbm, gain_s, w_sem.at[1])
    own(0).start()
    own(win_count - 1).start()
    gain.start()
    weight.start()
    for w in range(1, win_count - 1):
        own(w).start()

    pieces = []
    for i in range(HALO_WIN):
        place = pl.ds(i * STRIP, STRIP)
        high = (win_count - HALO_WIN + i + 1) * TOK - STRIP
        pieces.append((after, tok_hbm.at[pl.ds(high, STRIP)], tok_s.at[win_count, place]))
        pieces.append((before, tok_hbm.at[pl.ds(i * TOK, STRIP)], tok_s.at[win_count + 1, place]))
    pieces.append((after, edge_s.at[0], side_s.at[pl.ds(STRIP, STRIP)]))
    pieces.append((before, edge_s.at[1], side_s.at[pl.ds(0, STRIP)]))
    copies = [
        pltpu.make_async_remote_copy(
            src_ref=source,
            dst_ref=target,
            send_sem=send_sem.at[i],
            recv_sem=recv_sem.at[i],
            device_id=where,
            device_id_type=pl.DeviceIdType.MESH,
        )
        for i, (where, source, target) in enumerate(pieces)
    ]
    forward, backward = me < count - 1, me > 0
    barrier = pltpu.get_barrier_semaphore()
    for there, where in ((forward, after), (backward, before)):

        @pl.when(there)
        def _(where=where):
            pl.semaphore_signal(
                barrier, inc=1, device_id=where, device_id_type=pl.DeviceIdType.MESH
            )

    @pl.when(jnp.logical_not(backward))
    def _():
        tok_s[win_count] = jnp.zeros((TOK, D), bf)
        side_s[STRIP:] = jnp.zeros((STRIP, D), bf)

    @pl.when(jnp.logical_not(forward))
    def _():
        tok_s[win_count + 1] = jnp.zeros((TOK, D), bf)
        side_s[:STRIP] = jnp.zeros((STRIP, D), bf)

    def lane_mean(values):
        folded = values[:, :128]
        for lo in range(128, D, 128):
            folded = folded + values[:, lo : lo + 128]
        return jnp.sum(folded, axis=1, keepdims=True) * (1.0 / D)

    def norm_part(rows, out_s, lo):
        values = rows[lo : lo + CHUNK].astype(jnp.float32)
        center = values - lane_mean(values)
        spread = lane_mean(center * center)
        scaled = center * lax.rsqrt(spread + EPS) * gain_s[...]
        out_s[lo : lo + CHUNK] = scaled.astype(bf)
        folded = values[:8]
        for at in range(8, CHUNK, 8):
            folded = folded + values[at : at + 8]
        return folded

    def norm(rows, out_s):
        total = norm_part(rows, out_s, 0)
        for lo in range(CHUNK, rows.shape[0], CHUNK):
            total = total + norm_part(rows, out_s, lo)
        return jnp.sum(total, axis=0, keepdims=True)

    def keys_values(values, block):
        for part, out_ref, edge_ref in ((1, k_ref, ek_ref), (2, v_ref, ev_ref)):
            made = nn_dot(values, w_s[part])
            if block is None:
                sides, at = [made[:STRIP].astype(bf), made[STRIP:].astype(bf)], win_count + 2
            else:
                sides, at = edge_columns(made), block
            made = made.astype(bf)
            for g in range(groups):
                lanes = slice(g * 128, (g + 1) * 128)
                if block is not None:
                    out_ref[block, g] = made[:, lanes]
                edge_ref[at, g, :STRIP] = sides[0][:, lanes]
                edge_ref[at, g, STRIP:] = sides[1][:, lanes]

    def queries(values, block):
        q = nn_dot(values, w_s[0]).astype(bf)
        for g in range(groups):
            qt_ref[block, g] = q[:, g * 128 : (g + 1) * 128].T

    def project(block, in_s):
        values = in_s[...]
        queries(values, block)
        keys_values(values, block)

    def send(first, last):
        for i in range(first, last):
            pl.when((forward, backward)[i % 2])(copies[i].start)

    def receive(which):
        for i in which:
            pl.when((backward, forward)[i % 2])(copies[i].wait_recv)

    pl.semaphore_wait(barrier, jnp.where(forward, 1, 0) + jnp.where(backward, 1, 0))
    sides = 2 * HALO_WIN
    send(0, sides)
    own(win_count - 1).wait()
    edge_s[0] = edge_columns(tok_s[win_count - 1].astype(jnp.float32))[1]
    own(0).wait()
    edge_s[1] = edge_columns(tok_s[0].astype(jnp.float32))[0]
    send(sides, sides + 2)
    gain.wait()
    tsum_ref[pl.ds(0, 1)] = norm(tok_s.at[0], even_s)
    weight.wait()

    def arrive(block):
        @pl.when(block < win_count - 1)
        def _():
            own(jnp.minimum(block, win_count - 2)).wait()

    def both(block, in_s, out_s):
        project(block, in_s)
        tsum_ref[pl.ds(block + 1, 1)] = norm(tok_s.at[block + 1], out_s)

    def pair(i, carry):
        arrive(2 * i + 1)
        both(2 * i, even_s, odd_s)
        arrive(2 * i + 2)
        both(2 * i + 1, odd_s, even_s)
        return carry

    lax.fori_loop(0, win_count // 2 - 1, pair, 0)
    both(win_count - 2, even_s, odd_s)
    project(win_count - 1, odd_s)
    receive(range(0, sides, 2))
    norm(tok_s.at[win_count], even_s)
    receive(range(1, sides, 2))
    keys_values(even_s[...], win_count)
    norm(tok_s.at[win_count + 1], odd_s)
    receive(range(sides, sides + 2))
    keys_values(odd_s[...], win_count + 1)
    norm(side_s, even_s)
    keys_values(even_s[: 2 * STRIP], None)
    for i, copy in enumerate(copies):
        pl.when((forward, backward)[i % 2])(copy.wait_send)


def window_qkv(tokens, gain, weight):
    win_count = tokens.shape[0] // TOK
    width = weight.shape[2]
    groups = width // 128
    bf = jnp.bfloat16
    vmem = pl.BlockSpec(memory_space=pltpu.VMEM)
    hbm = pl.BlockSpec(memory_space=pltpu.HBM)
    edges = (win_count + 3, groups, 2 * STRIP, 128)
    return pl.pallas_call(
        functools.partial(qkv_kernel, lax.axis_size("pack"), win_count, width),
        out_shape=(
            pltpu.VMEM((win_count, groups, 128, TOK), bf),
            pltpu.VMEM((win_count + 2, groups, TOK, 128), bf),
            pltpu.VMEM((win_count + 2, groups, TOK, 128), bf),
            pltpu.VMEM(edges, bf),
            pltpu.VMEM(edges, bf),
            pltpu.VMEM((ROWS, D), jnp.float32),
        ),
        in_specs=[hbm, hbm, hbm],
        out_specs=(vmem,) * 6,
        scratch_shapes=[
            pltpu.VMEM((1, D), jnp.float32),
            pltpu.VMEM((win_count + 2, TOK, D), bf),
            pltpu.VMEM((2 * STRIP, D), bf),
            pltpu.VMEM((2, STRIP, D), bf),
            pltpu.VMEM((3, D, width), bf),
            pltpu.VMEM((TOK, D), bf),
            pltpu.VMEM((TOK, D), bf),
            pltpu.SemaphoreType.DMA((win_count,)),
            pltpu.SemaphoreType.DMA((2,)),
            pltpu.SemaphoreType.DMA((2 * HALO_WIN + 2,)),
            pltpu.SemaphoreType.DMA((2 * HALO_WIN + 2,)),
        ],
        compiler_params=pltpu.CompilerParams(
            collective_id=1, has_side_effects=True, vmem_limit_bytes=24 << 20
        ),
    )(
        pltpu.with_memory_space_constraint(tokens, pltpu.HBM),
        pltpu.with_memory_space_constraint(gain.reshape(1, D), pltpu.HBM),
        pltpu.with_memory_space_constraint(weight.transpose(1, 0, 2), pltpu.HBM),
    )


def attend_kernel(
    win_count,
    width,
    pages,
    windows_ref,
    across_ref,
    qt_ref,
    k_ref,
    v_ref,
    ek_ref,
    ev_ref,
    proj_hbm,
    mixed_hbm,
    projected_ref,
    msum_s,
    proj_s,
    proj_sem,
    pk_s,
    pv_s,
    mask_s,
    prob_s,
    out_s,
    low_s,
    high_s,
    out_sem,
):
    first = lax.axis_index("pack") * win_count
    groups = width // 128
    per = 128 // HDIM
    extra_most = KEYS - TOK
    factor = LOG2E / math.sqrt(HDIM)
    bf = jnp.bfloat16

    def copy_out(w):
        slot = lax.rem(w, 2)
        return pltpu.make_async_copy(
            out_s.at[slot], mixed_hbm.at[pl.ds(w * TOK, TOK)], out_sem.at[slot]
        )

    def find(p, carry):
        page, begin, run = carry
        run = run + windows_ref[p]
        passed = run <= first
        return jnp.where(passed, p + 1, page), jnp.where(passed, run, begin), run

    def pack(w, page, begin):
        across = across_ref[page]
        total = windows_ref[page]
        inside = first + w - begin
        row = lax.div(inside, across)
        col = inside - row * across
        filled = jnp.int32(0)
        for a, b in OFFSETS:
            place = inside + a * across + b
            valid = (col + b >= 0) & (col + b < across) & (row + a >= 0) & (place < total)
            near = w + a * across + b
            size = CORNER if a and b else STRIP
            early, late = near < 0, near >= win_count
            if a < 0:
                block = jnp.where(early, win_count, near)
                index = jnp.where(early, near + HALO_WIN, HALO_WIN - 1)
            elif a > 0:
                block = jnp.where(late, win_count + 1, near)
                index = jnp.where(late, near - win_count, 0)
            else:
                block = jnp.where(early | late, win_count + 2, near)
                index = 0
            start = index * size + (STRIP if b < 0 else 0)
            keys, values = (ek_ref, ev_ref) if b else (k_ref, v_ref)

            @pl.when(valid)
            def _(block=block, start=start, size=size, keys=keys, values=values, filled=filled):
                source = pl.ds(pl.multiple_of(start, 16), size)
                target = pl.ds(pl.multiple_of(filled, 16), size)
                pk_s[:, target, :] = keys[block, :, source, :]
                pv_s[:, target, :] = values[block, :, source, :]

            filled = filled + jnp.where(valid, size, 0)
        blank = jnp.zeros((groups, 3 * CORNER, 128), bf)
        target = pl.ds(pl.multiple_of(filled, 16), 3 * CORNER)
        pk_s[:, target, :] = blank
        pv_s[:, target, :] = blank
        lane = lax.broadcasted_iota(jnp.int32, mask_s.shape, 1)
        mask_s[...] = jnp.where(lane < filled, 1.0, 0.0).astype(bf)
        return filled

    def finish(w, g, parts):
        piece = jnp.concatenate(parts, axis=0).T
        lanes = pl.ds(pl.multiple_of(g * 128, 128), 128)
        out_s[lax.rem(w, 2), :, lanes] = piece
        msum_s[w, :, lanes] = jnp.sum(piece.astype(jnp.float32), axis=0, keepdims=True)

    def spread(queries, j):
        above = [jnp.zeros((j * HDIM, TOK), bf)] if j else []
        below = [jnp.zeros((128 - (j + 1) * HDIM, TOK), bf)] if j + 1 < per else []
        return jnp.concatenate(above + [queries[j * HDIM : (j + 1) * HDIM]] + below, axis=0)

    def fast(w, extra):
        keys = TOK + extra
        for g in range(groups):
            queries = qt_ref[w, g]
            rows = jnp.concatenate([k_ref[w, g], pk_s[g, :extra]], axis=0) if extra else k_ref[w, g]
            for j in range(per):
                scores = nn_dot(rows, spread(queries, j))
                prob_s[g * per + j, :keys] = jnp.exp2(scores * factor).astype(bf)
        low, high = low_s[...], high_s[...]
        for g in range(groups):
            values = v_ref[w, g].T
            marks = jnp.ones((16, TOK), bf)
            if extra:
                values = jnp.concatenate([values, pv_s[g, :extra].T], axis=1)
                marks = jnp.concatenate([marks, mask_s[:, :extra]], axis=1)
            parts = []
            for j in range(per):
                lhs = jnp.concatenate([values[j * HDIM : (j + 1) * HDIM], marks], axis=0)
                summed = nn_dot(lhs, prob_s[g * per + j, :keys])
                total = summed[HDIM : HDIM + 1]
                low = jnp.minimum(low, total)
                high = jnp.maximum(high, total)
                parts.append((summed[:HDIM] * (1.0 / total)).astype(bf))
            finish(w, g, parts)
        low_s[...] = low
        high_s[...] = high

    def safe(w, filled):
        row = lax.broadcasted_iota(jnp.int32, (extra_most, TOK), 0)

        def group(g, carry):
            queries = qt_ref[w, g]
            values = jnp.concatenate([v_ref[w, g].T, pv_s[g, :extra_most].T], axis=1)
            parts = []
            for j in range(per):
                qz = spread(queries, j)
                near = nn_dot(pk_s[g, :extra_most], qz) * factor
                near = jnp.where(row < filled, near, -1e30)
                scores = jnp.concatenate([nn_dot(k_ref[w, g], qz) * factor, near], axis=0)
                weights = jnp.exp2(scores - jnp.max(scores, axis=0, keepdims=True))
                total = jnp.sum(weights, axis=0, keepdims=True)
                summed = nn_dot(values[j * HDIM : (j + 1) * HDIM], weights.astype(bf))
                parts.append((summed * (1.0 / total)).astype(bf))
            finish(w, g, parts)
            return carry

        lax.fori_loop(0, groups, group, 0)

    def sweep(guarded):
        def step(w, carry):
            page, begin = carry
            end = begin + windows_ref[page]
            passed = first + w >= end
            page = jnp.where(passed, page + 1, page)
            begin = jnp.where(passed, end, begin)
            filled = pack(w, page, begin)

            @pl.when(w >= 2)
            def _():
                copy_out(w - 2).wait()

            if guarded:
                safe(w, filled)
            else:
                chunks = lax.div(filled + STRIP - 1, STRIP)
                for c in range(extra_most // STRIP + 1):

                    @pl.when(chunks == c)
                    def _(c=c):
                        fast(w, c * STRIP)

            copy_out(w).start()
            return page, begin

        zero = jnp.int32(0)
        page, begin, _ = lax.fori_loop(0, pages, find, (zero, zero, zero))
        lax.fori_loop(0, win_count, step, (page, begin))
        copy_out(win_count - 2).wait()
        copy_out(win_count - 1).wait()

    proj_load = pltpu.make_async_copy(proj_hbm, proj_s, proj_sem.at[0])
    proj_load.start()
    msum_s[...] = jnp.zeros_like(msum_s)
    pk_s[...] = jnp.zeros_like(pk_s)
    pv_s[...] = jnp.zeros_like(pv_s)
    low_s[...] = jnp.ones_like(low_s)
    high_s[...] = jnp.ones_like(high_s)
    sweep(False)
    calm = (jnp.min(low_s[...]) >= SUM_LEAST) & (jnp.max(high_s[...]) <= SUM_MOST)

    @pl.when(jnp.logical_not(calm))
    def _():
        sweep(True)

    proj_load.wait()
    sums = msum_s[:, 0, :]
    high = sums.astype(bf)
    low = (sums - high.astype(jnp.float32)).astype(bf)
    both = nn_dot(jnp.concatenate([high, low], axis=0), proj_s[...])
    projected_ref[...] = both[:ROWS] + both[ROWS:]


def window_attention(tables, proj, page_windows, page_width, win_count):
    qt, k, v, ek, ev = tables
    groups = k.shape[1]
    width = groups * 128
    bf = jnp.bfloat16
    vmem = pl.BlockSpec(memory_space=pltpu.VMEM)
    smem = pl.BlockSpec(memory_space=pltpu.SMEM)
    hbm = pl.BlockSpec(memory_space=pltpu.HBM)
    room = KEYS - TOK + STRIP
    arrays = [pltpu.with_memory_space_constraint(a, pltpu.VMEM) for a in tables]
    return pl.pallas_call(
        functools.partial(attend_kernel, win_count, width, page_windows.shape[0]),
        out_shape=(
            jax.ShapeDtypeStruct((win_count * TOK, width), bf),
            pltpu.VMEM((ROWS, D), jnp.float32),
        ),
        in_specs=[smem, smem] + [vmem] * 5 + [hbm],
        out_specs=(hbm, vmem),
        scratch_shapes=[
            pltpu.VMEM((ROWS, 1, width), jnp.float32),
            pltpu.VMEM((width, D), bf),
            pltpu.SemaphoreType.DMA((1,)),
            pltpu.VMEM((groups, room, 128), bf),
            pltpu.VMEM((groups, room, 128), bf),
            pltpu.VMEM((16, room), bf),
            pltpu.VMEM((width // HDIM, KEYS, TOK), bf),
            pltpu.VMEM((2, TOK, width), bf),
            pltpu.VMEM((1, TOK), jnp.float32),
            pltpu.VMEM((1, TOK), jnp.float32),
            pltpu.SemaphoreType.DMA((2,)),
        ],
        compiler_params=pltpu.CompilerParams(vmem_limit_bytes=20 << 20),
    )(page_windows, page_width, *arrays, proj)


def page_kernel(
    count,
    heads,
    win_count,
    proj_ref,
    tsum_ref,
    gain_ref,
    windows_ref,
    docs_ref,
    w_hbm,
    out_hbm,
    out_ref,
    share_s,
    land_s,
    all_s,
    half_s,
    give_s,
    back_s,
    w_s,
    out_s,
    load_sem,
    head_send,
    head_recv,
    pack_send,
    pack_recv,
):
    me, head = lax.axis_index("pack"), lax.axis_index("head")
    pages, columns = out_ref.shape
    width = w_s.shape[2]
    bf = jnp.bfloat16
    mesh_id = pl.DeviceIdType.MESH

    loads = [
        pltpu.make_async_copy(w_hbm, w_s, load_sem.at[0]),
        pltpu.make_async_copy(out_hbm, out_s, load_sem.at[1]),
    ]
    for load in loads:
        load.start()

    def other_pack(k):
        return {"pack": lax.rem(me + k, count)}

    def other_head(k):
        return {"head": lax.rem(head + k, heads)}

    barrier = pltpu.get_barrier_semaphore()
    for k in range(1, heads):
        pl.semaphore_signal(barrier, inc=1, device_id=other_head(k), device_id_type=mesh_id)

    @pl.loop(1, count)
    def _(k):
        pl.semaphore_signal(barrier, inc=1, device_id=other_pack(k), device_id_type=mesh_id)

    def head_copy(phase, k, source, target):
        return pltpu.make_async_remote_copy(
            src_ref=source,
            dst_ref=target,
            send_sem=head_send.at[phase, k],
            recv_sem=head_recv.at[phase, k],
            device_id=other_head(k),
            device_id_type=mesh_id,
        )

    def features(k):
        start = lax.rem(head + k, heads) * columns
        return pl.ds(pl.multiple_of(start, 128), columns)

    rows = pl.ds(pl.multiple_of(me * ROWS, ROWS), ROWS)

    def pack_copy(k):
        return pltpu.make_async_remote_copy(
            src_ref=all_s.at[rows],
            dst_ref=all_s.at[rows],
            send_sem=pack_send.at[k],
            recv_sem=pack_recv.at[k],
            device_id=other_pack(k),
            device_id_type=mesh_id,
        )

    for k in range(1, heads):
        share_s[k] = proj_ref[:, features(k)].astype(share_s.dtype)
    pl.semaphore_wait(barrier, count + heads - 2)
    first = [head_copy(0, k, share_s.at[k], land_s.at[k]) for k in range(1, heads)]
    for copy in first:
        copy.start()
    total = proj_ref[:, features(0)] + tsum_ref[:, features(0)]
    for k, copy in enumerate(first):
        copy.wait_recv()
        total = total + land_s[k + 1].astype(jnp.float32)
    real = lax.broadcasted_iota(jnp.int32, total.shape, 0) < win_count
    all_s[rows] = jnp.where(real, total, 0.0).astype(all_s.dtype)

    @pl.loop(1, count)
    def _(k):
        pack_copy(k).start()

    def grid(shape, axis):
        return lax.broadcasted_iota(jnp.int32, shape, axis)

    square = (pages, pages)
    sizes = windows_ref[...].reshape(1, pages)
    upto = jnp.where(grid(square, 1) <= grid(square, 0), sizes, 0)
    ends = jnp.sum(upto, axis=1, keepdims=True)
    mine = jnp.sum(
        jnp.where(grid(square, 1) == grid(square, 0), sizes, 0), axis=1, keepdims=True
    )
    begins = ends - mine
    shape = (pages, count * ROWS)
    place = grid(shape, 1)
    inner = place & (ROWS - 1)
    window = (place // ROWS) * win_count + inner
    member = (window >= begins) & (window < ends) & (inner < win_count)
    member = jnp.where(member, 1.0, 0.0).astype(bf)
    scale = 1.0 / (mine.astype(jnp.float32) * TOK)
    docs = docs_ref.shape[0]
    lengths = docs_ref[...].reshape(1, docs)
    small = (docs, docs)
    column = jnp.sum(
        jnp.where(grid(small, 1) <= grid(small, 0), lengths, 0), axis=1, keepdims=True
    )
    across = jnp.sum(jnp.where(grid(small, 1) == grid(small, 0), column, 0), axis=0, keepdims=True)
    doc_row = jnp.sum(
        jnp.where(grid((docs, pages), 1) >= column, 1, 0), axis=0, keepdims=True
    )
    doc_col = jnp.sum(
        jnp.where(grid((pages, docs), 0) >= across, 1, 0), axis=1, keepdims=True
    )
    same = doc_row == doc_col

    @pl.loop(1, count)
    def _(k):
        pack_copy(k).wait_recv()

    gathered = all_s[...]
    high = gathered.astype(bf)
    pooled = nn_dot(member, high)
    if gathered.dtype != bf:
        pooled = pooled + nn_dot(member, (gathered - high.astype(jnp.float32)).astype(bf))
    pooled = pooled * scale
    half_s[head] = pooled.astype(half_s.dtype)
    second = [head_copy(1, k, half_s.at[head], half_s.at[head]) for k in range(1, heads)]
    for copy in second:
        copy.start()
    for copy in second:
        copy.wait_recv()
    parts = [jnp.where(head == k, pooled, half_s[k].astype(jnp.float32)) for k in range(heads)]
    normed = normalize(jnp.concatenate(parts, axis=1), gain_ref[...])
    for load in loads:
        load.wait()
    query, keys, values = (nn_dot(normed, w_s[i]).astype(bf) for i in range(3))
    owner = grid((pages, width), 1) // HDIM
    local = width // HDIM
    wide = jnp.concatenate(
        [jnp.where(owner == h, query.astype(jnp.float32), 0.0).astype(bf) for h in range(local)],
        axis=0,
    )
    scores = lax.dot_general(
        wide, keys, (((1,), (1,)), ((), ())), preferred_element_type=jnp.float32
    ) / math.sqrt(HDIM)
    scores = scores.reshape(local, pages, pages)
    scores = jnp.where(same[None], scores, -1e30)
    weights = jnp.exp(scores - jnp.max(scores, axis=-1, keepdims=True))
    probs = (weights / jnp.sum(weights, axis=-1, keepdims=True)).astype(bf)
    mixed = nn_dot(probs.reshape(local * pages, pages), values).reshape(local, pages, width)
    context = jnp.zeros((pages, width), jnp.float32)
    for h in range(local):
        context = jnp.where(owner == h, mixed[h], context)
    branch = nn_dot(context.astype(bf), out_s[...])
    give_s[0] = branch
    for k in range(1, heads):
        back_s[k] = give_s[0, :, features(k)].astype(back_s.dtype)
    third = [head_copy(2, k, back_s.at[k], back_s.at[heads + k]) for k in range(1, heads)]
    for copy in third:
        copy.start()
    result = pooled + give_s[0, :, features(0)]
    for k, copy in enumerate(third):
        copy.wait_recv()
        result = result + back_s[heads + k + 1].astype(jnp.float32)
    out_ref[...] = result
    for copy in first + second + third:
        copy.wait_send()

    @pl.loop(1, count)
    def _(k):
        pack_copy(k).wait_send()


def page_layer(projected, token_sums, gain, weight, proj, page_windows, doc_pages, win_count):
    heads = lax.axis_size("head")
    count = lax.axis_size("pack")
    pages = page_windows.shape[0]
    width = weight.shape[2]
    columns = D // heads
    bf = jnp.bfloat16
    vmem = pl.BlockSpec(memory_space=pltpu.VMEM)
    hbm = pl.BlockSpec(memory_space=pltpu.HBM)
    return pl.pallas_call(
        functools.partial(page_kernel, count, heads, win_count),
        out_shape=jax.ShapeDtypeStruct((pages, columns), jnp.float32),
        in_specs=[vmem] * 5 + [hbm] * 2,
        out_specs=vmem,
        scratch_shapes=[
            pltpu.VMEM((heads, ROWS, columns), jnp.float32),
            pltpu.VMEM((heads, ROWS, columns), jnp.float32),
            pltpu.VMEM((count * ROWS, columns), bf),
            pltpu.VMEM((heads, pages, columns), bf),
            pltpu.VMEM((1, pages, D), jnp.float32),
            pltpu.VMEM((2 * heads, pages, columns), bf),
            pltpu.VMEM((3, D, width), bf),
            pltpu.VMEM((width, D), bf),
            pltpu.SemaphoreType.DMA((2,)),
            pltpu.SemaphoreType.DMA((3, heads)),
            pltpu.SemaphoreType.DMA((3, heads)),
            pltpu.SemaphoreType.DMA((count,)),
            pltpu.SemaphoreType.DMA((count,)),
        ],
        compiler_params=pltpu.CompilerParams(
            collective_id=2, has_side_effects=True, vmem_limit_bytes=24 << 20
        ),
    )(
        projected,
        token_sums,
        gain.reshape(1, D),
        page_windows,
        doc_pages,
        weight.transpose(1, 0, 2),
        proj,
    )


def shards(
    tokens,
    ln_gain,
    attn_weight,
    attn_proj,
    page_gain,
    page_weight,
    page_proj,
    page_windows,
    page_width,
    doc_pages,
):
    win_count = tokens.shape[0] // TOK
    *tables, token_sums = window_qkv(tokens, ln_gain, attn_weight)
    mixed, projected = window_attention(tables, attn_proj, page_windows, page_width, win_count)
    page_out = page_layer(
        projected,
        token_sums,
        page_gain,
        page_weight,
        page_proj,
        page_windows,
        doc_pages,
        win_count,
    )
    return (mixed, page_out)


def solution(mesh):
    placed = (
        P(("rep", "pack"), None),
        P(),
        P(None, None, "head"),
        P("head", None),
        P(),
        P(None, None, "head"),
        P("head", None),
        P("rep"),
        P("rep"),
        P("rep"),
    )
    return jax.shard_map(
        shards,
        mesh=mesh,
        in_specs=placed,
        out_specs=(P(("rep", "pack"), "head"), P("rep", "head")),
        check_vma=False,
    )
```

```python
import functools
import math

import jax
import jax.numpy as jnp
import numpy as np
from jax import lax
from jax.experimental import pallas as pl
from jax.experimental.pallas import tpu as pltpu
from jax.sharding import PartitionSpec as P

D = 1024
HDIM = 32
WIN = 16
HALO = 4
HALO_WIN = 4
TOK = WIN * WIN
STRIP = WIN * HALO
CORNER = HALO * HALO
SIDE_KEYS = 4 * STRIP + 4 * CORNER
KEYS = TOK + SIDE_KEYS
SUM_LEAST = 2.0**-60
SUM_MOST = 2.0**60
ROWS = 16
EPS = 1e-05
LOG2E = 1.4426950408889634
OFFSETS = ((-1, 0), (1, 0), (0, -1), (0, 1), (-1, -1), (-1, 1), (1, -1), (1, 1))


CHUNK = 32


def edge_columns(values):
    tall = values.reshape(WIN // 2, 2 * WIN, values.shape[1])
    upper = lax.broadcasted_iota(jnp.int32, (WIN // 2, 8, values.shape[1]), 1) < HALO

    def turned(lo):
        return pltpu.roll(tall[:, lo : lo + 8], HALO, 1)

    left = jnp.where(upper, tall[:, :8], turned(WIN))
    right = jnp.where(upper, turned(8), tall[:, WIN + 8 :])
    return [side.reshape(STRIP, values.shape[1]).astype(jnp.bfloat16) for side in (left, right)]


def nn_dot(a, b):
    return jnp.dot(a, b, preferred_element_type=jnp.float32)


def normalize(values, gain):
    center = values - jnp.mean(values, axis=-1, keepdims=True)
    spread = jnp.mean(center * center, axis=-1, keepdims=True)
    return (center * lax.rsqrt(spread + EPS) * gain).astype(jnp.bfloat16)


def qkv_kernel(
    count,
    win_count,
    width,
    tok_hbm,
    gain_hbm,
    w_hbm,
    qt_ref,
    k_ref,
    v_ref,
    ek_ref,
    ev_ref,
    tsum_ref,
    gain_s,
    tok_s,
    side_s,
    edge_s,
    w_s,
    even_s,
    odd_s,
    own_sem,
    w_sem,
    send_sem,
    recv_sem,
):
    me = lax.axis_index("pack")
    after = {"pack": lax.rem(me + 1, count)}
    before = {"pack": lax.rem(me + count - 1, count)}
    groups = width // 128
    bf = jnp.bfloat16

    def own(w):
        return pltpu.make_async_copy(
            tok_hbm.at[pl.ds(w * TOK, TOK)], tok_s.at[w], own_sem.at[w]
        )

    weight = pltpu.make_async_copy(w_hbm, w_s, w_sem.at[0])
    gain = pltpu.make_async_copy(gain_hbm, gain_s, w_sem.at[1])
    own(0).start()
    own(win_count - 1).start()
    gain.start()
    weight.start()
    for w in range(1, win_count - 1):
        own(w).start()

    pieces = []
    for i in range(HALO_WIN):
        place = pl.ds(i * STRIP, STRIP)
        high = (win_count - HALO_WIN + i + 1) * TOK - STRIP
        pieces.append((after, tok_hbm.at[pl.ds(high, STRIP)], tok_s.at[win_count, place]))
        pieces.append((before, tok_hbm.at[pl.ds(i * TOK, STRIP)], tok_s.at[win_count + 1, place]))
    pieces.append((after, edge_s.at[0], side_s.at[pl.ds(STRIP, STRIP)]))
    pieces.append((before, edge_s.at[1], side_s.at[pl.ds(0, STRIP)]))
    copies = [
        pltpu.make_async_remote_copy(
            src_ref=source,
            dst_ref=target,
            send_sem=send_sem.at[i],
            recv_sem=recv_sem.at[i],
            device_id=where,
            device_id_type=pl.DeviceIdType.MESH,
        )
        for i, (where, source, target) in enumerate(pieces)
    ]
    forward, backward = me < count - 1, me > 0
    barrier = pltpu.get_barrier_semaphore()
    for there, where in ((forward, after), (backward, before)):

        @pl.when(there)
        def _(where=where):
            pl.semaphore_signal(
                barrier, inc=1, device_id=where, device_id_type=pl.DeviceIdType.MESH
            )

    @pl.when(jnp.logical_not(backward))
    def _():
        tok_s[win_count] = jnp.zeros((TOK, D), bf)
        side_s[STRIP:] = jnp.zeros((STRIP, D), bf)

    @pl.when(jnp.logical_not(forward))
    def _():
        tok_s[win_count + 1] = jnp.zeros((TOK, D), bf)
        side_s[:STRIP] = jnp.zeros((STRIP, D), bf)

    def lane_mean(values):
        folded = values[:, :128]
        for lo in range(128, D, 128):
            folded = folded + values[:, lo : lo + 128]
        return jnp.sum(folded, axis=1, keepdims=True) * (1.0 / D)

    def norm_part(rows, out_s, lo):
        values = rows[lo : lo + CHUNK].astype(jnp.float32)
        center = values - lane_mean(values)
        spread = lane_mean(center * center)
        scaled = center * lax.rsqrt(spread + EPS) * gain_s[...]
        out_s[lo : lo + CHUNK] = scaled.astype(bf)
        folded = values[:8]
        for at in range(8, CHUNK, 8):
            folded = folded + values[at : at + 8]
        return folded

    def norm(rows, out_s):
        total = norm_part(rows, out_s, 0)
        for lo in range(CHUNK, rows.shape[0], CHUNK):
            total = total + norm_part(rows, out_s, lo)
        return jnp.sum(total, axis=0, keepdims=True)

    def keys_values(values, block):
        for part, out_ref, edge_ref in ((1, k_ref, ek_ref), (2, v_ref, ev_ref)):
            made = nn_dot(values, w_s[part])
            if block is None:
                sides, at = [made[:STRIP].astype(bf), made[STRIP:].astype(bf)], win_count + 2
            else:
                sides, at = edge_columns(made), block
            made = made.astype(bf)
            for g in range(groups):
                lanes = slice(g * 128, (g + 1) * 128)
                if block is not None:
                    out_ref[block, g] = made[:, lanes]
                edge_ref[at, g, :STRIP] = sides[0][:, lanes]
                edge_ref[at, g, STRIP:] = sides[1][:, lanes]

    def queries(values, block):
        q = nn_dot(values, w_s[0]).astype(bf)
        for g in range(groups):
            qt_ref[block, g] = q[:, g * 128 : (g + 1) * 128].T

    def project(block, in_s):
        values = in_s[...]
        queries(values, block)
        keys_values(values, block)

    def send(first, last):
        for i in range(first, last):
            pl.when((forward, backward)[i % 2])(copies[i].start)

    def receive(which):
        for i in which:
            pl.when((backward, forward)[i % 2])(copies[i].wait_recv)

    pl.semaphore_wait(barrier, jnp.where(forward, 1, 0) + jnp.where(backward, 1, 0))
    sides = 2 * HALO_WIN
    send(0, sides)
    own(win_count - 1).wait()
    edge_s[0] = edge_columns(tok_s[win_count - 1].astype(jnp.float32))[1]
    own(0).wait()
    edge_s[1] = edge_columns(tok_s[0].astype(jnp.float32))[0]
    send(sides, sides + 2)
    gain.wait()
    tsum_ref[pl.ds(0, 1)] = norm(tok_s.at[0], even_s)
    weight.wait()

    def arrive(block):
        @pl.when(block < win_count - 1)
        def _():
            own(jnp.minimum(block, win_count - 2)).wait()

    def both(block, in_s, out_s):
        project(block, in_s)
        tsum_ref[pl.ds(block + 1, 1)] = norm(tok_s.at[block + 1], out_s)

    def pair(i, carry):
        arrive(2 * i + 1)
        both(2 * i, even_s, odd_s)
        arrive(2 * i + 2)
        both(2 * i + 1, odd_s, even_s)
        return carry

    lax.fori_loop(0, win_count // 2 - 1, pair, 0)
    both(win_count - 2, even_s, odd_s)
    project(win_count - 1, odd_s)
    receive(range(0, sides, 2))
    norm(tok_s.at[win_count], even_s)
    receive(range(1, sides, 2))
    keys_values(even_s[...], win_count)
    norm(tok_s.at[win_count + 1], odd_s)
    receive(range(sides, sides + 2))
    keys_values(odd_s[...], win_count + 1)
    norm(side_s, even_s)
    keys_values(even_s[: 2 * STRIP], None)
    for i, copy in enumerate(copies):
        pl.when((forward, backward)[i % 2])(copy.wait_send)


def window_qkv(tokens, gain, weight):
    win_count = tokens.shape[0] // TOK
    width = weight.shape[2]
    groups = width // 128
    bf = jnp.bfloat16
    vmem = pl.BlockSpec(memory_space=pltpu.VMEM)
    hbm = pl.BlockSpec(memory_space=pltpu.HBM)
    edges = (win_count + 3, groups, 2 * STRIP, 128)
    return pl.pallas_call(
        functools.partial(qkv_kernel, lax.axis_size("pack"), win_count, width),
        out_shape=(
            pltpu.VMEM((win_count, groups, 128, TOK), bf),
            pltpu.VMEM((win_count + 2, groups, TOK, 128), bf),
            pltpu.VMEM((win_count + 2, groups, TOK, 128), bf),
            pltpu.VMEM(edges, bf),
            pltpu.VMEM(edges, bf),
            pltpu.VMEM((ROWS, D), jnp.float32),
        ),
        in_specs=[hbm, hbm, hbm],
        out_specs=(vmem,) * 6,
        scratch_shapes=[
            pltpu.VMEM((1, D), jnp.float32),
            pltpu.VMEM((win_count + 2, TOK, D), bf),
            pltpu.VMEM((2 * STRIP, D), bf),
            pltpu.VMEM((2, STRIP, D), bf),
            pltpu.VMEM((3, D, width), bf),
            pltpu.VMEM((TOK, D), bf),
            pltpu.VMEM((TOK, D), bf),
            pltpu.SemaphoreType.DMA((win_count,)),
            pltpu.SemaphoreType.DMA((2,)),
            pltpu.SemaphoreType.DMA((2 * HALO_WIN + 2,)),
            pltpu.SemaphoreType.DMA((2 * HALO_WIN + 2,)),
        ],
        compiler_params=pltpu.CompilerParams(
            collective_id=1, has_side_effects=True, vmem_limit_bytes=24 << 20
        ),
    )(
        pltpu.with_memory_space_constraint(tokens, pltpu.HBM),
        pltpu.with_memory_space_constraint(gain.reshape(1, D), pltpu.HBM),
        pltpu.with_memory_space_constraint(weight.transpose(1, 0, 2), pltpu.HBM),
    )


def attend_kernel(
    win_count,
    width,
    pages,
    windows_ref,
    across_ref,
    qt_ref,
    k_ref,
    v_ref,
    ek_ref,
    ev_ref,
    proj_hbm,
    mixed_hbm,
    projected_ref,
    msum_s,
    proj_s,
    proj_sem,
    pk_s,
    pv_s,
    mask_s,
    prob_s,
    out_s,
    low_s,
    high_s,
    out_sem,
):
    first = lax.axis_index("pack") * win_count
    groups = width // 128
    per = 128 // HDIM
    extra_most = KEYS - TOK
    factor = LOG2E / math.sqrt(HDIM)
    bf = jnp.bfloat16

    def copy_out(w):
        slot = lax.rem(w, 2)
        return pltpu.make_async_copy(
            out_s.at[slot], mixed_hbm.at[pl.ds(w * TOK, TOK)], out_sem.at[slot]
        )

    def find(p, carry):
        page, begin, run = carry
        run = run + windows_ref[p]
        passed = run <= first
        return jnp.where(passed, p + 1, page), jnp.where(passed, run, begin), run

    def pack(w, page, begin):
        across = across_ref[page]
        total = windows_ref[page]
        inside = first + w - begin
        row = lax.div(inside, across)
        col = inside - row * across
        filled = jnp.int32(0)
        for a, b in OFFSETS:
            place = inside + a * across + b
            valid = (col + b >= 0) & (col + b < across) & (row + a >= 0) & (place < total)
            near = w + a * across + b
            size = CORNER if a and b else STRIP
            early, late = near < 0, near >= win_count
            if a < 0:
                block = jnp.where(early, win_count, near)
                index = jnp.where(early, near + HALO_WIN, HALO_WIN - 1)
            elif a > 0:
                block = jnp.where(late, win_count + 1, near)
                index = jnp.where(late, near - win_count, 0)
            else:
                block = jnp.where(early | late, win_count + 2, near)
                index = 0
            start = index * size + (STRIP if b < 0 else 0)
            keys, values = (ek_ref, ev_ref) if b else (k_ref, v_ref)

            block = jnp.where(valid, block, 0)
            start = jnp.where(valid, start, 0)
            source = pl.ds(pl.multiple_of(start, 16), size)
            target = pl.ds(pl.multiple_of(filled, 16), size)
            pk_s[:, target, :] = keys[block, :, source, :]
            pv_s[:, target, :] = values[block, :, source, :]
            filled = filled + jnp.where(valid, size, 0)
        blank = jnp.zeros((groups, 3 * CORNER, 128), bf)
        target = pl.ds(pl.multiple_of(filled, 16), 3 * CORNER)
        pk_s[:, target, :] = blank
        pv_s[:, target, :] = blank
        lane = lax.broadcasted_iota(jnp.int32, mask_s.shape, 1)
        mask_s[...] = jnp.where(lane < filled, 1.0, 0.0).astype(bf)
        return filled

    def finish(w, g, parts):
        piece = jnp.concatenate(parts, axis=0).T
        lanes = pl.ds(pl.multiple_of(g * 128, 128), 128)
        out_s[lax.rem(w, 2), :, lanes] = piece
        msum_s[w, :, lanes] = jnp.sum(piece.astype(jnp.float32), axis=0, keepdims=True)

    def spread(queries, j):
        above = [jnp.zeros((j * HDIM, TOK), bf)] if j else []
        below = [jnp.zeros((128 - (j + 1) * HDIM, TOK), bf)] if j + 1 < per else []
        return jnp.concatenate(above + [queries[j * HDIM : (j + 1) * HDIM]] + below, axis=0)

    def fast(w, extra):
        keys = TOK + extra
        for g in range(groups):
            queries = qt_ref[w, g]
            rows = jnp.concatenate([k_ref[w, g], pk_s[g, :extra]], axis=0) if extra else k_ref[w, g]
            for j in range(per):
                scores = nn_dot(rows, spread(queries, j))
                prob_s[g * per + j, :keys] = jnp.exp2(scores * factor).astype(bf)
        low, high = low_s[...], high_s[...]
        for g in range(groups):
            values = v_ref[w, g].T
            marks = jnp.ones((16, TOK), bf)
            if extra:
                values = jnp.concatenate([values, pv_s[g, :extra].T], axis=1)
                marks = jnp.concatenate([marks, mask_s[:, :extra]], axis=1)
            parts = []
            for j in range(per):
                lhs = jnp.concatenate([values[j * HDIM : (j + 1) * HDIM], marks], axis=0)
                summed = nn_dot(lhs, prob_s[g * per + j, :keys])
                total = summed[HDIM : HDIM + 1]
                low = jnp.minimum(low, total)
                high = jnp.maximum(high, total)
                parts.append((summed[:HDIM] * (1.0 / total)).astype(bf))
            finish(w, g, parts)
        low_s[...] = low
        high_s[...] = high

    def safe(w, filled):
        row = lax.broadcasted_iota(jnp.int32, (extra_most, TOK), 0)

        def group(g, carry):
            queries = qt_ref[w, g]
            values = jnp.concatenate([v_ref[w, g].T, pv_s[g, :extra_most].T], axis=1)
            parts = []
            for j in range(per):
                qz = spread(queries, j)
                near = nn_dot(pk_s[g, :extra_most], qz) * factor
                near = jnp.where(row < filled, near, -1e30)
                scores = jnp.concatenate([nn_dot(k_ref[w, g], qz) * factor, near], axis=0)
                weights = jnp.exp2(scores - jnp.max(scores, axis=0, keepdims=True))
                total = jnp.sum(weights, axis=0, keepdims=True)
                summed = nn_dot(values[j * HDIM : (j + 1) * HDIM], weights.astype(bf))
                parts.append((summed * (1.0 / total)).astype(bf))
            finish(w, g, parts)
            return carry

        lax.fori_loop(0, groups, group, 0)

    def sweep(guarded):
        def step(w, carry):
            page, begin = carry
            end = begin + windows_ref[page]
            passed = first + w >= end
            page = jnp.where(passed, page + 1, page)
            begin = jnp.where(passed, end, begin)
            filled = pack(w, page, begin)

            @pl.when(w >= 2)
            def _():
                copy_out(w - 2).wait()

            if guarded:
                safe(w, filled)
            else:
                chunks = lax.div(filled + STRIP - 1, STRIP)
                for c in range(extra_most // STRIP + 1):

                    @pl.when(chunks == c)
                    def _(c=c):
                        fast(w, c * STRIP)

            copy_out(w).start()
            return page, begin

        zero = jnp.int32(0)
        page, begin, _ = lax.fori_loop(0, pages, find, (zero, zero, zero))
        lax.fori_loop(0, win_count, step, (page, begin))
        copy_out(win_count - 2).wait()
        copy_out(win_count - 1).wait()

    proj_load = pltpu.make_async_copy(proj_hbm, proj_s, proj_sem.at[0])
    proj_load.start()
    msum_s[...] = jnp.zeros_like(msum_s)
    low_s[...] = jnp.ones_like(low_s)
    high_s[...] = jnp.ones_like(high_s)
    sweep(False)
    calm = (jnp.min(low_s[...]) >= SUM_LEAST) & (jnp.max(high_s[...]) <= SUM_MOST)

    @pl.when(jnp.logical_not(calm))
    def _():
        pk_s[...] = jnp.zeros_like(pk_s)
        pv_s[...] = jnp.zeros_like(pv_s)
        sweep(True)

    proj_load.wait()
    sums = msum_s[:, 0, :]
    high = sums.astype(bf)
    low = (sums - high.astype(jnp.float32)).astype(bf)
    both = nn_dot(jnp.concatenate([high, low], axis=0), proj_s[...])
    projected_ref[...] = both[:ROWS] + both[ROWS:]


def window_attention(tables, proj, page_windows, page_width, win_count):
    qt, k, v, ek, ev = tables
    groups = k.shape[1]
    width = groups * 128
    bf = jnp.bfloat16
    vmem = pl.BlockSpec(memory_space=pltpu.VMEM)
    smem = pl.BlockSpec(memory_space=pltpu.SMEM)
    hbm = pl.BlockSpec(memory_space=pltpu.HBM)
    room = KEYS - TOK + STRIP
    arrays = [pltpu.with_memory_space_constraint(a, pltpu.VMEM) for a in tables]
    return pl.pallas_call(
        functools.partial(attend_kernel, win_count, width, page_windows.shape[0]),
        out_shape=(
            jax.ShapeDtypeStruct((win_count * TOK, width), bf),
            pltpu.VMEM((ROWS, D), jnp.float32),
        ),
        in_specs=[smem, smem] + [vmem] * 5 + [hbm],
        out_specs=(hbm, vmem),
        scratch_shapes=[
            pltpu.VMEM((ROWS, 1, width), jnp.float32),
            pltpu.VMEM((width, D), bf),
            pltpu.SemaphoreType.DMA((1,)),
            pltpu.VMEM((groups, room, 128), bf),
            pltpu.VMEM((groups, room, 128), bf),
            pltpu.VMEM((16, room), bf),
            pltpu.VMEM((width // HDIM, KEYS, TOK), bf),
            pltpu.VMEM((2, TOK, width), bf),
            pltpu.VMEM((1, TOK), jnp.float32),
            pltpu.VMEM((1, TOK), jnp.float32),
            pltpu.SemaphoreType.DMA((2,)),
        ],
        compiler_params=pltpu.CompilerParams(vmem_limit_bytes=20 << 20),
    )(page_windows, page_width, *arrays, proj)


def page_kernel(
    count,
    heads,
    win_count,
    proj_ref,
    tsum_ref,
    gain_ref,
    windows_ref,
    docs_ref,
    w_hbm,
    out_hbm,
    out_ref,
    share_s,
    land_s,
    all_s,
    half_s,
    give_s,
    back_s,
    w_s,
    out_s,
    load_sem,
    head_send,
    head_recv,
    pack_send,
    pack_recv,
):
    me, head = lax.axis_index("pack"), lax.axis_index("head")
    pages, columns = out_ref.shape
    width = w_s.shape[2]
    bf = jnp.bfloat16
    mesh_id = pl.DeviceIdType.MESH

    loads = [
        pltpu.make_async_copy(w_hbm, w_s, load_sem.at[0]),
        pltpu.make_async_copy(out_hbm, out_s, load_sem.at[1]),
    ]
    for load in loads:
        load.start()

    half = count // 2
    twin = {"pack": me + 1 - 2 * lax.rem(me, 2)}

    def other_pack(k):
        return {"pack": lax.rem(me + 2 * k, count)}

    def other_head(k):
        return {"head": lax.rem(head + k, heads)}

    barrier = pltpu.get_barrier_semaphore()
    for k in range(1, heads):
        pl.semaphore_signal(barrier, inc=1, device_id=other_head(k), device_id_type=mesh_id)

    pl.semaphore_signal(barrier, inc=1, device_id=twin, device_id_type=mesh_id)

    @pl.loop(1, half)
    def _(k):
        pl.semaphore_signal(barrier, inc=1, device_id=other_pack(k), device_id_type=mesh_id)

    def head_copy(phase, k, source, target):
        return pltpu.make_async_remote_copy(
            src_ref=source,
            dst_ref=target,
            send_sem=head_send.at[phase, k],
            recv_sem=head_recv.at[phase, k],
            device_id=other_head(k),
            device_id_type=mesh_id,
        )

    def features(k):
        start = lax.rem(head + k, heads) * columns
        return pl.ds(pl.multiple_of(start, 128), columns)

    def rows_of(k):
        source = lax.rem(me + count - 2 * k, count)
        return pl.ds(pl.multiple_of(source * ROWS, ROWS), ROWS)

    def pack_copy(k):
        return pltpu.make_async_remote_copy(
            src_ref=all_s.at[rows_of(0)],
            dst_ref=all_s.at[rows_of(0)],
            send_sem=pack_send.at[0, k],
            recv_sem=pack_recv.at[0, k],
            device_id=other_pack(k),
            device_id_type=mesh_id,
        )

    def twin_copy(k):
        return pltpu.make_async_remote_copy(
            src_ref=all_s.at[rows_of(k)],
            dst_ref=all_s.at[rows_of(k)],
            send_sem=pack_send.at[1, k],
            recv_sem=pack_recv.at[1, k],
            device_id=twin,
            device_id_type=mesh_id,
        )

    for k in range(1, heads):
        share_s[k] = proj_ref[:, features(k)].astype(share_s.dtype)
    pl.semaphore_wait(barrier, half + heads - 1)
    first = [head_copy(0, k, share_s.at[k], land_s.at[k]) for k in range(1, heads)]
    for copy in first:
        copy.start()
    total = proj_ref[:, features(0)] + tsum_ref[:, features(0)]
    for k, copy in enumerate(first):
        copy.wait_recv()
        total = total + land_s[k + 1].astype(jnp.float32)
    real = lax.broadcasted_iota(jnp.int32, total.shape, 0) < win_count
    all_s[rows_of(0)] = jnp.where(real, total, 0.0).astype(all_s.dtype)

    @pl.loop(1, half)
    def _(k):
        pack_copy(k).start()

    twin_copy(0).start()

    def grid(shape, axis):
        return lax.broadcasted_iota(jnp.int32, shape, axis)

    square = (pages, pages)
    sizes = windows_ref[...].reshape(1, pages)
    upto = jnp.where(grid(square, 1) <= grid(square, 0), sizes, 0)
    ends = jnp.sum(upto, axis=1, keepdims=True)
    mine = jnp.sum(
        jnp.where(grid(square, 1) == grid(square, 0), sizes, 0), axis=1, keepdims=True
    )
    begins = ends - mine
    shape = (pages, count * ROWS)
    place = grid(shape, 1)
    inner = place & (ROWS - 1)
    window = (place // ROWS) * win_count + inner
    member = (window >= begins) & (window < ends) & (inner < win_count)
    member = jnp.where(member, 1.0, 0.0).astype(bf)
    scale = 1.0 / (mine.astype(jnp.float32) * TOK)
    docs = docs_ref.shape[0]
    lengths = docs_ref[...].reshape(1, docs)
    small = (docs, docs)
    column = jnp.sum(
        jnp.where(grid(small, 1) <= grid(small, 0), lengths, 0), axis=1, keepdims=True
    )
    across = jnp.sum(jnp.where(grid(small, 1) == grid(small, 0), column, 0), axis=0, keepdims=True)
    doc_row = jnp.sum(
        jnp.where(grid((docs, pages), 1) >= column, 1, 0), axis=0, keepdims=True
    )
    doc_col = jnp.sum(
        jnp.where(grid((pages, docs), 0) >= across, 1, 0), axis=1, keepdims=True
    )
    same = doc_row == doc_col

    @pl.loop(1, half)
    def _(k):
        pack_copy(k).wait_recv()
        twin_copy(k).start()

    @pl.loop(0, half)
    def _(k):
        twin_copy(k).wait_recv()

    gathered = all_s[...]
    high = gathered.astype(bf)
    pooled = nn_dot(member, high)
    if gathered.dtype != bf:
        pooled = pooled + nn_dot(member, (gathered - high.astype(jnp.float32)).astype(bf))
    pooled = pooled * scale
    half_s[head] = pooled.astype(half_s.dtype)
    second = [head_copy(1, k, half_s.at[head], half_s.at[head]) for k in range(1, heads)]
    for copy in second:
        copy.start()
    for copy in second:
        copy.wait_recv()
    parts = [jnp.where(head == k, pooled, half_s[k].astype(jnp.float32)) for k in range(heads)]
    normed = normalize(jnp.concatenate(parts, axis=1), gain_ref[...])
    for load in loads:
        load.wait()
    query, keys, values = (nn_dot(normed, w_s[i]).astype(bf) for i in range(3))
    owner = grid((pages, width), 1) // HDIM
    local = width // HDIM
    wide = jnp.concatenate(
        [jnp.where(owner == h, query.astype(jnp.float32), 0.0).astype(bf) for h in range(local)],
        axis=0,
    )
    scores = lax.dot_general(
        wide, keys, (((1,), (1,)), ((), ())), preferred_element_type=jnp.float32
    ) / math.sqrt(HDIM)
    scores = scores.reshape(local, pages, pages)
    scores = jnp.where(same[None], scores, -1e30)
    weights = jnp.exp(scores - jnp.max(scores, axis=-1, keepdims=True))
    probs = (weights / jnp.sum(weights, axis=-1, keepdims=True)).astype(bf)
    mixed = nn_dot(probs.reshape(local * pages, pages), values).reshape(local, pages, width)
    context = jnp.zeros((pages, width), jnp.float32)
    for h in range(local):
        context = jnp.where(owner == h, mixed[h], context)
    branch = nn_dot(context.astype(bf), out_s[...])
    give_s[0] = branch
    for k in range(1, heads):
        back_s[k] = give_s[0, :, features(k)].astype(back_s.dtype)
    third = [head_copy(2, k, back_s.at[k], back_s.at[heads + k]) for k in range(1, heads)]
    for copy in third:
        copy.start()
    result = pooled + give_s[0, :, features(0)]
    for k, copy in enumerate(third):
        copy.wait_recv()
        result = result + back_s[heads + k + 1].astype(jnp.float32)
    out_ref[...] = result
    for copy in first + second + third:
        copy.wait_send()

    @pl.loop(1, half)
    def _(k):
        pack_copy(k).wait_send()

    @pl.loop(0, half)
    def _(k):
        twin_copy(k).wait_send()


def page_layer(projected, token_sums, gain, weight, proj, page_windows, doc_pages, win_count):
    heads = lax.axis_size("head")
    count = lax.axis_size("pack")
    pages = page_windows.shape[0]
    width = weight.shape[2]
    columns = D // heads
    bf = jnp.bfloat16
    vmem = pl.BlockSpec(memory_space=pltpu.VMEM)
    hbm = pl.BlockSpec(memory_space=pltpu.HBM)
    return pl.pallas_call(
        functools.partial(page_kernel, count, heads, win_count),
        out_shape=jax.ShapeDtypeStruct((pages, columns), jnp.float32),
        in_specs=[vmem] * 5 + [hbm] * 2,
        out_specs=vmem,
        scratch_shapes=[
            pltpu.VMEM((heads, ROWS, columns), jnp.float32),
            pltpu.VMEM((heads, ROWS, columns), jnp.float32),
            pltpu.VMEM((count * ROWS, columns), bf),
            pltpu.VMEM((heads, pages, columns), bf),
            pltpu.VMEM((1, pages, D), jnp.float32),
            pltpu.VMEM((2 * heads, pages, columns), bf),
            pltpu.VMEM((3, D, width), bf),
            pltpu.VMEM((width, D), bf),
            pltpu.SemaphoreType.DMA((2,)),
            pltpu.SemaphoreType.DMA((3, heads)),
            pltpu.SemaphoreType.DMA((3, heads)),
            pltpu.SemaphoreType.DMA((2, count // 2)),
            pltpu.SemaphoreType.DMA((2, count // 2)),
        ],
        compiler_params=pltpu.CompilerParams(
            collective_id=2, has_side_effects=True, vmem_limit_bytes=24 << 20
        ),
    )(
        projected,
        token_sums,
        gain.reshape(1, D),
        page_windows,
        doc_pages,
        weight.transpose(1, 0, 2),
        proj,
    )


def shards(
    tokens,
    ln_gain,
    attn_weight,
    attn_proj,
    page_gain,
    page_weight,
    page_proj,
    page_windows,
    page_width,
    doc_pages,
):
    win_count = tokens.shape[0] // TOK
    *tables, token_sums = window_qkv(tokens, ln_gain, attn_weight)
    mixed, projected = window_attention(tables, attn_proj, page_windows, page_width, win_count)
    page_out = page_layer(
        projected,
        token_sums,
        page_gain,
        page_weight,
        page_proj,
        page_windows,
        doc_pages,
        win_count,
    )
    return (mixed, page_out)


def solution(mesh):
    placed = (
        P(("rep", "pack"), None),
        P(),
        P(None, None, "head"),
        P("head", None),
        P(),
        P(None, None, "head"),
        P("head", None),
        P("rep"),
        P("rep"),
        P("rep"),
    )
    return jax.shard_map(
        shards,
        mesh=mesh,
        in_specs=placed,
        out_specs=(P(("rep", "pack"), "head"), P("rep", "head")),
        check_vma=False,
    )
```

```python
import functools
import math

import jax
import jax.numpy as jnp
import numpy as np
from jax import lax
from jax.experimental import pallas as pl
from jax.experimental.pallas import tpu as pltpu
from jax.sharding import PartitionSpec as P

D = 1024
HDIM = 32
WIN = 16
HALO = 4
HALO_WIN = 4
TOK = WIN * WIN
STRIP = WIN * HALO
CORNER = HALO * HALO
SIDE_KEYS = 4 * STRIP + 4 * CORNER
KEYS = TOK + SIDE_KEYS
SUM_LEAST = 2.0**-60
SUM_MOST = 2.0**60
ROWS = 16
UNIT = 32
EPS = 1e-05
LOG2E = 1.4426950408889634
OFFSETS = ((-1, 0), (1, 0), (0, -1), (0, 1), (-1, -1), (-1, 1), (1, -1), (1, 1))


CHUNK = 32


def edge_columns(values):
    tall = values.reshape(WIN // 2, 2 * WIN, values.shape[1])
    upper = lax.broadcasted_iota(jnp.int32, (WIN // 2, 8, values.shape[1]), 1) < HALO

    def turned(lo):
        return pltpu.roll(tall[:, lo : lo + 8], HALO, 1)

    left = jnp.where(upper, tall[:, :8], turned(WIN))
    right = jnp.where(upper, turned(8), tall[:, WIN + 8 :])
    return [side.reshape(STRIP, values.shape[1]).astype(jnp.bfloat16) for side in (left, right)]


def nn_dot(a, b):
    return jnp.dot(a, b, preferred_element_type=jnp.float32)


def normalize(values, gain):
    center = values - jnp.mean(values, axis=-1, keepdims=True)
    spread = jnp.mean(center * center, axis=-1, keepdims=True)
    return (center * lax.rsqrt(spread + EPS) * gain).astype(jnp.bfloat16)


def qkv_kernel(
    count,
    win_count,
    width,
    tok_hbm,
    gain_hbm,
    w_hbm,
    qt_ref,
    k_ref,
    v_ref,
    ek_ref,
    ev_ref,
    tsum_ref,
    gain_s,
    tok_s,
    side_s,
    edge_s,
    w_s,
    even_s,
    odd_s,
    own_sem,
    w_sem,
    send_sem,
    recv_sem,
):
    me = lax.axis_index("pack")
    after = {"pack": lax.rem(me + 1, count)}
    before = {"pack": lax.rem(me + count - 1, count)}
    groups = width // 128
    bf = jnp.bfloat16

    def own(w):
        return pltpu.make_async_copy(
            tok_hbm.at[pl.ds(w * TOK, TOK)], tok_s.at[w], own_sem.at[w]
        )

    weight = pltpu.make_async_copy(w_hbm, w_s, w_sem.at[0])
    gain = pltpu.make_async_copy(gain_hbm, gain_s, w_sem.at[1])
    own(0).start()
    own(win_count - 1).start()
    gain.start()
    weight.start()
    for w in range(1, win_count - 1):
        own(w).start()

    pieces = []
    for i in range(HALO_WIN):
        place = pl.ds(i * STRIP, STRIP)
        high = (win_count - HALO_WIN + i + 1) * TOK - STRIP
        pieces.append((after, tok_hbm.at[pl.ds(high, STRIP)], tok_s.at[win_count, place]))
        pieces.append((before, tok_hbm.at[pl.ds(i * TOK, STRIP)], tok_s.at[win_count + 1, place]))
    pieces.append((after, edge_s.at[0], side_s.at[pl.ds(STRIP, STRIP)]))
    pieces.append((before, edge_s.at[1], side_s.at[pl.ds(0, STRIP)]))
    copies = [
        pltpu.make_async_remote_copy(
            src_ref=source,
            dst_ref=target,
            send_sem=send_sem.at[i],
            recv_sem=recv_sem.at[i],
            device_id=where,
            device_id_type=pl.DeviceIdType.MESH,
        )
        for i, (where, source, target) in enumerate(pieces)
    ]
    forward, backward = me < count - 1, me > 0
    barrier = pltpu.get_barrier_semaphore()
    for there, where in ((forward, after), (backward, before)):

        @pl.when(there)
        def _(where=where):
            pl.semaphore_signal(
                barrier, inc=1, device_id=where, device_id_type=pl.DeviceIdType.MESH
            )

    @pl.when(jnp.logical_not(backward))
    def _():
        tok_s[win_count] = jnp.zeros((TOK, D), bf)
        side_s[STRIP:] = jnp.zeros((STRIP, D), bf)

    @pl.when(jnp.logical_not(forward))
    def _():
        tok_s[win_count + 1] = jnp.zeros((TOK, D), bf)
        side_s[:STRIP] = jnp.zeros((STRIP, D), bf)

    def lane_mean(values):
        folded = values[:, :128]
        for lo in range(128, D, 128):
            folded = folded + values[:, lo : lo + 128]
        return jnp.sum(folded, axis=1, keepdims=True) * (1.0 / D)

    def norm_part(rows, out_s, lo):
        values = rows[lo : lo + CHUNK].astype(jnp.float32)
        center = values - lane_mean(values)
        spread = lane_mean(center * center)
        scaled = center * lax.rsqrt(spread + EPS) * gain_s[...]
        out_s[lo : lo + CHUNK] = scaled.astype(bf)
        folded = values[:8]
        for at in range(8, CHUNK, 8):
            folded = folded + values[at : at + 8]
        return folded

    def norm(rows, out_s):
        total = norm_part(rows, out_s, 0)
        for lo in range(CHUNK, rows.shape[0], CHUNK):
            total = total + norm_part(rows, out_s, lo)
        return jnp.sum(total, axis=0, keepdims=True)

    def keys_values(values, block):
        for part, out_ref, edge_ref in ((1, k_ref, ek_ref), (2, v_ref, ev_ref)):
            made = nn_dot(values, w_s[part])
            if block is None:
                sides, at = [made[:STRIP].astype(bf), made[STRIP:].astype(bf)], win_count + 2
            else:
                sides, at = edge_columns(made), block
            made = made.astype(bf)
            for g in range(groups):
                lanes = slice(g * 128, (g + 1) * 128)
                if block is not None:
                    out_ref[block, g] = made[:, lanes]
                edge_ref[at, g, :STRIP] = sides[0][:, lanes]
                edge_ref[at, g, STRIP:] = sides[1][:, lanes]

    def queries(values, block):
        q = nn_dot(values, w_s[0]).astype(bf)
        for g in range(groups):
            qt_ref[block, g] = q[:, g * 128 : (g + 1) * 128].T

    def project(block, in_s):
        values = in_s[...]
        queries(values, block)
        keys_values(values, block)

    def send(first, last):
        for i in range(first, last):
            pl.when((forward, backward)[i % 2])(copies[i].start)

    def receive(which):
        for i in which:
            pl.when((backward, forward)[i % 2])(copies[i].wait_recv)

    pl.semaphore_wait(barrier, jnp.where(forward, 1, 0) + jnp.where(backward, 1, 0))
    sides = 2 * HALO_WIN
    send(0, sides)
    own(win_count - 1).wait()
    edge_s[0] = edge_columns(tok_s[win_count - 1].astype(jnp.float32))[1]
    own(0).wait()
    edge_s[1] = edge_columns(tok_s[0].astype(jnp.float32))[0]
    send(sides, sides + 2)
    gain.wait()
    tsum_ref[pl.ds(0, 1)] = norm(tok_s.at[0], even_s)
    weight.wait()

    def arrive(block):
        @pl.when(block < win_count - 1)
        def _():
            own(jnp.minimum(block, win_count - 2)).wait()

    def both(block, in_s, out_s):
        project(block, in_s)
        tsum_ref[pl.ds(block + 1, 1)] = norm(tok_s.at[block + 1], out_s)

    def pair(i, carry):
        arrive(2 * i + 1)
        both(2 * i, even_s, odd_s)
        arrive(2 * i + 2)
        both(2 * i + 1, odd_s, even_s)
        return carry

    lax.fori_loop(0, win_count // 2 - 1, pair, 0)
    both(win_count - 2, even_s, odd_s)
    project(win_count - 1, odd_s)
    receive(range(0, sides, 2))
    norm(tok_s.at[win_count], even_s)
    receive(range(1, sides, 2))
    keys_values(even_s[...], win_count)
    norm(tok_s.at[win_count + 1], odd_s)
    receive(range(sides, sides + 2))
    keys_values(odd_s[...], win_count + 1)
    norm(side_s, even_s)
    keys_values(even_s[: 2 * STRIP], None)
    for i, copy in enumerate(copies):
        pl.when((forward, backward)[i % 2])(copy.wait_send)


def window_qkv(tokens, gain, weight):
    win_count = tokens.shape[0] // TOK
    width = weight.shape[2]
    groups = width // 128
    bf = jnp.bfloat16
    vmem = pl.BlockSpec(memory_space=pltpu.VMEM)
    hbm = pl.BlockSpec(memory_space=pltpu.HBM)
    edges = (win_count + 3, groups, 2 * STRIP, 128)
    return pl.pallas_call(
        functools.partial(qkv_kernel, lax.axis_size("pack"), win_count, width),
        out_shape=(
            pltpu.VMEM((win_count, groups, 128, TOK), bf),
            pltpu.VMEM((win_count + 2, groups, TOK, 128), bf),
            pltpu.VMEM((win_count + 2, groups, TOK, 128), bf),
            pltpu.VMEM(edges, bf),
            pltpu.VMEM(edges, bf),
            pltpu.VMEM((ROWS, D), jnp.float32),
        ),
        in_specs=[hbm, hbm, hbm],
        out_specs=(vmem,) * 6,
        scratch_shapes=[
            pltpu.VMEM((1, D), jnp.float32),
            pltpu.VMEM((win_count + 2, TOK, D), bf),
            pltpu.VMEM((2 * STRIP, D), bf),
            pltpu.VMEM((2, STRIP, D), bf),
            pltpu.VMEM((3, D, width), bf),
            pltpu.VMEM((TOK, D), bf),
            pltpu.VMEM((TOK, D), bf),
            pltpu.SemaphoreType.DMA((win_count,)),
            pltpu.SemaphoreType.DMA((2,)),
            pltpu.SemaphoreType.DMA((2 * HALO_WIN + 2,)),
            pltpu.SemaphoreType.DMA((2 * HALO_WIN + 2,)),
        ],
        compiler_params=pltpu.CompilerParams(
            collective_id=1, has_side_effects=True, vmem_limit_bytes=24 << 20
        ),
    )(
        pltpu.with_memory_space_constraint(tokens, pltpu.HBM),
        pltpu.with_memory_space_constraint(gain.reshape(1, D), pltpu.HBM),
        pltpu.with_memory_space_constraint(weight.transpose(1, 0, 2), pltpu.HBM),
    )


def attend_kernel(
    win_count,
    width,
    pages,
    windows_ref,
    across_ref,
    qt_ref,
    k_ref,
    v_ref,
    ek_ref,
    ev_ref,
    proj_hbm,
    mixed_hbm,
    projected_ref,
    msum_s,
    proj_s,
    proj_sem,
    pk_s,
    pv_s,
    mask_s,
    prob_s,
    out_s,
    low_s,
    high_s,
    out_sem,
):
    first = lax.axis_index("pack") * win_count
    groups = width // 128
    per = 128 // HDIM
    extra_most = KEYS - TOK
    factor = LOG2E / math.sqrt(HDIM)
    bf = jnp.bfloat16

    def copy_out(w):
        slot = lax.rem(w, 2)
        return pltpu.make_async_copy(
            out_s.at[slot], mixed_hbm.at[pl.ds(w * TOK, TOK)], out_sem.at[slot]
        )

    def find(p, carry):
        page, begin, run = carry
        run = run + windows_ref[p]
        passed = run <= first
        return jnp.where(passed, p + 1, page), jnp.where(passed, run, begin), run

    def pack(w, page, begin):
        across = across_ref[page]
        total = windows_ref[page]
        inside = first + w - begin
        row = lax.div(inside, across)
        col = inside - row * across
        filled = jnp.int32(0)
        for a, b in OFFSETS:
            place = inside + a * across + b
            valid = (col + b >= 0) & (col + b < across) & (row + a >= 0) & (place < total)
            near = w + a * across + b
            size = CORNER if a and b else STRIP
            early, late = near < 0, near >= win_count
            if a < 0:
                block = jnp.where(early, win_count, near)
                index = jnp.where(early, near + HALO_WIN, HALO_WIN - 1)
            elif a > 0:
                block = jnp.where(late, win_count + 1, near)
                index = jnp.where(late, near - win_count, 0)
            else:
                block = jnp.where(early | late, win_count + 2, near)
                index = 0
            start = index * size + (STRIP if b < 0 else 0)
            keys, values = (ek_ref, ev_ref) if b else (k_ref, v_ref)

            block = jnp.where(valid, block, 0)
            start = jnp.where(valid, start, 0)
            source = pl.ds(pl.multiple_of(start, 16), size)
            target = pl.ds(pl.multiple_of(filled, 16), size)
            pk_s[:, target, :] = keys[block, :, source, :]
            pv_s[:, target, :] = values[block, :, source, :]
            filled = filled + jnp.where(valid, size, 0)
        blank = jnp.zeros((groups, UNIT - CORNER, 128), bf)
        target = pl.ds(pl.multiple_of(filled, 16), UNIT - CORNER)
        pk_s[:, target, :] = blank
        pv_s[:, target, :] = blank
        lane = lax.broadcasted_iota(jnp.int32, mask_s.shape, 1)
        mask_s[...] = jnp.where(lane < filled, 1.0, 0.0).astype(bf)
        return filled

    def finish(w, g, parts):
        piece = jnp.concatenate(parts, axis=0).T
        lanes = pl.ds(pl.multiple_of(g * 128, 128), 128)
        out_s[lax.rem(w, 2), :, lanes] = piece
        msum_s[w, :, lanes] = jnp.sum(piece.astype(jnp.float32), axis=0, keepdims=True)

    def spread(queries, j):
        above = [jnp.zeros((j * HDIM, TOK), bf)] if j else []
        below = [jnp.zeros((128 - (j + 1) * HDIM, TOK), bf)] if j + 1 < per else []
        return jnp.concatenate(above + [queries[j * HDIM : (j + 1) * HDIM]] + below, axis=0)

    def fast(w, extra):
        keys = TOK + extra
        for g in range(groups):
            queries = qt_ref[w, g]
            rows = jnp.concatenate([k_ref[w, g], pk_s[g, :extra]], axis=0) if extra else k_ref[w, g]
            for j in range(per):
                scores = nn_dot(rows, spread(queries, j))
                prob_s[g * per + j, :keys] = jnp.exp2(scores * factor).astype(bf)
        low, high = low_s[...], high_s[...]
        for g in range(groups):
            values = v_ref[w, g].T
            marks = jnp.ones((16, TOK), bf)
            if extra:
                values = jnp.concatenate([values, pv_s[g, :extra].T], axis=1)
                marks = jnp.concatenate([marks, mask_s[:, :extra]], axis=1)
            parts = []
            for j in range(per):
                lhs = jnp.concatenate([values[j * HDIM : (j + 1) * HDIM], marks], axis=0)
                summed = nn_dot(lhs, prob_s[g * per + j, :keys])
                total = summed[HDIM : HDIM + 1]
                low = jnp.minimum(low, total)
                high = jnp.maximum(high, total)
                parts.append((summed[:HDIM] * (1.0 / total)).astype(bf))
            finish(w, g, parts)
        low_s[...] = low
        high_s[...] = high

    def safe(w, filled):
        row = lax.broadcasted_iota(jnp.int32, (extra_most, TOK), 0)

        def group(g, carry):
            queries = qt_ref[w, g]
            values = jnp.concatenate([v_ref[w, g].T, pv_s[g, :extra_most].T], axis=1)
            parts = []
            for j in range(per):
                qz = spread(queries, j)
                near = nn_dot(pk_s[g, :extra_most], qz) * factor
                near = jnp.where(row < filled, near, -1e30)
                scores = jnp.concatenate([nn_dot(k_ref[w, g], qz) * factor, near], axis=0)
                weights = jnp.exp2(scores - jnp.max(scores, axis=0, keepdims=True))
                total = jnp.sum(weights, axis=0, keepdims=True)
                summed = nn_dot(values[j * HDIM : (j + 1) * HDIM], weights.astype(bf))
                parts.append((summed * (1.0 / total)).astype(bf))
            finish(w, g, parts)
            return carry

        lax.fori_loop(0, groups, group, 0)

    def sweep(guarded):
        def step(w, carry):
            page, begin = carry
            end = begin + windows_ref[page]
            passed = first + w >= end
            page = jnp.where(passed, page + 1, page)
            begin = jnp.where(passed, end, begin)
            filled = pack(w, page, begin)

            @pl.when(w >= 2)
            def _():
                copy_out(w - 2).wait()

            if guarded:
                safe(w, filled)
            else:
                chunks = lax.div(filled + UNIT - 1, UNIT)
                for c in range(extra_most // UNIT + 1):

                    @pl.when(chunks == c)
                    def _(c=c):
                        fast(w, c * UNIT)

            copy_out(w).start()
            return page, begin

        zero = jnp.int32(0)
        page, begin, _ = lax.fori_loop(0, pages, find, (zero, zero, zero))
        lax.fori_loop(0, win_count, step, (page, begin))
        copy_out(win_count - 2).wait()
        copy_out(win_count - 1).wait()

    proj_load = pltpu.make_async_copy(proj_hbm, proj_s, proj_sem.at[0])
    proj_load.start()
    msum_s[...] = jnp.zeros_like(msum_s)
    low_s[...] = jnp.ones_like(low_s)
    high_s[...] = jnp.ones_like(high_s)
    sweep(False)
    calm = (jnp.min(low_s[...]) >= SUM_LEAST) & (jnp.max(high_s[...]) <= SUM_MOST)

    @pl.when(jnp.logical_not(calm))
    def _():
        pk_s[...] = jnp.zeros_like(pk_s)
        pv_s[...] = jnp.zeros_like(pv_s)
        sweep(True)

    proj_load.wait()
    sums = msum_s[:, 0, :]
    high = sums.astype(bf)
    low = (sums - high.astype(jnp.float32)).astype(bf)
    both = nn_dot(jnp.concatenate([high, low], axis=0), proj_s[...])
    projected_ref[...] = both[:ROWS] + both[ROWS:]


def window_attention(tables, proj, page_windows, page_width, win_count):
    qt, k, v, ek, ev = tables
    groups = k.shape[1]
    width = groups * 128
    bf = jnp.bfloat16
    vmem = pl.BlockSpec(memory_space=pltpu.VMEM)
    smem = pl.BlockSpec(memory_space=pltpu.SMEM)
    hbm = pl.BlockSpec(memory_space=pltpu.HBM)
    room = KEYS - TOK + STRIP
    arrays = [pltpu.with_memory_space_constraint(a, pltpu.VMEM) for a in tables]
    return pl.pallas_call(
        functools.partial(attend_kernel, win_count, width, page_windows.shape[0]),
        out_shape=(
            jax.ShapeDtypeStruct((win_count * TOK, width), bf),
            pltpu.VMEM((ROWS, D), jnp.float32),
        ),
        in_specs=[smem, smem] + [vmem] * 5 + [hbm],
        out_specs=(hbm, vmem),
        scratch_shapes=[
            pltpu.VMEM((ROWS, 1, width), jnp.float32),
            pltpu.VMEM((width, D), bf),
            pltpu.SemaphoreType.DMA((1,)),
            pltpu.VMEM((groups, room, 128), bf),
            pltpu.VMEM((groups, room, 128), bf),
            pltpu.VMEM((16, room), bf),
            pltpu.VMEM((width // HDIM, KEYS, TOK), bf),
            pltpu.VMEM((2, TOK, width), bf),
            pltpu.VMEM((1, TOK), jnp.float32),
            pltpu.VMEM((1, TOK), jnp.float32),
            pltpu.SemaphoreType.DMA((2,)),
        ],
        compiler_params=pltpu.CompilerParams(vmem_limit_bytes=20 << 20),
    )(page_windows, page_width, *arrays, proj)


def page_kernel(
    count,
    heads,
    win_count,
    proj_ref,
    tsum_ref,
    gain_ref,
    windows_ref,
    docs_ref,
    w_hbm,
    out_hbm,
    out_ref,
    share_s,
    land_s,
    all_s,
    half_s,
    give_s,
    back_s,
    w_s,
    out_s,
    load_sem,
    head_send,
    head_recv,
    pack_send,
    pack_recv,
):
    me, head = lax.axis_index("pack"), lax.axis_index("head")
    pages, columns = out_ref.shape
    width = w_s.shape[2]
    bf = jnp.bfloat16
    mesh_id = pl.DeviceIdType.MESH

    loads = [
        pltpu.make_async_copy(w_hbm, w_s, load_sem.at[0]),
        pltpu.make_async_copy(out_hbm, out_s, load_sem.at[1]),
    ]
    for load in loads:
        load.start()

    half = count // 2
    twin = {"pack": me + 1 - 2 * lax.rem(me, 2)}

    def other_pack(k):
        return {"pack": lax.rem(me + 2 * k, count)}

    def other_head(k):
        return {"head": lax.rem(head + k, heads)}

    barrier = pltpu.get_barrier_semaphore()
    for k in range(1, heads):
        pl.semaphore_signal(barrier, inc=1, device_id=other_head(k), device_id_type=mesh_id)

    pl.semaphore_signal(barrier, inc=1, device_id=twin, device_id_type=mesh_id)

    @pl.loop(1, half)
    def _(k):
        pl.semaphore_signal(barrier, inc=1, device_id=other_pack(k), device_id_type=mesh_id)

    def head_copy(phase, k, source, target):
        return pltpu.make_async_remote_copy(
            src_ref=source,
            dst_ref=target,
            send_sem=head_send.at[phase, k],
            recv_sem=head_recv.at[phase, k],
            device_id=other_head(k),
            device_id_type=mesh_id,
        )

    def features(k):
        start = lax.rem(head + k, heads) * columns
        return pl.ds(pl.multiple_of(start, 128), columns)

    def rows_of(k):
        source = lax.rem(me + count - 2 * k, count)
        return pl.ds(pl.multiple_of(source * ROWS, ROWS), ROWS)

    def pack_copy(k):
        return pltpu.make_async_remote_copy(
            src_ref=all_s.at[rows_of(0)],
            dst_ref=all_s.at[rows_of(0)],
            send_sem=pack_send.at[0, k],
            recv_sem=pack_recv.at[0, k],
            device_id=other_pack(k),
            device_id_type=mesh_id,
        )

    def twin_copy(k):
        return pltpu.make_async_remote_copy(
            src_ref=all_s.at[rows_of(k)],
            dst_ref=all_s.at[rows_of(k)],
            send_sem=pack_send.at[1, k],
            recv_sem=pack_recv.at[1, k],
            device_id=twin,
            device_id_type=mesh_id,
        )

    for k in range(1, heads):
        share_s[k] = proj_ref[:, features(k)].astype(share_s.dtype)
    pl.semaphore_wait(barrier, half + heads - 1)
    first = [head_copy(0, k, share_s.at[k], land_s.at[k]) for k in range(1, heads)]
    for copy in first:
        copy.start()
    total = proj_ref[:, features(0)] + tsum_ref[:, features(0)]
    for k, copy in enumerate(first):
        copy.wait_recv()
        total = total + land_s[k + 1].astype(jnp.float32)
    real = lax.broadcasted_iota(jnp.int32, total.shape, 0) < win_count
    all_s[rows_of(0)] = jnp.where(real, total, 0.0).astype(all_s.dtype)

    @pl.loop(1, half)
    def _(k):
        pack_copy(k).start()

    twin_copy(0).start()

    def grid(shape, axis):
        return lax.broadcasted_iota(jnp.int32, shape, axis)

    square = (pages, pages)
    sizes = windows_ref[...].reshape(1, pages)
    upto = jnp.where(grid(square, 1) <= grid(square, 0), sizes, 0)
    ends = jnp.sum(upto, axis=1, keepdims=True)
    mine = jnp.sum(
        jnp.where(grid(square, 1) == grid(square, 0), sizes, 0), axis=1, keepdims=True
    )
    begins = ends - mine
    shape = (pages, count * ROWS)
    place = grid(shape, 1)
    inner = place & (ROWS - 1)
    window = (place // ROWS) * win_count + inner
    member = (window >= begins) & (window < ends) & (inner < win_count)
    member = jnp.where(member, 1.0, 0.0).astype(bf)
    scale = 1.0 / (mine.astype(jnp.float32) * TOK)
    docs = docs_ref.shape[0]
    lengths = docs_ref[...].reshape(1, docs)
    small = (docs, docs)
    column = jnp.sum(
        jnp.where(grid(small, 1) <= grid(small, 0), lengths, 0), axis=1, keepdims=True
    )
    across = jnp.sum(jnp.where(grid(small, 1) == grid(small, 0), column, 0), axis=0, keepdims=True)
    doc_row = jnp.sum(
        jnp.where(grid((docs, pages), 1) >= column, 1, 0), axis=0, keepdims=True
    )
    doc_col = jnp.sum(
        jnp.where(grid((pages, docs), 0) >= across, 1, 0), axis=1, keepdims=True
    )
    same = doc_row == doc_col

    @pl.loop(1, half)
    def _(k):
        pack_copy(k).wait_recv()
        twin_copy(k).start()

    @pl.loop(0, half)
    def _(k):
        twin_copy(k).wait_recv()

    gathered = all_s[...]
    high = gathered.astype(bf)
    pooled = nn_dot(member, high)
    if gathered.dtype != bf:
        pooled = pooled + nn_dot(member, (gathered - high.astype(jnp.float32)).astype(bf))
    pooled = pooled * scale
    half_s[head] = pooled.astype(half_s.dtype)
    second = [head_copy(1, k, half_s.at[head], half_s.at[head]) for k in range(1, heads)]
    for copy in second:
        copy.start()
    for copy in second:
        copy.wait_recv()
    parts = [jnp.where(head == k, pooled, half_s[k].astype(jnp.float32)) for k in range(heads)]
    normed = normalize(jnp.concatenate(parts, axis=1), gain_ref[...])
    for load in loads:
        load.wait()
    query, keys, values = (nn_dot(normed, w_s[i]).astype(bf) for i in range(3))
    owner = grid((pages, width), 1) // HDIM
    local = width // HDIM
    wide = jnp.concatenate(
        [jnp.where(owner == h, query.astype(jnp.float32), 0.0).astype(bf) for h in range(local)],
        axis=0,
    )
    scores = lax.dot_general(
        wide, keys, (((1,), (1,)), ((), ())), preferred_element_type=jnp.float32
    ) / math.sqrt(HDIM)
    scores = scores.reshape(local, pages, pages)
    scores = jnp.where(same[None], scores, -1e30)
    weights = jnp.exp(scores - jnp.max(scores, axis=-1, keepdims=True))
    probs = (weights / jnp.sum(weights, axis=-1, keepdims=True)).astype(bf)
    mixed = nn_dot(probs.reshape(local * pages, pages), values).reshape(local, pages, width)
    context = jnp.zeros((pages, width), jnp.float32)
    for h in range(local):
        context = jnp.where(owner == h, mixed[h], context)
    branch = nn_dot(context.astype(bf), out_s[...])
    give_s[0] = branch
    for k in range(1, heads):
        back_s[k] = give_s[0, :, features(k)].astype(back_s.dtype)
    third = [head_copy(2, k, back_s.at[k], back_s.at[heads + k]) for k in range(1, heads)]
    for copy in third:
        copy.start()
    result = pooled + give_s[0, :, features(0)]
    for k, copy in enumerate(third):
        copy.wait_recv()
        result = result + back_s[heads + k + 1].astype(jnp.float32)
    out_ref[...] = result
    for copy in first + second + third:
        copy.wait_send()

    @pl.loop(1, half)
    def _(k):
        pack_copy(k).wait_send()

    @pl.loop(0, half)
    def _(k):
        twin_copy(k).wait_send()


def page_layer(projected, token_sums, gain, weight, proj, page_windows, doc_pages, win_count):
    heads = lax.axis_size("head")
    count = lax.axis_size("pack")
    pages = page_windows.shape[0]
    width = weight.shape[2]
    columns = D // heads
    bf = jnp.bfloat16
    vmem = pl.BlockSpec(memory_space=pltpu.VMEM)
    hbm = pl.BlockSpec(memory_space=pltpu.HBM)
    return pl.pallas_call(
        functools.partial(page_kernel, count, heads, win_count),
        out_shape=jax.ShapeDtypeStruct((pages, columns), jnp.float32),
        in_specs=[vmem] * 5 + [hbm] * 2,
        out_specs=vmem,
        scratch_shapes=[
            pltpu.VMEM((heads, ROWS, columns), jnp.float32),
            pltpu.VMEM((heads, ROWS, columns), jnp.float32),
            pltpu.VMEM((count * ROWS, columns), bf),
            pltpu.VMEM((heads, pages, columns), bf),
            pltpu.VMEM((1, pages, D), jnp.float32),
            pltpu.VMEM((2 * heads, pages, columns), bf),
            pltpu.VMEM((3, D, width), bf),
            pltpu.VMEM((width, D), bf),
            pltpu.SemaphoreType.DMA((2,)),
            pltpu.SemaphoreType.DMA((3, heads)),
            pltpu.SemaphoreType.DMA((3, heads)),
            pltpu.SemaphoreType.DMA((2, count // 2)),
            pltpu.SemaphoreType.DMA((2, count // 2)),
        ],
        compiler_params=pltpu.CompilerParams(
            collective_id=2, has_side_effects=True, vmem_limit_bytes=24 << 20
        ),
    )(
        projected,
        token_sums,
        gain.reshape(1, D),
        page_windows,
        doc_pages,
        weight.transpose(1, 0, 2),
        proj,
    )


def shards(
    tokens,
    ln_gain,
    attn_weight,
    attn_proj,
    page_gain,
    page_weight,
    page_proj,
    page_windows,
    page_width,
    doc_pages,
):
    win_count = tokens.shape[0] // TOK
    *tables, token_sums = window_qkv(tokens, ln_gain, attn_weight)
    mixed, projected = window_attention(tables, attn_proj, page_windows, page_width, win_count)
    page_out = page_layer(
        projected,
        token_sums,
        page_gain,
        page_weight,
        page_proj,
        page_windows,
        doc_pages,
        win_count,
    )
    return (mixed, page_out)


def solution(mesh):
    placed = (
        P(("rep", "pack"), None),
        P(),
        P(None, None, "head"),
        P("head", None),
        P(),
        P(None, None, "head"),
        P("head", None),
        P("rep"),
        P("rep"),
        P("rep"),
    )
    return jax.shard_map(
        shards,
        mesh=mesh,
        in_specs=placed,
        out_specs=(P(("rep", "pack"), "head"), P("rep", "head")),
        check_vma=False,
    )
```

```python
import functools
import math

import jax
import jax.numpy as jnp
import numpy as np
from jax import lax
from jax.experimental import pallas as pl
from jax.experimental.pallas import tpu as pltpu
from jax.sharding import PartitionSpec as P

D = 1024
HDIM = 32
WIN = 16
HALO = 4
HALO_WIN = 4
TOK = WIN * WIN
STRIP = WIN * HALO
CORNER = HALO * HALO
SIDE_KEYS = 4 * STRIP + 4 * CORNER
KEYS = TOK + SIDE_KEYS
SUM_LEAST = 2.0**-60
SUM_MOST = 2.0**60
ROWS = 16
UNIT = 16
EPS = 1e-05
LOG2E = 1.4426950408889634
OFFSETS = ((-1, 0), (1, 0), (0, -1), (0, 1), (-1, -1), (-1, 1), (1, -1), (1, 1))


CHUNK = 32


def edge_columns(values):
    tall = values.reshape(WIN // 2, 2 * WIN, values.shape[1])
    upper = lax.broadcasted_iota(jnp.int32, (WIN // 2, 8, values.shape[1]), 1) < HALO

    def turned(lo):
        return pltpu.roll(tall[:, lo : lo + 8], HALO, 1)

    left = jnp.where(upper, tall[:, :8], turned(WIN))
    right = jnp.where(upper, turned(8), tall[:, WIN + 8 :])
    return [side.reshape(STRIP, values.shape[1]).astype(jnp.bfloat16) for side in (left, right)]


def nn_dot(a, b):
    return jnp.dot(a, b, preferred_element_type=jnp.float32)


def normalize(values, gain):
    center = values - jnp.mean(values, axis=-1, keepdims=True)
    spread = jnp.mean(center * center, axis=-1, keepdims=True)
    return (center * lax.rsqrt(spread + EPS) * gain).astype(jnp.bfloat16)


def qkv_kernel(
    count,
    win_count,
    width,
    tok_hbm,
    gain_hbm,
    w_hbm,
    qt_ref,
    k_ref,
    v_ref,
    ek_ref,
    ev_ref,
    tsum_ref,
    gain_s,
    tok_s,
    side_s,
    edge_s,
    w_s,
    even_s,
    odd_s,
    own_sem,
    w_sem,
    send_sem,
    recv_sem,
):
    me = lax.axis_index("pack")
    after = {"pack": lax.rem(me + 1, count)}
    before = {"pack": lax.rem(me + count - 1, count)}
    groups = width // 128
    bf = jnp.bfloat16

    def own(w):
        return pltpu.make_async_copy(
            tok_hbm.at[pl.ds(w * TOK, TOK)], tok_s.at[w], own_sem.at[w]
        )

    weight = pltpu.make_async_copy(w_hbm, w_s, w_sem.at[0])
    gain = pltpu.make_async_copy(gain_hbm, gain_s, w_sem.at[1])
    own(0).start()
    own(win_count - 1).start()
    gain.start()
    weight.start()
    for w in range(1, win_count - 1):
        own(w).start()

    pieces = []
    for i in range(HALO_WIN):
        place = pl.ds(i * STRIP, STRIP)
        high = (win_count - HALO_WIN + i + 1) * TOK - STRIP
        pieces.append((after, tok_hbm.at[pl.ds(high, STRIP)], tok_s.at[win_count, place]))
        pieces.append((before, tok_hbm.at[pl.ds(i * TOK, STRIP)], tok_s.at[win_count + 1, place]))
    pieces.append((after, edge_s.at[0], side_s.at[pl.ds(STRIP, STRIP)]))
    pieces.append((before, edge_s.at[1], side_s.at[pl.ds(0, STRIP)]))
    copies = [
        pltpu.make_async_remote_copy(
            src_ref=source,
            dst_ref=target,
            send_sem=send_sem.at[i],
            recv_sem=recv_sem.at[i],
            device_id=where,
            device_id_type=pl.DeviceIdType.MESH,
        )
        for i, (where, source, target) in enumerate(pieces)
    ]
    forward, backward = me < count - 1, me > 0
    barrier = pltpu.get_barrier_semaphore()
    for there, where in ((forward, after), (backward, before)):

        @pl.when(there)
        def _(where=where):
            pl.semaphore_signal(
                barrier, inc=1, device_id=where, device_id_type=pl.DeviceIdType.MESH
            )

    @pl.when(jnp.logical_not(backward))
    def _():
        tok_s[win_count] = jnp.zeros((TOK, D), bf)
        side_s[STRIP:] = jnp.zeros((STRIP, D), bf)

    @pl.when(jnp.logical_not(forward))
    def _():
        tok_s[win_count + 1] = jnp.zeros((TOK, D), bf)
        side_s[:STRIP] = jnp.zeros((STRIP, D), bf)

    def lane_mean(values):
        folded = values[:, :128]
        for lo in range(128, D, 128):
            folded = folded + values[:, lo : lo + 128]
        return jnp.sum(folded, axis=1, keepdims=True) * (1.0 / D)

    def norm_part(rows, out_s, lo):
        values = rows[lo : lo + CHUNK].astype(jnp.float32)
        center = values - lane_mean(values)
        spread = lane_mean(center * center)
        scaled = center * lax.rsqrt(spread + EPS) * gain_s[...]
        out_s[lo : lo + CHUNK] = scaled.astype(bf)
        folded = values[:8]
        for at in range(8, CHUNK, 8):
            folded = folded + values[at : at + 8]
        return folded

    def norm(rows, out_s):
        total = norm_part(rows, out_s, 0)
        for lo in range(CHUNK, rows.shape[0], CHUNK):
            total = total + norm_part(rows, out_s, lo)
        return jnp.sum(total, axis=0, keepdims=True)

    def keys_values(values, block):
        for part, out_ref, edge_ref in ((1, k_ref, ek_ref), (2, v_ref, ev_ref)):
            made = nn_dot(values, w_s[part])
            if block is None:
                sides, at = [made[:STRIP].astype(bf), made[STRIP:].astype(bf)], win_count + 2
            else:
                sides, at = edge_columns(made), block
            made = made.astype(bf)
            for g in range(groups):
                lanes = slice(g * 128, (g + 1) * 128)
                if block is not None:
                    out_ref[block, g] = made[:, lanes]
                edge_ref[at, g, :STRIP] = sides[0][:, lanes]
                edge_ref[at, g, STRIP:] = sides[1][:, lanes]

    def queries(values, block):
        q = nn_dot(values, w_s[0]).astype(bf)
        for g in range(groups):
            qt_ref[block, g] = q[:, g * 128 : (g + 1) * 128].T

    def project(block, in_s):
        values = in_s[...]
        queries(values, block)
        keys_values(values, block)

    def send(first, last):
        for i in range(first, last):
            pl.when((forward, backward)[i % 2])(copies[i].start)

    def receive(which):
        for i in which:
            pl.when((backward, forward)[i % 2])(copies[i].wait_recv)

    pl.semaphore_wait(barrier, jnp.where(forward, 1, 0) + jnp.where(backward, 1, 0))
    sides = 2 * HALO_WIN
    send(0, sides)
    own(win_count - 1).wait()
    edge_s[0] = edge_columns(tok_s[win_count - 1].astype(jnp.float32))[1]
    own(0).wait()
    edge_s[1] = edge_columns(tok_s[0].astype(jnp.float32))[0]
    send(sides, sides + 2)
    gain.wait()
    tsum_ref[pl.ds(0, 1)] = norm(tok_s.at[0], even_s)
    weight.wait()

    def arrive(block):
        @pl.when(block < win_count - 1)
        def _():
            own(jnp.minimum(block, win_count - 2)).wait()

    def both(block, in_s, out_s):
        project(block, in_s)
        tsum_ref[pl.ds(block + 1, 1)] = norm(tok_s.at[block + 1], out_s)

    def pair(i, carry):
        arrive(2 * i + 1)
        both(2 * i, even_s, odd_s)
        arrive(2 * i + 2)
        both(2 * i + 1, odd_s, even_s)
        return carry

    lax.fori_loop(0, win_count // 2 - 1, pair, 0)
    both(win_count - 2, even_s, odd_s)
    project(win_count - 1, odd_s)
    receive(range(0, sides, 2))
    norm(tok_s.at[win_count], even_s)
    receive(range(1, sides, 2))
    keys_values(even_s[...], win_count)
    norm(tok_s.at[win_count + 1], odd_s)
    receive(range(sides, sides + 2))
    keys_values(odd_s[...], win_count + 1)
    norm(side_s, even_s)
    keys_values(even_s[: 2 * STRIP], None)
    for i, copy in enumerate(copies):
        pl.when((forward, backward)[i % 2])(copy.wait_send)


def window_qkv(tokens, gain, weight):
    win_count = tokens.shape[0] // TOK
    width = weight.shape[2]
    groups = width // 128
    bf = jnp.bfloat16
    vmem = pl.BlockSpec(memory_space=pltpu.VMEM)
    hbm = pl.BlockSpec(memory_space=pltpu.HBM)
    edges = (win_count + 3, groups, 2 * STRIP, 128)
    return pl.pallas_call(
        functools.partial(qkv_kernel, lax.axis_size("pack"), win_count, width),
        out_shape=(
            pltpu.VMEM((win_count, groups, 128, TOK), bf),
            pltpu.VMEM((win_count + 2, groups, TOK, 128), bf),
            pltpu.VMEM((win_count + 2, groups, TOK, 128), bf),
            pltpu.VMEM(edges, bf),
            pltpu.VMEM(edges, bf),
            pltpu.VMEM((ROWS, D), jnp.float32),
        ),
        in_specs=[hbm, hbm, hbm],
        out_specs=(vmem,) * 6,
        scratch_shapes=[
            pltpu.VMEM((1, D), jnp.float32),
            pltpu.VMEM((win_count + 2, TOK, D), bf),
            pltpu.VMEM((2 * STRIP, D), bf),
            pltpu.VMEM((2, STRIP, D), bf),
            pltpu.VMEM((3, D, width), bf),
            pltpu.VMEM((TOK, D), bf),
            pltpu.VMEM((TOK, D), bf),
            pltpu.SemaphoreType.DMA((win_count,)),
            pltpu.SemaphoreType.DMA((2,)),
            pltpu.SemaphoreType.DMA((2 * HALO_WIN + 2,)),
            pltpu.SemaphoreType.DMA((2 * HALO_WIN + 2,)),
        ],
        compiler_params=pltpu.CompilerParams(
            collective_id=1, has_side_effects=True, vmem_limit_bytes=24 << 20
        ),
    )(
        pltpu.with_memory_space_constraint(tokens, pltpu.HBM),
        pltpu.with_memory_space_constraint(gain.reshape(1, D), pltpu.HBM),
        pltpu.with_memory_space_constraint(weight.transpose(1, 0, 2), pltpu.HBM),
    )


def attend_kernel(
    win_count,
    width,
    pages,
    windows_ref,
    across_ref,
    qt_ref,
    k_ref,
    v_ref,
    ek_ref,
    ev_ref,
    proj_hbm,
    mixed_hbm,
    projected_ref,
    msum_s,
    proj_s,
    proj_sem,
    pk_s,
    pv_s,
    mask_s,
    prob_s,
    out_s,
    low_s,
    high_s,
    out_sem,
):
    first = lax.axis_index("pack") * win_count
    groups = width // 128
    per = 128 // HDIM
    extra_most = KEYS - TOK
    factor = LOG2E / math.sqrt(HDIM)
    bf = jnp.bfloat16

    def copy_out(w):
        slot = lax.rem(w, 2)
        return pltpu.make_async_copy(
            out_s.at[slot], mixed_hbm.at[pl.ds(w * TOK, TOK)], out_sem.at[slot]
        )

    def find(p, carry):
        page, begin, run = carry
        run = run + windows_ref[p]
        passed = run <= first
        return jnp.where(passed, p + 1, page), jnp.where(passed, run, begin), run

    def pack(w, page, begin):
        across = across_ref[page]
        total = windows_ref[page]
        inside = first + w - begin
        row = lax.div(inside, across)
        col = inside - row * across
        filled = jnp.int32(0)
        for a, b in OFFSETS:
            place = inside + a * across + b
            valid = (col + b >= 0) & (col + b < across) & (row + a >= 0) & (place < total)
            near = w + a * across + b
            size = CORNER if a and b else STRIP
            early, late = near < 0, near >= win_count
            if a < 0:
                block = jnp.where(early, win_count, near)
                index = jnp.where(early, near + HALO_WIN, HALO_WIN - 1)
            elif a > 0:
                block = jnp.where(late, win_count + 1, near)
                index = jnp.where(late, near - win_count, 0)
            else:
                block = jnp.where(early | late, win_count + 2, near)
                index = 0
            start = index * size + (STRIP if b < 0 else 0)
            keys, values = (ek_ref, ev_ref) if b else (k_ref, v_ref)

            block = jnp.where(valid, block, 0)
            start = jnp.where(valid, start, 0)
            source = pl.ds(pl.multiple_of(start, 16), size)
            target = pl.ds(pl.multiple_of(filled, 16), size)
            pk_s[:, target, :] = keys[block, :, source, :]
            pv_s[:, target, :] = values[block, :, source, :]
            filled = filled + jnp.where(valid, size, 0)
        lane = lax.broadcasted_iota(jnp.int32, mask_s.shape, 1)
        mask_s[...] = jnp.where(lane < filled, 1.0, 0.0).astype(bf)
        return filled

    def finish(w, g, parts):
        piece = jnp.concatenate(parts, axis=0).T
        lanes = pl.ds(pl.multiple_of(g * 128, 128), 128)
        out_s[lax.rem(w, 2), :, lanes] = piece
        msum_s[w, :, lanes] = jnp.sum(piece.astype(jnp.float32), axis=0, keepdims=True)

    def spread(queries, j):
        above = [jnp.zeros((j * HDIM, TOK), bf)] if j else []
        below = [jnp.zeros((128 - (j + 1) * HDIM, TOK), bf)] if j + 1 < per else []
        return jnp.concatenate(above + [queries[j * HDIM : (j + 1) * HDIM]] + below, axis=0)

    def fast(w, extra):
        keys = TOK + extra
        for g in range(groups):
            queries = qt_ref[w, g]
            rows = jnp.concatenate([k_ref[w, g], pk_s[g, :extra]], axis=0) if extra else k_ref[w, g]
            for j in range(per):
                scores = nn_dot(rows, spread(queries, j))
                prob_s[g * per + j, :keys] = jnp.exp2(scores * factor).astype(bf)
        low, high = low_s[...], high_s[...]
        for g in range(groups):
            values = v_ref[w, g].T
            marks = jnp.ones((16, TOK), bf)
            if extra:
                values = jnp.concatenate([values, pv_s[g, :extra].T], axis=1)
                marks = jnp.concatenate([marks, mask_s[:, :extra]], axis=1)
            parts = []
            for j in range(per):
                lhs = jnp.concatenate([values[j * HDIM : (j + 1) * HDIM], marks], axis=0)
                summed = nn_dot(lhs, prob_s[g * per + j, :keys])
                total = summed[HDIM : HDIM + 1]
                low = jnp.minimum(low, total)
                high = jnp.maximum(high, total)
                parts.append((summed[:HDIM] * (1.0 / total)).astype(bf))
            finish(w, g, parts)
        low_s[...] = low
        high_s[...] = high

    def safe(w, filled):
        row = lax.broadcasted_iota(jnp.int32, (extra_most, TOK), 0)

        def group(g, carry):
            queries = qt_ref[w, g]
            values = jnp.concatenate([v_ref[w, g].T, pv_s[g, :extra_most].T], axis=1)
            parts = []
            for j in range(per):
                qz = spread(queries, j)
                near = nn_dot(pk_s[g, :extra_most], qz) * factor
                near = jnp.where(row < filled, near, -1e30)
                scores = jnp.concatenate([nn_dot(k_ref[w, g], qz) * factor, near], axis=0)
                weights = jnp.exp2(scores - jnp.max(scores, axis=0, keepdims=True))
                total = jnp.sum(weights, axis=0, keepdims=True)
                summed = nn_dot(values[j * HDIM : (j + 1) * HDIM], weights.astype(bf))
                parts.append((summed * (1.0 / total)).astype(bf))
            finish(w, g, parts)
            return carry

        lax.fori_loop(0, groups, group, 0)

    def sweep(guarded):
        def step(w, carry):
            page, begin = carry
            end = begin + windows_ref[page]
            passed = first + w >= end
            page = jnp.where(passed, page + 1, page)
            begin = jnp.where(passed, end, begin)
            filled = pack(w, page, begin)

            @pl.when(w >= 2)
            def _():
                copy_out(w - 2).wait()

            if guarded:
                safe(w, filled)
            else:
                chunks = lax.div(filled + UNIT - 1, UNIT)
                for c in range(extra_most // UNIT + 1):

                    @pl.when(chunks == c)
                    def _(c=c):
                        fast(w, c * UNIT)

            copy_out(w).start()
            return page, begin

        zero = jnp.int32(0)
        page, begin, _ = lax.fori_loop(0, pages, find, (zero, zero, zero))
        lax.fori_loop(0, win_count, step, (page, begin))
        copy_out(win_count - 2).wait()
        copy_out(win_count - 1).wait()

    proj_load = pltpu.make_async_copy(proj_hbm, proj_s, proj_sem.at[0])
    proj_load.start()
    msum_s[...] = jnp.zeros_like(msum_s)
    low_s[...] = jnp.ones_like(low_s)
    high_s[...] = jnp.ones_like(high_s)
    sweep(False)
    calm = (jnp.min(low_s[...]) >= SUM_LEAST) & (jnp.max(high_s[...]) <= SUM_MOST)

    @pl.when(jnp.logical_not(calm))
    def _():
        pk_s[...] = jnp.zeros_like(pk_s)
        pv_s[...] = jnp.zeros_like(pv_s)
        sweep(True)

    proj_load.wait()
    sums = msum_s[:, 0, :]
    high = sums.astype(bf)
    low = (sums - high.astype(jnp.float32)).astype(bf)
    both = nn_dot(jnp.concatenate([high, low], axis=0), proj_s[...])
    projected_ref[...] = both[:ROWS] + both[ROWS:]


def window_attention(tables, proj, page_windows, page_width, win_count):
    qt, k, v, ek, ev = tables
    groups = k.shape[1]
    width = groups * 128
    bf = jnp.bfloat16
    vmem = pl.BlockSpec(memory_space=pltpu.VMEM)
    smem = pl.BlockSpec(memory_space=pltpu.SMEM)
    hbm = pl.BlockSpec(memory_space=pltpu.HBM)
    room = KEYS - TOK + STRIP
    arrays = [pltpu.with_memory_space_constraint(a, pltpu.VMEM) for a in tables]
    return pl.pallas_call(
        functools.partial(attend_kernel, win_count, width, page_windows.shape[0]),
        out_shape=(
            jax.ShapeDtypeStruct((win_count * TOK, width), bf),
            pltpu.VMEM((ROWS, D), jnp.float32),
        ),
        in_specs=[smem, smem] + [vmem] * 5 + [hbm],
        out_specs=(hbm, vmem),
        scratch_shapes=[
            pltpu.VMEM((ROWS, 1, width), jnp.float32),
            pltpu.VMEM((width, D), bf),
            pltpu.SemaphoreType.DMA((1,)),
            pltpu.VMEM((groups, room, 128), bf),
            pltpu.VMEM((groups, room, 128), bf),
            pltpu.VMEM((16, room), bf),
            pltpu.VMEM((width // HDIM, KEYS, TOK), bf),
            pltpu.VMEM((2, TOK, width), bf),
            pltpu.VMEM((1, TOK), jnp.float32),
            pltpu.VMEM((1, TOK), jnp.float32),
            pltpu.SemaphoreType.DMA((2,)),
        ],
        compiler_params=pltpu.CompilerParams(vmem_limit_bytes=20 << 20),
    )(page_windows, page_width, *arrays, proj)


def page_kernel(
    count,
    heads,
    win_count,
    proj_ref,
    tsum_ref,
    gain_ref,
    windows_ref,
    docs_ref,
    w_hbm,
    out_hbm,
    out_ref,
    share_s,
    land_s,
    all_s,
    half_s,
    give_s,
    back_s,
    w_s,
    out_s,
    load_sem,
    head_send,
    head_recv,
    pack_send,
    pack_recv,
):
    me, head = lax.axis_index("pack"), lax.axis_index("head")
    pages, columns = out_ref.shape
    width = w_s.shape[2]
    bf = jnp.bfloat16
    mesh_id = pl.DeviceIdType.MESH

    loads = [
        pltpu.make_async_copy(w_hbm, w_s, load_sem.at[0]),
        pltpu.make_async_copy(out_hbm, out_s, load_sem.at[1]),
    ]
    for load in loads:
        load.start()

    half = count // 2
    twin = {"pack": me + 1 - 2 * lax.rem(me, 2)}

    def other_pack(k):
        return {"pack": lax.rem(me + 2 * k, count)}

    def other_head(k):
        return {"head": lax.rem(head + k, heads)}

    barrier = pltpu.get_barrier_semaphore()
    for k in range(1, heads):
        pl.semaphore_signal(barrier, inc=1, device_id=other_head(k), device_id_type=mesh_id)

    pl.semaphore_signal(barrier, inc=1, device_id=twin, device_id_type=mesh_id)

    @pl.loop(1, half)
    def _(k):
        pl.semaphore_signal(barrier, inc=1, device_id=other_pack(k), device_id_type=mesh_id)

    def head_copy(phase, k, source, target):
        return pltpu.make_async_remote_copy(
            src_ref=source,
            dst_ref=target,
            send_sem=head_send.at[phase, k],
            recv_sem=head_recv.at[phase, k],
            device_id=other_head(k),
            device_id_type=mesh_id,
        )

    def features(k):
        start = lax.rem(head + k, heads) * columns
        return pl.ds(pl.multiple_of(start, 128), columns)

    def rows_of(k):
        source = lax.rem(me + count - 2 * k, count)
        return pl.ds(pl.multiple_of(source * ROWS, ROWS), ROWS)

    def pack_copy(k):
        return pltpu.make_async_remote_copy(
            src_ref=all_s.at[rows_of(0)],
            dst_ref=all_s.at[rows_of(0)],
            send_sem=pack_send.at[0, k],
            recv_sem=pack_recv.at[0, k],
            device_id=other_pack(k),
            device_id_type=mesh_id,
        )

    def twin_copy(k):
        return pltpu.make_async_remote_copy(
            src_ref=all_s.at[rows_of(k)],
            dst_ref=all_s.at[rows_of(k)],
            send_sem=pack_send.at[1, k],
            recv_sem=pack_recv.at[1, k],
            device_id=twin,
            device_id_type=mesh_id,
        )

    for k in range(1, heads):
        share_s[k] = proj_ref[:, features(k)].astype(share_s.dtype)
    pl.semaphore_wait(barrier, half + heads - 1)
    first = [head_copy(0, k, share_s.at[k], land_s.at[k]) for k in range(1, heads)]
    for copy in first:
        copy.start()
    total = proj_ref[:, features(0)] + tsum_ref[:, features(0)]
    for k, copy in enumerate(first):
        copy.wait_recv()
        total = total + land_s[k + 1].astype(jnp.float32)
    real = lax.broadcasted_iota(jnp.int32, total.shape, 0) < win_count
    all_s[rows_of(0)] = jnp.where(real, total, 0.0).astype(all_s.dtype)

    @pl.loop(1, half)
    def _(k):
        pack_copy(k).start()

    twin_copy(0).start()

    def grid(shape, axis):
        return lax.broadcasted_iota(jnp.int32, shape, axis)

    square = (pages, pages)
    sizes = windows_ref[...].reshape(1, pages)
    upto = jnp.where(grid(square, 1) <= grid(square, 0), sizes, 0)
    ends = jnp.sum(upto, axis=1, keepdims=True)
    mine = jnp.sum(
        jnp.where(grid(square, 1) == grid(square, 0), sizes, 0), axis=1, keepdims=True
    )
    begins = ends - mine
    shape = (pages, count * ROWS)
    place = grid(shape, 1)
    inner = place & (ROWS - 1)
    window = (place // ROWS) * win_count + inner
    member = (window >= begins) & (window < ends) & (inner < win_count)
    member = jnp.where(member, 1.0, 0.0).astype(bf)
    scale = 1.0 / (mine.astype(jnp.float32) * TOK)
    docs = docs_ref.shape[0]
    lengths = docs_ref[...].reshape(1, docs)
    small = (docs, docs)
    column = jnp.sum(
        jnp.where(grid(small, 1) <= grid(small, 0), lengths, 0), axis=1, keepdims=True
    )
    across = jnp.sum(jnp.where(grid(small, 1) == grid(small, 0), column, 0), axis=0, keepdims=True)
    doc_row = jnp.sum(
        jnp.where(grid((docs, pages), 1) >= column, 1, 0), axis=0, keepdims=True
    )
    doc_col = jnp.sum(
        jnp.where(grid((pages, docs), 0) >= across, 1, 0), axis=1, keepdims=True
    )
    same = doc_row == doc_col

    @pl.loop(1, half)
    def _(k):
        pack_copy(k).wait_recv()
        twin_copy(k).start()

    @pl.loop(0, half)
    def _(k):
        twin_copy(k).wait_recv()

    gathered = all_s[...]
    high = gathered.astype(bf)
    pooled = nn_dot(member, high)
    if gathered.dtype != bf:
        pooled = pooled + nn_dot(member, (gathered - high.astype(jnp.float32)).astype(bf))
    pooled = pooled * scale
    half_s[head] = pooled.astype(half_s.dtype)
    second = [head_copy(1, k, half_s.at[head], half_s.at[head]) for k in range(1, heads)]
    for copy in second:
        copy.start()
    for copy in second:
        copy.wait_recv()
    parts = [jnp.where(head == k, pooled, half_s[k].astype(jnp.float32)) for k in range(heads)]
    normed = normalize(jnp.concatenate(parts, axis=1), gain_ref[...])
    for load in loads:
        load.wait()
    query, keys, values = (nn_dot(normed, w_s[i]).astype(bf) for i in range(3))
    owner = grid((pages, width), 1) // HDIM
    local = width // HDIM
    wide = jnp.concatenate(
        [jnp.where(owner == h, query.astype(jnp.float32), 0.0).astype(bf) for h in range(local)],
        axis=0,
    )
    scores = lax.dot_general(
        wide, keys, (((1,), (1,)), ((), ())), preferred_element_type=jnp.float32
    ) / math.sqrt(HDIM)
    scores = scores.reshape(local, pages, pages)
    scores = jnp.where(same[None], scores, -1e30)
    weights = jnp.exp(scores - jnp.max(scores, axis=-1, keepdims=True))
    probs = (weights / jnp.sum(weights, axis=-1, keepdims=True)).astype(bf)
    mixed = nn_dot(probs.reshape(local * pages, pages), values).reshape(local, pages, width)
    context = jnp.zeros((pages, width), jnp.float32)
    for h in range(local):
        context = jnp.where(owner == h, mixed[h], context)
    branch = nn_dot(context.astype(bf), out_s[...])
    give_s[0] = branch
    for k in range(1, heads):
        back_s[k] = give_s[0, :, features(k)].astype(back_s.dtype)
    third = [head_copy(2, k, back_s.at[k], back_s.at[heads + k]) for k in range(1, heads)]
    for copy in third:
        copy.start()
    result = pooled + give_s[0, :, features(0)]
    for k, copy in enumerate(third):
        copy.wait_recv()
        result = result + back_s[heads + k + 1].astype(jnp.float32)
    out_ref[...] = result
    for copy in first + second + third:
        copy.wait_send()

    @pl.loop(1, half)
    def _(k):
        pack_copy(k).wait_send()

    @pl.loop(0, half)
    def _(k):
        twin_copy(k).wait_send()


def page_layer(projected, token_sums, gain, weight, proj, page_windows, doc_pages, win_count):
    heads = lax.axis_size("head")
    count = lax.axis_size("pack")
    pages = page_windows.shape[0]
    width = weight.shape[2]
    columns = D // heads
    bf = jnp.bfloat16
    vmem = pl.BlockSpec(memory_space=pltpu.VMEM)
    hbm = pl.BlockSpec(memory_space=pltpu.HBM)
    return pl.pallas_call(
        functools.partial(page_kernel, count, heads, win_count),
        out_shape=jax.ShapeDtypeStruct((pages, columns), jnp.float32),
        in_specs=[vmem] * 5 + [hbm] * 2,
        out_specs=vmem,
        scratch_shapes=[
            pltpu.VMEM((heads, ROWS, columns), jnp.float32),
            pltpu.VMEM((heads, ROWS, columns), jnp.float32),
            pltpu.VMEM((count * ROWS, columns), bf),
            pltpu.VMEM((heads, pages, columns), bf),
            pltpu.VMEM((1, pages, D), jnp.float32),
            pltpu.VMEM((2 * heads, pages, columns), bf),
            pltpu.VMEM((3, D, width), bf),
            pltpu.VMEM((width, D), bf),
            pltpu.SemaphoreType.DMA((2,)),
            pltpu.SemaphoreType.DMA((3, heads)),
            pltpu.SemaphoreType.DMA((3, heads)),
            pltpu.SemaphoreType.DMA((2, count // 2)),
            pltpu.SemaphoreType.DMA((2, count // 2)),
        ],
        compiler_params=pltpu.CompilerParams(
            collective_id=2, has_side_effects=True, vmem_limit_bytes=24 << 20
        ),
    )(
        projected,
        token_sums,
        gain.reshape(1, D),
        page_windows,
        doc_pages,
        weight.transpose(1, 0, 2),
        proj,
    )


def shards(
    tokens,
    ln_gain,
    attn_weight,
    attn_proj,
    page_gain,
    page_weight,
    page_proj,
    page_windows,
    page_width,
    doc_pages,
):
    win_count = tokens.shape[0] // TOK
    *tables, token_sums = window_qkv(tokens, ln_gain, attn_weight)
    mixed, projected = window_attention(tables, attn_proj, page_windows, page_width, win_count)
    page_out = page_layer(
        projected,
        token_sums,
        page_gain,
        page_weight,
        page_proj,
        page_windows,
        doc_pages,
        win_count,
    )
    return (mixed, page_out)


def solution(mesh):
    placed = (
        P(("rep", "pack"), None),
        P(),
        P(None, None, "head"),
        P("head", None),
        P(),
        P(None, None, "head"),
        P("head", None),
        P("rep"),
        P("rep"),
        P("rep"),
    )
    return jax.shard_map(
        shards,
        mesh=mesh,
        in_specs=placed,
        out_specs=(P(("rep", "pack"), "head"), P("rep", "head")),
        check_vma=False,
    )
```
